256 devices in a mesh: rep: 8 (over y, x_lo), blk: 32 (over x_hi, z, core).
Axes of the slice: x: 4 (x_hi: 2, x_lo: 2; x = x_hi * 2 + x_lo), y: 4, z: 8, core: 2. Of those that a mesh axis runs over, the one named last changes fastest.
Arguments:
- features: bfloat16 [32, 2048, 128], P('blk', 'rep'), may hold values from -6 to 6
- node_ids: int32 [32, 2048], P('blk', 'rep'), may hold values from 0 to 8388607
- labels: int32 [32, 2048], P('blk', 'rep'), may hold values from 0 to 171
- train_mask: int32 [32, 2048], P('blk', 'rep'), may hold values 0 or 1
- tile_values: bfloat16 [32, 8, 4, 16, 128, 128], P('blk', 'rep'), may hold values from -0.125 to 0.125
- tile_place: int32 [32, 8, 4, 16], P('blk', 'rep'), may hold values from 0 to 255, as said below
- tile_count: int32 [32, 8, 4], P('blk', 'rep'), may hold values from 1 to 16, as said below
- weight_in: bfloat16 [128, 256], replicated, may hold values from -0.5 to 0.5
- weight_out: bfloat16 [256, 172], replicated, may hold values from -8 to 8
- class_bias: float32 [172], replicated, may hold values from -5 to 5
Outputs:
- logits: float32 [32, 2048, 172], P('blk', 'rep')
- grad_in: float32 [128, 256], replicated
- grad_out: float32 [256, 172], replicated
The draws below stay inside these ranges and needn't reach their ends.
Inputs may be any that keep to these rules, and one draw needn't show every extreme that they name: `tile_place`: within one block pair the slots name distinct positions. `tile_count`: the live slots of a pair are its first ones; some device has 16 live slots in each of its pairs.
All inputs are finite; a program needn't handle non-finite values. No bound on the sum of `train_mask` on one device may be relied on, other than what follows from the above.
Results may differ from the reference program's by a relative error of at most 0.015.
The reference program's roundings to bfloat16 on the way count: a program that leaves them out, or rounds other values in their place, can miss the bound.
Values may be sent and summed in bfloat16 or wider, within the bound.
A program may use at most 128 MiB of HBM per device.

```python
import math
import jax
import jax.numpy as jnp
from jax import lax

IN_WIDTH = 128
UNITS = 256
CLASSES = 172
TILE = 128
TMAX = 16
BLOCKS = 32
SECTIONS = 4
BROWS = 2048
TILES_SIDE = 16
NODES = 65536
N_REP = 8


def draw_tile_place(key, part):
    pair_total = BLOCKS * (BLOCKS // SECTIONS) * SECTIONS
    position_total = TILES_SIDE * TILES_SIDE
    pair_keys = jax.random.split(key, pair_total)
    orders = jax.vmap(lambda pair_key: jax.random.permutation(pair_key, position_total)[:TMAX])(pair_keys)
    ascending = jnp.arange(TMAX, dtype=jnp.int32)
    descending = position_total - 1 - ascending
    orders = orders.astype(jnp.int32).at[0].set(descending).at[pair_total - 1].set(ascending)
    return orders.reshape(BLOCKS, BLOCKS // SECTIONS, SECTIONS, TMAX).astype(jnp.int32)


def draw_tile_count(key, part):
    heavy_key, light_key = jax.random.split(key)
    rep_total = BLOCKS // SECTIONS
    heavy_device = jax.random.randint(heavy_key, (BLOCKS, rep_total, 1), 0, 4) == 0
    light_count = jax.random.randint(light_key, (BLOCKS, rep_total, SECTIONS), 1, TMAX // 2 + 1)
    counts = jnp.where(heavy_device, TMAX, light_count).astype(jnp.int32)
    counts = counts.at[0, 0, :].set(TMAX).at[BLOCKS - 1, rep_total - 1, 0].set(1)
    return counts.astype(jnp.int32)


def draw_weight_out(key, part):
    base_key = jax.random.fold_in(key, 0)
    values = jnp.clip(jax.random.normal(base_key, (UNITS, CLASSES), jnp.float32), -6.0, 6.0) * (3.5 / math.sqrt(UNITS))
    return values.astype(jnp.bfloat16)


def draw_class_bias(key, part):
    values = jax.random.uniform(key, (CLASSES,), jnp.float32, -3.0, 3.0)
    return values


def touch_ends(values, rng, smallest, high):
    longest = values.shape.index(max(values.shape))
    spots = []
    for shift in (0, 1):
        where = [jax.random.randint(jax.random.fold_in(rng, axis), (), 0, length) for axis, length in enumerate(values.shape)]
        where[longest] = (where[longest] + shift) % values.shape[longest]
        spots.append(tuple(where))
    return values.at[spots[0]].set(smallest).at[spots[1]].set(high)


def shard_levels(key, shape, shards, low, largest):
    def one(position, blocks):
        draws = jax.random.uniform(jax.random.fold_in(jax.random.fold_in(key, 6), position), (blocks,), jnp.float32, low / len(shards), largest / len(shards))
        return jnp.repeat(jnp.exp(draws), shape[position] // blocks).reshape((-1,) + (1,) * (len(shape) - position - 1))

    loudness = one(*shards[0])
    for cut in shards[1:]:
        loudness = loudness * one(*cut)
    return loudness


def gaussian(rng, shape, scale, most, cuts=(), kind=jnp.bfloat16):
    factor_of = shard_levels(rng, shape, cuts, -0.22, 0.18) if cuts else 1.0
    values = jax.random.normal(rng, shape, jnp.float32) * scale * factor_of
    return jnp.minimum(jnp.maximum(values, -most), most).astype(kind)


def setup_inputs(seed: int = 0) -> dict:
    arg_keys = jax.random.split(jax.random.key(seed), 11)
    features = gaussian(arg_keys[0], (BLOCKS, BROWS, IN_WIDTH), 1.0, 6.0, ((0, 32), (1, 8)))
    node_ids = touch_ends(jax.random.randint(arg_keys[1], (BLOCKS, BROWS), 0, 8388608), jax.random.fold_in(arg_keys[1], 1), 0, 8388607).astype(jnp.int32)
    labels = touch_ends(jax.random.randint(arg_keys[2], (BLOCKS, BROWS), 0, CLASSES), jax.random.fold_in(arg_keys[2], 1), 0, CLASSES - 1).astype(jnp.int32)
    train_mask = touch_ends((jax.random.randint(arg_keys[3], (BLOCKS, BROWS), 0, 2) < 1).astype(jnp.int32), jax.random.fold_in(arg_keys[3], 1), 0, 1)
    tile_values = gaussian(arg_keys[4], (BLOCKS, N_REP, SECTIONS, TMAX, TILE, TILE), (BLOCKS * TMAX * TILE // (2 * TILES_SIDE)) ** -0.5, 0.125, ((0, 32), (1, 8)))
    tile_place = draw_tile_place(jax.random.fold_in(arg_keys[10], 71), 0)
    tile_count = draw_tile_count(jax.random.fold_in(arg_keys[10], 71), 0)
    weight_in = gaussian(arg_keys[7], (IN_WIDTH, UNITS), IN_WIDTH ** -0.5, 0.5)
    weight_out = draw_weight_out(jax.random.fold_in(arg_keys[10], 71), 0)
    class_bias = draw_class_bias(jax.random.fold_in(arg_keys[10], 71), 0)
    return dict(features=features, node_ids=node_ids, labels=labels, train_mask=train_mask, tile_values=tile_values, tile_place=tile_place, tile_count=tile_count, weight_in=weight_in, weight_out=weight_out, class_bias=class_bias)


def keep_factor(id_values, unit_count):
    columns = jnp.arange(unit_count, dtype=jnp.int32)
    mixed = id_values[:, None] * 73244475 + columns[None, :] * 19349663 + 12345
    mixed = mixed ^ jnp.right_shift(mixed, 15)
    mixed = mixed * 40503
    mixed = mixed ^ jnp.right_shift(mixed, 13)
    kept_mask = jnp.bitwise_and(mixed, 3) != 0
    return jnp.where(kept_mask, jnp.float32(4.0 / 3.0), jnp.float32(0.0))

def forward_section(section_tiles, section_place, section_count, source, tile_side):
    tile_edge = section_tiles.shape[-1]
    feat_width = source.shape[-1]
    pieces = source.reshape(tile_side, tile_edge, feat_width)
    gathered = jnp.take(pieces, section_place % tile_side, axis=0).astype(jnp.float32)
    products = jnp.einsum('tij,tjf->tif', section_tiles.astype(jnp.float32), gathered, precision=lax.Precision.HIGHEST)
    live_slots = jnp.arange(section_tiles.shape[0], dtype=jnp.int32) < section_count
    placing = ((section_place // tile_side)[None, :] == jnp.arange(tile_side, dtype=jnp.int32)[:, None]) & live_slots[None, :]
    summed = jnp.einsum('rt,tif->rif', placing.astype(jnp.float32), products, precision=lax.Precision.HIGHEST)
    return summed.reshape(tile_side * tile_edge, feat_width)

def backward_section(section_tiles, section_place, section_count, source, tile_side):
    tile_edge = section_tiles.shape[-1]
    feat_width = source.shape[-1]
    pieces = source.reshape(tile_side, tile_edge, feat_width)
    gathered = jnp.take(pieces, section_place // tile_side, axis=0).astype(jnp.float32)
    products = jnp.einsum('tji,tjf->tif', section_tiles.astype(jnp.float32), gathered, precision=lax.Precision.HIGHEST)
    live_slots = jnp.arange(section_tiles.shape[0], dtype=jnp.int32) < section_count
    placing = ((section_place % tile_side)[None, :] == jnp.arange(tile_side, dtype=jnp.int32)[:, None]) & live_slots[None, :]
    summed = jnp.einsum('rt,tif->rif', placing.astype(jnp.float32), products, precision=lax.Precision.HIGHEST)
    return summed.reshape(tile_side * tile_edge, feat_width)

def pair_data(tile_values, tile_place, tile_count, block_index):
    section_tiles = tile_values[block_index].reshape(BLOCKS, TMAX, TILE, TILE)
    section_place = tile_place[block_index].reshape(BLOCKS, TMAX)
    section_count = tile_count[block_index].reshape(BLOCKS)
    sources = jnp.mod(block_index - jnp.arange(BLOCKS, dtype=jnp.int32), BLOCKS).astype(jnp.int32)
    return (section_tiles, section_place, section_count, sources)

def aggregate(rows_all, tile_values, tile_place, tile_count):

    def per_block(block_index):
        section_tiles, section_place, section_count, sources = pair_data(tile_values, tile_place, tile_count, block_index)
        blocks_in = rows_all[sources]
        parts_all = jax.vmap(forward_section, in_axes=(0, 0, 0, 0, None))(section_tiles, section_place, section_count, blocks_in, TILES_SIDE)
        return lax.optimization_barrier(jnp.sum(parts_all, axis=0))
    return lax.map(per_block, jnp.arange(BLOCKS, dtype=jnp.int32))

def aggregate_back(rows_all, tile_values, tile_place, tile_count):

    def per_block(carried, block_index):
        section_tiles, section_place, section_count, sources = pair_data(tile_values, tile_place, tile_count, block_index)
        parts_all = jax.vmap(backward_section, in_axes=(0, 0, 0, None, None))(section_tiles, section_place, section_count, rows_all[block_index], TILES_SIDE)
        return (carried.at[sources].add(parts_all), None)
    start_zero = jnp.zeros((BLOCKS, BROWS, rows_all.shape[-1]), jnp.float32)
    result, unused = lax.scan(per_block, start_zero, jnp.arange(BLOCKS, dtype=jnp.int32))
    return result

def reference(features, node_ids, labels, train_mask, tile_values, tile_place, tile_count, weight_in, weight_out, class_bias):
    z_input = aggregate(features, tile_values, tile_place, tile_count).astype(jnp.bfloat16)
    pre_act = jnp.einsum('bnf,fh->bnh', z_input.astype(jnp.float32), weight_in.astype(jnp.float32), precision=lax.Precision.HIGHEST)
    kept = keep_factor(node_ids.reshape(-1), UNITS).reshape(BLOCKS, BROWS, UNITS)
    dropped = (jnp.maximum(pre_act, 0.0) * kept).astype(jnp.bfloat16)
    z_output = aggregate(dropped, tile_values, tile_place, tile_count).astype(jnp.bfloat16)
    logits = jnp.einsum('bnh,hc->bnc', z_output.astype(jnp.float32), weight_out.astype(jnp.float32), precision=lax.Precision.HIGHEST) + class_bias
    likelihood = jax.nn.softmax(logits, axis=-1)
    onehot = (labels[..., None] == jnp.arange(CLASSES, dtype=jnp.int32)).astype(jnp.float32)
    scale = 1.0 / math.sqrt(NODES)
    slope = ((likelihood - onehot) * train_mask[..., None].astype(jnp.float32) * scale).astype(jnp.bfloat16)
    grad_out = jnp.einsum('bnh,bnc->hc', z_output.astype(jnp.float32), slope.astype(jnp.float32), precision=lax.Precision.HIGHEST)
    grad_rows = jnp.einsum('bnc,hc->bnh', slope.astype(jnp.float32), weight_out.astype(jnp.float32), precision=lax.Precision.HIGHEST).astype(jnp.bfloat16)
    back_rows = aggregate_back(grad_rows, tile_values, tile_place, tile_count)
    pre_slope = (back_rows * kept * (pre_act > 0)).astype(jnp.bfloat16)
    grad_in = jnp.einsum('bnf,bnh->fh', z_input.astype(jnp.float32), pre_slope.astype(jnp.float32), precision=lax.Precision.HIGHEST)
    return (logits, grad_in, grad_out)
```

```python
import functools
import math

import jax
import jax.numpy as jnp
from jax import lax
from jax.experimental import pallas as pl
from jax.experimental.pallas import tpu as pltpu
from jax.sharding import PartitionSpec as P

MESH = pl.DeviceIdType.MESH
F32 = jnp.float32
BF16 = jnp.bfloat16
REP = 8
BLK = 32
SEC = 4
TILE = 128
SLOTS = 16
WIDE = 256
CLASSES = 172
VMEM_LIMIT = 56 << 20


def whole():
    return pl.BlockSpec(memory_space=pltpu.VMEM)


def in_smem():
    return pl.BlockSpec(memory_space=pltpu.SMEM)


def params(collective):
    if collective is None:
        return pltpu.CompilerParams(vmem_limit_bytes=VMEM_LIMIT)
    return pltpu.CompilerParams(
        collective_id=collective, has_side_effects=True, vmem_limit_bytes=VMEM_LIMIT
    )


def where_am_i():
    return lax.axis_index("rep"), lax.axis_index("blk")


def remote(source, target, send, arrive, device):
    return pltpu.make_async_remote_copy(
        src_ref=source,
        dst_ref=target,
        send_sem=send,
        recv_sem=arrive,
        device_id=device,
        device_id_type=MESH,
    )


def landed(target, send, arrive, device):
    remote(target, target, send, arrive, device).wait_recv()


def greet(device):
    pl.semaphore_signal(
        pltpu.get_barrier_semaphore(), inc=1, device_id=device, device_id_type=MESH
    )


def greet_group():
    rep, blk = where_am_i()
    for step in range(1, REP):
        greet((lax.rem(rep + step, REP), blk))
    return REP - 1


def greet_spread_sources():
    rep, blk = where_am_i()
    count = 0
    for other in range(REP):
        first = lax.rem(blk - SEC * rep + BLK, BLK)
        last = lax.rem(blk - SEC * rep - (SEC - 1) + 2 * BLK, BLK)
        if other == 0:
            @pl.when(rep != 0)
            def _():
                greet((0, first))
        else:
            greet((other, first))
        greet((other, last))
        count += 2
    greet((rep, lax.rem(blk + 1, BLK)))
    greet((rep, lax.rem(blk + BLK - 1, BLK)))
    return count + 2


def greet_fold_sources():
    rep, blk = where_am_i()
    count = 0
    for other in range(REP):
        first = lax.rem(blk + SEC * other, BLK)
        last = lax.rem(blk + SEC * other + (SEC - 1), BLK)
        if other == 0:
            @pl.when(rep != 0)
            def _():
                greet((0, first))
        else:
            greet((other, first))
        greet((other, last))
        count += 2
    greet((rep, lax.rem(blk + 1, BLK)))
    greet((rep, lax.rem(blk + BLK - 1, BLK)))
    return count + 2


def spread(shard, sections, send, chain_send, arrive):
    rep, blk = where_am_i()
    here = (rep, blk)
    up = lax.rem(blk + 1, BLK)
    down = lax.rem(blk + BLK - 1, BLK)

    def first_copy(other):
        return remote(
            shard.at[0],
            sections.at[0, 0, rep],
            send.at[0, other],
            arrive.at[0, 0, rep],
            (other, lax.rem(blk + SEC * other, BLK)),
        )

    def last_copy(other):
        return remote(
            shard.at[1],
            sections.at[SEC - 1, 1, rep],
            send.at[1, other],
            arrive.at[SEC - 1, 1, rep],
            (other, lax.rem(blk + SEC * other + SEC - 1, BLK)),
        )

    for step in range(REP):
        other = lax.rem(rep + step, REP)
        if step == 0:
            @pl.when(rep == 0)
            def _():
                sections[0, 0, 0] = shard[0]

            @pl.when(rep != 0)
            def _():
                first_copy(other).start()
        else:
            first_copy(other).start()
        last_copy(other).start()

    def hop(index, carry):
        section = index // REP
        step = lax.rem(index, REP)
        piece = lax.rem(rep + REP - step, REP)
        local = jnp.logical_and(jnp.logical_and(rep == 0, piece == 0), section == 0)
        other_section = SEC - 1 - section

        @pl.when(jnp.logical_not(local))
        def _():
            landed(
                sections.at[section, 0, piece],
                chain_send.at[0, 0, 0],
                arrive.at[section, 0, piece],
                here,
            )

        remote(
            sections.at[section, 0, piece],
            sections.at[section + 1, 0, piece],
            chain_send.at[0, section, piece],
            arrive.at[section + 1, 0, piece],
            (rep, up),
        ).start()
        landed(
            sections.at[other_section, 1, piece],
            chain_send.at[0, 0, 0],
            arrive.at[other_section, 1, piece],
            here,
        )
        remote(
            sections.at[other_section, 1, piece],
            sections.at[other_section - 1, 1, piece],
            chain_send.at[1, section, piece],
            arrive.at[other_section - 1, 1, piece],
            (rep, down),
        ).start()
        return carry

    lax.fori_loop(0, (SEC - 1) * REP, hop, 0)

    def finish(piece, carry):
        landed(
            sections.at[SEC - 1, 0, piece],
            chain_send.at[0, 0, 0],
            arrive.at[SEC - 1, 0, piece],
            here,
        )
        landed(
            sections.at[0, 1, piece], chain_send.at[0, 0, 0], arrive.at[0, 1, piece], here
        )
        @pl.when(jnp.logical_not(jnp.logical_and(rep == 0, piece == 0)))
        def _():
            first_copy(piece).wait_send()

        last_copy(piece).wait_send()
        for section in range(SEC - 1):
            remote(
                sections.at[section, 0, piece],
                sections.at[section + 1, 0, piece],
                chain_send.at[0, section, piece],
                arrive.at[section + 1, 0, piece],
                (rep, up),
            ).wait_send()
            remote(
                sections.at[SEC - 1 - section, 1, piece],
                sections.at[SEC - 2 - section, 1, piece],
                chain_send.at[1, section, piece],
                arrive.at[SEC - 2 - section, 1, piece],
                (rep, down),
            ).wait_send()
        return carry

    lax.fori_loop(0, REP, finish, 0)


SPREAD_SEMS = (
    pltpu.SemaphoreType.DMA((2, REP)),
    pltpu.SemaphoreType.DMA((2, SEC - 1, REP)),
    pltpu.SemaphoreType.DMA((SEC, 2, REP)),
)


def group_send(pieces, landing, send, arrive):
    rep, blk = where_am_i()
    for step in range(1, REP):
        other = lax.rem(rep + step, REP)
        remote(
            pieces.at[other], landing.at[rep], send.at[other], arrive.at[rep], (other, blk)
        ).start()


def group_wait(pieces, landing, send, arrive):
    rep, blk = where_am_i()
    for step in range(1, REP):
        other = lax.rem(rep + step, REP)
        copy = remote(
            pieces.at[other], landing.at[other], send.at[other], arrive.at[other], (other, blk)
        )
        copy.wait_recv()
        copy.wait_send()


def group_sum(pieces, landing):
    rep, blk = where_am_i()
    landing[rep] = pieces[rep]
    total = landing[0].astype(F32)
    for index in range(1, REP):
        total = total + landing[index].astype(F32)
    return total


GROUP_SEMS = (pltpu.SemaphoreType.DMA((REP,)), pltpu.SemaphoreType.DMA((REP,)))


def keep_factor(ids):
    columns = lax.broadcasted_iota(jnp.int32, (1, WIDE), 1)
    mixed = ids * 73244475 + columns * 19349663 + 12345
    mixed = mixed ^ jnp.right_shift(mixed, 15)
    mixed = mixed * 40503
    mixed = mixed ^ jnp.right_shift(mixed, 13)
    return jnp.where(jnp.bitwise_and(mixed, 3) != 0, F32(4.0 / 3.0), F32(0.0))


def first_kernel(x, sections, send, chain_send, arrive):
    waits = greet_spread_sources()
    rep, blk = where_am_i()
    pl.semaphore_wait(pltpu.get_barrier_semaphore(), waits - jnp.where(rep == 0, 1, 0))
    spread(x, sections, send, chain_send, arrive)


def forward_kernel(place, count, tiles, sections, out, total):
    total[...] = jnp.zeros_like(total)
    for section in range(SEC):
        live = count[section]
        for group in range(SLOTS // 4):
            @pl.when(group * 4 < live)
            def _(section=section, group=group):
                for slot in range(group * 4, group * 4 + 4):
                    spot = place[section, slot]
                    row = spot // SLOTS
                    column = lax.rem(spot, SLOTS)
                    source = sections[section, lax.rem(column, 2), column // 2]
                    product = jnp.dot(
                        tiles[section, slot], source, preferred_element_type=F32
                    )
                    flag = jnp.where(slot < live, F32(1.0), F32(0.0))
                    total[row] = total[row] + product * flag
    out[...] = total[...].astype(out.dtype)


def backward_kernel(place, count, tiles, rows, out, total):
    total[...] = jnp.zeros_like(total)
    for section in range(SEC):
        live = count[section]
        for group in range(SLOTS // 4):
            @pl.when(group * 4 < live)
            def _(section=section, group=group):
                for slot in range(group * 4, group * 4 + 4):
                    spot = place[section, slot]
                    row = spot // SLOTS
                    column = lax.rem(spot, SLOTS)
                    product = lax.dot_general(
                        tiles[section, slot],
                        rows[row],
                        (((0,), (0,)), ((), ())),
                        preferred_element_type=F32,
                    )
                    flag = jnp.where(slot < live, F32(1.0), F32(0.0))
                    half = lax.rem(column, 2)
                    piece = column // 2
                    total[section, half, piece] = total[section, half, piece] + product * flag
    out[...] = total[...].astype(out.dtype)


def hidden_kernel(
    partial,
    ids,
    weight_in,
    weight_out,
    z_out,
    dropped_out,
    slope_factor,
    sections,
    landing,
    shard,
    group_sems_send,
    group_sems_arrive,
    send,
    chain_send,
    arrive,
):
    waits = greet_group() + greet_spread_sources()
    rep, blk = where_am_i()
    pl.semaphore_wait(pltpu.get_barrier_semaphore(), waits - jnp.where(rep == 0, 1, 0))
    group_send(partial, landing, group_sems_send, group_sems_arrive)
    group_wait(partial, landing, group_sems_send, group_sems_arrive)
    z_input = group_sum(partial, landing).astype(BF16)
    z_out[...] = z_input
    pre_act = jnp.dot(z_input, weight_in[...], preferred_element_type=F32)
    kept = keep_factor(ids[...])
    dropped = (jnp.maximum(pre_act, 0.0) * kept).astype(BF16)
    dropped_out[...] = dropped
    slope_factor[...] = jnp.where(pre_act > 0, kept, 0.0)
    mapped = jnp.dot(dropped, weight_out[...], preferred_element_type=F32).astype(BF16)
    shard[0] = mapped[:TILE]
    shard[1] = mapped[TILE:]
    spread(shard, sections, send, chain_send, arrive)


def class_kernel(
    scale,
    partial,
    labels,
    mask,
    bias,
    logits_out,
    slopes,
    landing,
    send,
    arrive,
    slope_send,
    slope_arrive,
):
    waits = greet_group()
    rep, blk = where_am_i()
    pl.semaphore_wait(pltpu.get_barrier_semaphore(), waits)
    group_send(partial, landing, send, arrive)
    group_wait(partial, landing, send, arrive)
    logits = group_sum(partial, landing) + bias[...]
    logits_out[...] = logits[:, :CLASSES]
    columns = lax.broadcasted_iota(jnp.int32, logits.shape, 1)
    real = columns < CLASSES
    top = jnp.max(jnp.where(real, logits, -jnp.inf), axis=1, keepdims=True)
    powers = jnp.where(real, jnp.exp(logits - top), 0.0)
    likelihood = powers / jnp.sum(powers, axis=1, keepdims=True)
    onehot = jnp.where(columns == labels[...], 1.0, 0.0)
    slope = (likelihood - onehot) * mask[...].astype(F32) * scale
    slopes[rep] = slope.astype(BF16)
    for step in range(1, REP):
        other = lax.rem(rep + step, REP)
        remote(
            slopes.at[rep], slopes.at[rep], slope_send.at[other], slope_arrive.at[rep], (other, blk)
        ).start()
    for step in range(1, REP):
        other = lax.rem(rep + step, REP)
        copy = remote(
            slopes.at[rep], slopes.at[other], slope_send.at[other], slope_arrive.at[other], (other, blk)
        )
        copy.wait_recv()
        copy.wait_send()


def blk_of(part, depth, core):
    return (part * (BLK // 4) + depth) * 2 + core


def last_kernel(
    parts,
    z_input,
    dropped,
    slope_factor,
    weight_out,
    grad_in,
    grad_out,
    low_in,
    high_in,
    low_out,
    high_out,
    final_out,
    final_in,
    mine,
    terms,
    landing,
    corner,
    corner_in,
    depth_in,
    full_corner,
    full,
    chain_send,
    chain_arrive,
    final_send,
    final_arrive,
    a_send,
    a_arrive,
    b_send,
    b_arrive,
    c_send,
    c_arrive,
    d_send,
    d_arrive,
    e_send,
    e_arrive,
):
    rep, blk = where_am_i()
    here = (rep, blk)
    core = lax.rem(blk, 2)
    depth = lax.rem(blk // 2, 8)
    part = blk // 16
    waits = greet_group() + greet_fold_sources()
    corner_me = part * 2 + core
    for step in range(1, 4):
        other = lax.rem(corner_me + step, 4)
        greet((rep, blk_of(other // 2, depth, lax.rem(other, 2))))
    for step in range(1, 8):
        greet((rep, blk_of(part, lax.rem(depth + step, 8), core)))
    waits = waits + 10
    pl.semaphore_wait(pltpu.get_barrier_semaphore(), waits - jnp.where(rep == 0, 1, 0))

    up = lax.rem(blk + 1, BLK)
    down = lax.rem(blk + BLK - 1, BLK)
    first = lax.rem(blk - SEC * rep + BLK, BLK)
    last = lax.rem(blk - SEC * rep - (SEC - 1) + 2 * BLK, BLK)

    def start(piece, carry):
        remote(
            parts.at[SEC - 1, 0, piece],
            low_in.at[SEC - 2, piece],
            chain_send.at[0, 0, piece],
            chain_arrive.at[0, SEC - 2, piece],
            (rep, down),
        ).start()
        remote(
            parts.at[0, 1, piece],
            high_in.at[0, piece],
            chain_send.at[1, 0, piece],
            chain_arrive.at[1, 0, piece],
            (rep, up),
        ).start()
        return carry

    lax.fori_loop(0, REP, start, 0)

    def hop(index, carry):
        step = index // REP
        piece = lax.rem(index, REP)
        low_section = SEC - 2 - step
        landed(
            low_in.at[low_section, piece],
            chain_send.at[0, 0, 0],
            chain_arrive.at[0, low_section, piece],
            here,
        )
        low_out[low_section, piece] = (
            low_in[low_section, piece].astype(F32) + parts[low_section, 0, piece].astype(F32)
        ).astype(BF16)
        remote(
            low_out.at[low_section, piece],
            low_in.at[low_section - 1, piece],
            chain_send.at[0, step + 1, piece],
            chain_arrive.at[0, low_section - 1, piece],
            (rep, down),
        ).start()
        landed(
            high_in.at[step, piece],
            chain_send.at[0, 0, 0],
            chain_arrive.at[1, step, piece],
            here,
        )
        high_out[step, piece] = (
            high_in[step, piece].astype(F32) + parts[step + 1, 1, piece].astype(F32)
        ).astype(BF16)
        remote(
            high_out.at[step, piece],
            high_in.at[step + 1, piece],
            chain_send.at[1, step + 1, piece],
            chain_arrive.at[1, step + 1, piece],
            (rep, up),
        ).start()
        return carry

    lax.fori_loop(0, (SEC - 2) * REP, hop, 0)

    def low_final(piece):
        return remote(
            final_out.at[0, piece],
            final_in.at[0, rep],
            final_send.at[0, piece],
            final_arrive.at[0, rep],
            (piece, first),
        )

    def high_final(piece):
        return remote(
            final_out.at[1, piece],
            final_in.at[1, rep],
            final_send.at[1, piece],
            final_arrive.at[1, rep],
            (piece, last),
        )

    def final(piece, carry):
        landed(
            low_in.at[0, piece], chain_send.at[0, 0, 0], chain_arrive.at[0, 0, piece], here
        )
        final_out[0, piece] = (
            low_in[0, piece].astype(F32) + parts[0, 0, piece].astype(F32)
        ).astype(BF16)
        self_piece = jnp.logical_and(rep == 0, piece == 0)

        @pl.when(self_piece)
        def _():
            final_in[0, 0] = final_out[0, 0]

        @pl.when(jnp.logical_not(self_piece))
        def _():
            low_final(piece).start()

        landed(
            high_in.at[SEC - 2, piece],
            chain_send.at[0, 0, 0],
            chain_arrive.at[1, SEC - 2, piece],
            here,
        )
        final_out[1, piece] = (
            high_in[SEC - 2, piece].astype(F32) + parts[SEC - 1, 1, piece].astype(F32)
        ).astype(BF16)
        high_final(piece).start()
        return carry

    lax.fori_loop(0, REP, final, 0)

    def gather_final(source, carry):
        @pl.when(jnp.logical_not(jnp.logical_and(rep == 0, source == 0)))
        def _():
            landed(
                final_in.at[0, source],
                chain_send.at[0, 0, 0],
                final_arrive.at[0, source],
                here,
            )

        landed(
            final_in.at[1, source], chain_send.at[0, 0, 0], final_arrive.at[1, source], here
        )
        return carry

    lax.fori_loop(0, REP, gather_final, 0)
    for half in range(2):
        total = final_in[half, 0].astype(F32)
        for source in range(1, REP):
            total = total + final_in[half, source].astype(F32)
        mine[pl.ds(half * TILE, TILE), :] = total.astype(BF16)

    back = mine[...]
    out_terms = lax.dot_general(
        dropped[...], back, (((0,), (0,)), ((), ())), preferred_element_type=F32
    )
    back_rows = lax.dot_general(
        back, weight_out[...], (((1,), (1,)), ((), ())), preferred_element_type=F32
    )
    pre_slope = (back_rows * slope_factor[...]).astype(BF16)
    in_terms = lax.dot_general(
        z_input[...], pre_slope, (((0,), (0,)), ((), ())), preferred_element_type=F32
    )
    in_rows = in_terms.shape[0]
    chunk = (in_rows + WIDE) // REP
    joined = jnp.concatenate([in_terms, out_terms], axis=0)
    for index in range(REP):
        terms[index] = joined[index * chunk : (index + 1) * chunk]
    group_send(terms, landing, a_send, a_arrive)
    group_wait(terms, landing, a_send, a_arrive)
    total = group_sum(terms, landing)
    for index in range(12):
        corner[index // 3, index % 3] = total[
            (index // 2) * 8 : (index // 2) * 8 + 8, (index % 2) * 128 : (index % 2) * 128 + 128
        ]

    def corner_device(index):
        return (rep, blk_of(index // 2, depth, lax.rem(index, 2)))

    for step in range(1, 4):
        other = lax.rem(corner_me + step, 4)
        remote(
            corner.at[other],
            corner_in.at[corner_me],
            b_send.at[other],
            b_arrive.at[corner_me],
            corner_device(other),
        ).start()
    for step in range(1, 4):
        other = lax.rem(corner_me + step, 4)
        copy = remote(
            corner.at[other],
            corner_in.at[other],
            b_send.at[other],
            b_arrive.at[other],
            corner_device(other),
        )
        copy.wait_recv()
        copy.wait_send()
    corner_in[corner_me] = corner[corner_me]
    total = corner_in[0] + corner_in[1] + corner_in[2] + corner_in[3]
    depth_in[depth] = total
    for step in range(1, 8):
        other = lax.rem(depth + step, 8)
        remote(
            depth_in.at[depth],
            depth_in.at[depth],
            c_send.at[other],
            c_arrive.at[depth],
            (rep, blk_of(part, other, core)),
        ).start()
    for step in range(1, 8):
        other = lax.rem(depth + step, 8)
        copy = remote(
            depth_in.at[depth],
            depth_in.at[other],
            c_send.at[other],
            c_arrive.at[other],
            (rep, blk_of(part, other, core)),
        )
        copy.wait_recv()
        copy.wait_send()
    total = depth_in[0]
    for index in range(1, 8):
        total = total + depth_in[index]
    full_corner[corner_me] = total
    for step in range(1, 4):
        other = lax.rem(corner_me + step, 4)
        remote(
            full_corner.at[corner_me],
            full_corner.at[corner_me],
            d_send.at[other],
            d_arrive.at[corner_me],
            corner_device(other),
        ).start()
    for step in range(1, 4):
        other = lax.rem(corner_me + step, 4)
        copy = remote(
            full_corner.at[corner_me],
            full_corner.at[other],
            d_send.at[other],
            d_arrive.at[other],
            corner_device(other),
        )
        copy.wait_recv()
        copy.wait_send()
    full[rep] = full_corner[...]
    for step in range(1, REP):
        other = lax.rem(rep + step, REP)
        remote(full.at[rep], full.at[rep], e_send.at[other], e_arrive.at[rep], (other, blk)).start()
    for step in range(1, REP):
        other = lax.rem(rep + step, REP)
        copy = remote(
            full.at[rep], full.at[other], e_send.at[other], e_arrive.at[other], (other, blk)
        )
        copy.wait_recv()
        copy.wait_send()
    for index in range(REP * 6):
        group, inner = index // 6, index % 6
        left, right = 2 * inner, 2 * inner + 1
        row = jnp.concatenate(
            [full[group, left // 3, left % 3], full[group, right // 3, right % 3]], axis=1
        )
        if index * 8 < in_rows:
            grad_in[index * 8 : index * 8 + 8, :] = row
        else:
            start_row = index * 8 - in_rows
            grad_out[start_row : start_row + 8, :] = row[:, :CLASSES]

    def drain(piece, carry):
        for direction in range(2):
            for step in range(SEC - 1):
                remote(
                    low_in.at[0, piece],
                    low_in.at[0, piece],
                    chain_send.at[direction, step, piece],
                    chain_arrive.at[0, 0, piece],
                    (rep, down),
                ).wait_send()
        @pl.when(jnp.logical_not(jnp.logical_and(rep == 0, piece == 0)))
        def _():
            low_final(piece).wait_send()

        high_final(piece).wait_send()
        return carry

    lax.fori_loop(0, REP, drain, 0)


def on_device(
    features,
    node_ids,
    labels,
    train_mask,
    tile_values,
    tile_place,
    tile_count,
    weight_in,
    weight_out,
    class_bias,
):
    width = features.shape[-1]
    own_rows = features.shape[1]
    scale = 1.0 / math.sqrt(own_rows * REP * BLK)
    tiles = tile_values[0, 0]
    place = tile_place[0, 0]
    count = tile_count[0, 0]
    shape = jax.ShapeDtypeStruct
    padded_out = jnp.pad(weight_out, ((0, 0), (0, WIDE - CLASSES)))
    padded_bias = jnp.pad(class_bias, (0, WIDE - CLASSES))[None, :]
    ids = node_ids.reshape(own_rows, 1)
    label_column = labels.reshape(own_rows, 1)
    mask_column = train_mask.reshape(own_rows, 1)

    sections = pl.pallas_call(
        first_kernel,
        out_shape=shape((SEC, 2, REP, TILE, width), BF16),
        in_specs=[whole()],
        out_specs=whole(),
        scratch_shapes=list(SPREAD_SEMS),
        compiler_params=params(0),
        name="spread_features",
    )(features.reshape(2, TILE, width))
    partial = pl.pallas_call(
        forward_kernel,
        out_shape=shape((2 * REP, TILE, width), F32),
        in_specs=[in_smem(), in_smem(), whole(), whole()],
        out_specs=whole(),
        scratch_shapes=[pltpu.VMEM((2 * REP, TILE, width), F32)],
        compiler_params=params(None),
        name="aggregate_features",
    )(place, count, tiles, sections)
    z_input, dropped, slope_factor, sections = pl.pallas_call(
        hidden_kernel,
        out_shape=(
            shape((own_rows, width), BF16),
            shape((own_rows, WIDE), BF16),
            shape((own_rows, WIDE), F32),
            shape((SEC, 2, REP, TILE, WIDE), BF16),
        ),
        in_specs=[whole()] * 4,
        out_specs=[whole()] * 4,
        scratch_shapes=[
            pltpu.VMEM((REP, own_rows, width), F32),
            pltpu.VMEM((2, TILE, WIDE), BF16),
            *GROUP_SEMS,
            *SPREAD_SEMS,
        ],
        compiler_params=params(1),
        name="hidden",
    )(partial.reshape(REP, own_rows, width), ids, weight_in, padded_out)
    partial = pl.pallas_call(
        forward_kernel,
        out_shape=shape((2 * REP, TILE, WIDE), BF16),
        in_specs=[in_smem(), in_smem(), whole(), whole()],
        out_specs=whole(),
        scratch_shapes=[pltpu.VMEM((2 * REP, TILE, WIDE), F32)],
        compiler_params=params(None),
        name="aggregate_hidden",
    )(place, count, tiles, sections)
    logits, slopes = pl.pallas_call(
        functools.partial(class_kernel, scale),
        out_shape=(
            shape((own_rows, CLASSES), F32),
            shape((REP, own_rows, WIDE), BF16),
        ),
        in_specs=[whole()] * 4,
        out_specs=[whole()] * 2,
        scratch_shapes=[
            pltpu.VMEM((REP, own_rows, WIDE), BF16),
            *GROUP_SEMS,
            *GROUP_SEMS,
        ],
        compiler_params=params(2),
        name="classes",
    )(partial.reshape(REP, own_rows, WIDE), label_column, mask_column, padded_bias)
    parts = pl.pallas_call(
        backward_kernel,
        out_shape=shape((SEC, 2, REP, TILE, WIDE), BF16),
        in_specs=[in_smem(), in_smem(), whole(), whole()],
        out_specs=whole(),
        scratch_shapes=[pltpu.VMEM((SEC, 2, REP, TILE, WIDE), F32)],
        compiler_params=params(None),
        name="aggregate_back",
    )(place, count, tiles, slopes.reshape(2 * REP, TILE, WIDE))
    chunk = (width + WIDE) // REP
    dma = pltpu.SemaphoreType.DMA
    grad_in, grad_out = pl.pallas_call(
        last_kernel,
        out_shape=(shape((width, WIDE), F32), shape((WIDE, CLASSES), F32)),
        in_specs=[whole()] * 5,
        out_specs=[whole()] * 2,
        scratch_shapes=[
            pltpu.VMEM((SEC - 1, REP, TILE, WIDE), BF16),
            pltpu.VMEM((SEC - 1, REP, TILE, WIDE), BF16),
            pltpu.VMEM((SEC - 1, REP, TILE, WIDE), BF16),
            pltpu.VMEM((SEC - 1, REP, TILE, WIDE), BF16),
            pltpu.VMEM((2, REP, TILE, WIDE), BF16),
            pltpu.VMEM((2, REP, TILE, WIDE), BF16),
            pltpu.VMEM((own_rows, WIDE), BF16),
            pltpu.VMEM((REP, chunk, WIDE), F32),
            pltpu.VMEM((REP, chunk, WIDE), F32),
            pltpu.VMEM((4, 3, 8, 128), F32),
            pltpu.VMEM((4, 3, 8, 128), F32),
            pltpu.VMEM((8, 3, 8, 128), F32),
            pltpu.VMEM((4, 3, 8, 128), F32),
            pltpu.VMEM((REP, 4, 3, 8, 128), F32),
            dma((2, SEC - 1, REP)),
            dma((2, SEC - 1, REP)),
            dma((2, REP)),
            dma((2, REP)),
            dma((REP,)),
            dma((REP,)),
            dma((4,)),
            dma((4,)),
            dma((8,)),
            dma((8,)),
            dma((4,)),
            dma((4,)),
            dma((REP,)),
            dma((REP,)),
        ],
        compiler_params=params(3),
        name="gradients",
    )(parts, z_input, dropped, slope_factor, padded_out)
    return (logits[None], grad_in, grad_out)


def solution(mesh):
    placed = (
        P("blk", "rep", None),
        P("blk", "rep"),
        P("blk", "rep"),
        P("blk", "rep"),
        P("blk", "rep", None, None, None, None),
        P("blk", "rep", None, None),
        P("blk", "rep", None),
        P(),
        P(),
        P(),
    )
    return jax.shard_map(
        on_device,
        mesh=mesh,
        in_specs=placed,
        out_specs=(P("blk", "rep", None), P(), P()),
        check_vma=False,
    )
```

```python
import functools
import math

import jax
import jax.numpy as jnp
from jax import lax
from jax.experimental import pallas as pl
from jax.experimental.pallas import tpu as pltpu
from jax.sharding import PartitionSpec as P

MESH = pl.DeviceIdType.MESH
F32 = jnp.float32
BF16 = jnp.bfloat16
REP = 8
BLK = 32
SEC = 4
TILE = 128
SLOTS = 16
WIDE = 256
CLASSES = 172
LANES = 128
PACKED = 192
DEPTH = 8
VMEM_LIMIT = 56 << 20


def whole():
    return pl.BlockSpec(memory_space=pltpu.VMEM)


def in_smem():
    return pl.BlockSpec(memory_space=pltpu.SMEM)


def params(collective):
    if collective is None:
        return pltpu.CompilerParams(vmem_limit_bytes=VMEM_LIMIT)
    return pltpu.CompilerParams(
        collective_id=collective, has_side_effects=True, vmem_limit_bytes=VMEM_LIMIT
    )


def where_am_i():
    return lax.axis_index("rep"), lax.axis_index("blk")


def remote(source, target, send, arrive, device):
    return pltpu.make_async_remote_copy(
        src_ref=source,
        dst_ref=target,
        send_sem=send,
        recv_sem=arrive,
        device_id=device,
        device_id_type=MESH,
    )


def landed(target, send, arrive, device):
    remote(target, target, send, arrive, device).wait_recv()


def greet(device):
    pl.semaphore_signal(
        pltpu.get_barrier_semaphore(), inc=1, device_id=device, device_id_type=MESH
    )


def greet_group():
    rep, blk = where_am_i()
    for step in range(1, REP):
        greet((lax.rem(rep + step, REP), blk))
    return REP - 1


def blk_of(part, depth, core):
    return (part * (BLK // 4) + depth) * 2 + core


class Spot:
    def __init__(self):
        self.rep = lax.axis_index("rep")
        self.blk = lax.axis_index("blk")
        self.core = lax.rem(self.blk, 2)
        self.depth = lax.rem(self.blk // 2, DEPTH)
        self.part = self.blk // 16
        self.here = (self.rep, self.blk)
        self.up = (self.rep, lax.rem(self.blk + 1, BLK))
        self.down = (self.rep, lax.rem(self.blk + BLK - 1, BLK))
        low_block = lax.rem(self.blk - SEC * self.rep + BLK, BLK)
        high_block = lax.rem(self.blk - SEC * self.rep - (SEC - 1) + 2 * BLK, BLK)
        self.low_relay = (low_block // 16) * 16 + lax.rem(self.blk, 16)
        self.high_relay = blk_of(high_block // 16, self.depth, 1 - self.core)
        self.own_relay = self.low_relay == self.blk

    def line(self, step):
        return (self.rep, blk_of(self.part, lax.rem(self.depth + step + DEPTH, DEPTH), self.core))

    def local(self, piece):
        return jnp.logical_and(self.own_relay, piece == self.rep)

    def targets(self, half, slot):
        offset = 2 * slot + half * (1 + self.core)
        source = blk_of(self.part, lax.rem(self.depth - offset + 2 * DEPTH, DEPTH), self.core)
        for other in (slot, slot + 4):
            yield other, (other, lax.rem(source + (SEC - 1) * half + SEC * other, BLK))


def greet_line(spot):
    for step in (-2, -1, 1, 2):
        greet(spot.line(step))
    return 4


def greet_spread(spot):
    for other in range(REP):
        @pl.when(jnp.logical_not(spot.local(other)))
        def _(other=other):
            greet((other, spot.low_relay))
        greet((other, spot.high_relay))
    greet(spot.up)
    greet(spot.down)
    return greet_line(spot) + 2 * REP + 2 - jnp.where(spot.own_relay, 1, 0)


def greet_fold(spot):
    for slot in range(4):
        for half in range(2):
            for other, device in spot.targets(half, slot):
                if half == 0:
                    same = jnp.logical_and(other == spot.rep, device[1] == spot.blk)

                    @pl.when(jnp.logical_not(same))
                    def _(device=device):
                        greet(device)
                else:
                    greet(device)
    greet(spot.up)
    greet(spot.down)
    return greet_line(spot) + 2 * REP + 2 - jnp.where(spot.own_relay, 1, 0)


def spread(spot, shard, sections, relay, line_send, line_arrive, send, chain_send, arrive):
    rep, blk, core, here = spot.rep, spot.blk, spot.core, spot.here
    dummy = chain_send.at[0, 0, 0]

    def line_copy(half, source, slot, step):
        return remote(
            source,
            relay.at[half, slot],
            line_send.at[half, slot],
            line_arrive.at[half, slot],
            spot.line(step),
        )

    def line_wait(half, slot):
        landed(relay.at[half, slot], dummy, line_arrive.at[half, slot], here)

    def hand_on(half, slot, source):
        section = (SEC - 1) * half
        for other, device in spot.targets(half, slot):
            copy = remote(
                source,
                sections.at[section, half, rep],
                send.at[half, other],
                arrive.at[section, half, rep],
                device,
            )
            if half == 0:
                same = jnp.logical_and(other == rep, device[1] == blk)

                @pl.when(same)
                def _(source=source):
                    sections[0, 0, rep] = source[...]

                @pl.when(jnp.logical_not(same))
                def _(copy=copy):
                    copy.start()
            else:
                copy.start()

    direct = [
        line_copy(0, shard.at[0], 1, 2),
        line_copy(0, shard.at[0], 3, -2),
        line_copy(1, shard.at[1], 0, 1 + core),
        line_copy(1, shard.at[1], 3 - core, -1 - core),
    ]
    for copy in direct:
        copy.start()
    hand_on(0, 0, shard.at[0])

    @pl.when(core == 1)
    def _():
        hand_on(1, 3, shard.at[1])

    line_wait(1, 3 - core)
    back = line_copy(1, relay.at[1, 3 - core], 2 - core, -2)
    back.start()
    line_wait(1, 0)
    forth = line_copy(1, relay.at[1, 0], 1, 2)

    @pl.when(core == 0)
    def _():
        forth.start()

    line_wait(0, 1)
    onward = line_copy(0, relay.at[0, 1], 2, 2)
    onward.start()
    hand_on(1, 0, relay.at[1, 0])
    hand_on(1, 3 - core, relay.at[1, 3 - core])
    hand_on(0, 1, relay.at[0, 1])
    line_wait(0, 3)
    hand_on(0, 3, relay.at[0, 3])
    line_wait(1, 2 - core)
    hand_on(1, 2 - core, relay.at[1, 2 - core])

    @pl.when(core == 0)
    def _():
        line_wait(1, 1)
        hand_on(1, 1, relay.at[1, 1])

    line_wait(0, 2)
    hand_on(0, 2, relay.at[0, 2])

    def hop(index, carry):
        section = index // REP
        step = lax.rem(index, REP)
        piece = lax.rem(rep + REP - step, REP)
        other_section = SEC - 1 - section

        @pl.when(jnp.logical_not(jnp.logical_and(spot.local(piece), section == 0)))
        def _():
            landed(
                sections.at[section, 0, piece], dummy, arrive.at[section, 0, piece], here
            )

        remote(
            sections.at[section, 0, piece],
            sections.at[section + 1, 0, piece],
            chain_send.at[0, section, piece],
            arrive.at[section + 1, 0, piece],
            spot.up,
        ).start()
        landed(
            sections.at[other_section, 1, piece],
            dummy,
            arrive.at[other_section, 1, piece],
            here,
        )
        remote(
            sections.at[other_section, 1, piece],
            sections.at[other_section - 1, 1, piece],
            chain_send.at[1, section, piece],
            arrive.at[other_section - 1, 1, piece],
            spot.down,
        ).start()
        return carry

    lax.fori_loop(0, (SEC - 1) * REP, hop, 0)

    def finish(piece, carry):
        landed(
            sections.at[SEC - 1, 0, piece], dummy, arrive.at[SEC - 1, 0, piece], here
        )
        landed(sections.at[0, 1, piece], dummy, arrive.at[0, 1, piece], here)
        for direction in range(2):
            for section in range(SEC - 1):
                remote(
                    sections.at[0, 1, piece],
                    sections.at[0, 1, piece],
                    chain_send.at[direction, section, piece],
                    arrive.at[0, 1, piece],
                    here,
                ).wait_send()
        return carry

    lax.fori_loop(0, REP, finish, 0)
    for copy in direct:
        copy.wait_send()
    back.wait_send()
    onward.wait_send()

    @pl.when(core == 0)
    def _():
        forth.wait_send()

    for other in range(REP):
        for half in range(2):
            done = remote(
                shard.at[half], shard.at[half], send.at[half, other], arrive.at[0, 0, 0], here
            )
            if half == 0:
                @pl.when(jnp.logical_not(spot.local(other)))
                def _(done=done):
                    done.wait_send()
            else:
                done.wait_send()


def spread_scratch(height):
    dma = pltpu.SemaphoreType.DMA
    return [
        pltpu.VMEM((2, 4, height, LANES), BF16),
        dma((2, 4)),
        dma((2, 4)),
        dma((2, REP)),
        dma((2, SEC - 1, REP)),
        dma((SEC, 2, REP)),
    ]


def fold(
    spot,
    parts,
    low_in,
    high_in,
    low_out,
    high_out,
    final_out,
    final_in,
    line_out,
    line_in,
    chain_send,
    chain_arrive,
    final_send,
    final_arrive,
    line_send,
    line_arrive,
):
    rep, blk, core, here = spot.rep, spot.blk, spot.core, spot.here
    dummy = chain_send.at[0, 0, 0]

    def start(piece, carry):
        remote(
            parts.at[SEC - 1, 0, piece],
            low_in.at[SEC - 2, piece],
            chain_send.at[0, 0, piece],
            chain_arrive.at[0, SEC - 2, piece],
            spot.down,
        ).start()
        remote(
            parts.at[0, 1, piece],
            high_in.at[0, piece],
            chain_send.at[1, 0, piece],
            chain_arrive.at[1, 0, piece],
            spot.up,
        ).start()
        return carry

    lax.fori_loop(0, REP, start, 0)

    def hop(index, carry):
        step = index // REP
        piece = lax.rem(index, REP)
        low_section = SEC - 2 - step
        landed(low_in.at[low_section, piece], dummy, chain_arrive.at[0, low_section, piece], here)
        low_out[low_section, piece] = (
            low_in[low_section, piece].astype(F32) + parts[low_section, 0, piece].astype(F32)
        ).astype(BF16)
        remote(
            low_out.at[low_section, piece],
            low_in.at[low_section - 1, piece],
            chain_send.at[0, step + 1, piece],
            chain_arrive.at[0, low_section - 1, piece],
            spot.down,
        ).start()
        landed(high_in.at[step, piece], dummy, chain_arrive.at[1, step, piece], here)
        high_out[step, piece] = (
            high_in[step, piece].astype(F32) + parts[step + 1, 1, piece].astype(F32)
        ).astype(BF16)
        remote(
            high_out.at[step, piece],
            high_in.at[step + 1, piece],
            chain_send.at[1, step + 1, piece],
            chain_arrive.at[1, step + 1, piece],
            spot.up,
        ).start()
        return carry

    lax.fori_loop(0, (SEC - 2) * REP, hop, 0)

    def final_copy(half, piece):
        return remote(
            final_out.at[half, piece],
            final_in.at[half, rep],
            final_send.at[half, piece],
            final_arrive.at[half, rep],
            (piece, spot.low_relay if half == 0 else spot.high_relay),
        )

    def final(index, carry):
        piece = lax.rem(index + rep, REP)
        landed(low_in.at[0, piece], dummy, chain_arrive.at[0, 0, piece], here)
        final_out[0, piece] = (
            low_in[0, piece].astype(F32) + parts[0, 0, piece].astype(F32)
        ).astype(BF16)

        @pl.when(spot.local(piece))
        def _():
            final_in[0, rep] = final_out[0, piece]

        @pl.when(jnp.logical_not(spot.local(piece)))
        def _():
            final_copy(0, piece).start()

        landed(high_in.at[SEC - 2, piece], dummy, chain_arrive.at[1, SEC - 2, piece], here)
        final_out[1, piece] = (
            high_in[SEC - 2, piece].astype(F32) + parts[SEC - 1, 1, piece].astype(F32)
        ).astype(BF16)
        final_copy(1, piece).start()
        return carry

    lax.fori_loop(0, REP, final, 0)

    def pair(half, slot):
        for other in (slot, slot + 4):
            if half == 0:
                @pl.when(jnp.logical_not(spot.local(other)))
                def _(other=other):
                    landed(
                        final_in.at[0, other], dummy, final_arrive.at[0, other], here
                    )
            else:
                landed(final_in.at[1, other], dummy, final_arrive.at[1, other], here)
        return final_in[half, slot].astype(F32) + final_in[half, slot + 4].astype(F32)

    def line_copy(half, index, step):
        return remote(
            line_out.at[half, index],
            line_in.at[half, index],
            line_send.at[half, index],
            line_arrive.at[half, index],
            spot.line(step),
        )

    def line_wait(half, index):
        landed(line_in.at[half, index], dummy, line_arrive.at[half, index], here)
        return line_in[half, index].astype(F32)

    low_far = line_copy(0, 0, -2)
    line_out[0, 0] = pair(0, 2).astype(BF16)
    low_far.start()
    high_far = line_copy(1, 0, 2)
    line_out[1, 0] = pair(1, 2 - core).astype(BF16)
    high_far.start()
    high_side = line_copy(1, 1, -2)

    @pl.when(core == 0)
    def _():
        line_out[1, 1] = pair(1, 1).astype(BF16)
        high_side.start()

    low_back = line_copy(0, 1, 2)
    line_out[0, 1] = pair(0, 3).astype(BF16)
    low_back.start()
    low_near = line_copy(0, 2, -2)
    line_out[0, 2] = (pair(0, 1) + line_wait(0, 0)).astype(BF16)
    low_near.start()
    high_up = line_copy(1, 2, 1 + core)
    line_out[1, 2] = (pair(1, 3 - core) + line_wait(1, 0)).astype(BF16)
    high_up.start()
    high_down = line_copy(1, 3, -1 - core)

    @pl.when(core == 0)
    def _():
        line_out[1, 3] = (pair(1, 0) + line_wait(1, 1)).astype(BF16)

    @pl.when(core == 1)
    def _():
        line_out[1, 3] = pair(1, 0).astype(BF16)
        line_in[1, 1] = pair(1, 3).astype(BF16)

    high_down.start()
    low = pair(0, 0) + line_wait(0, 1) + line_wait(0, 2)
    high = line_wait(1, 2) + line_wait(1, 3)
    high = high + jnp.where(core == 1, line_in[1, 1].astype(F32), 0.0)

    def drain(piece, carry):
        for direction in range(2):
            for step in range(SEC - 1):
                remote(
                    low_in.at[0, piece],
                    low_in.at[0, piece],
                    chain_send.at[direction, step, piece],
                    dummy,
                    here,
                ).wait_send()

        @pl.when(jnp.logical_not(spot.local(piece)))
        def _():
            final_copy(0, piece).wait_send()

        final_copy(1, piece).wait_send()
        return carry

    lax.fori_loop(0, REP, drain, 0)
    for copy in (low_far, high_far, low_back, low_near, high_up, high_down):
        copy.wait_send()

    @pl.when(core == 0)
    def _():
        high_side.wait_send()

    return low, high


def fold_scratch(height):
    dma = pltpu.SemaphoreType.DMA
    chain = pltpu.VMEM((SEC - 1, REP, height, LANES), BF16)
    final = pltpu.VMEM((2, REP, height, LANES), BF16)
    line = pltpu.VMEM((2, 4, height, LANES), BF16)
    return [
        chain,
        chain,
        chain,
        chain,
        final,
        final,
        line,
        line,
        dma((2, SEC - 1, REP)),
        dma((2, SEC - 1, REP)),
        dma((2, REP)),
        dma((2, REP)),
        dma((2, 4)),
        dma((2, 4)),
    ]


def pack(values):
    half = TILE // 2
    lanes = lax.broadcasted_iota(jnp.int32, (half, LANES), 1)
    rest = jnp.where(
        lanes < half,
        values[:half, LANES:],
        pltpu.roll(values[half:, LANES:], half, 1),
    )
    return jnp.concatenate([values[:, :LANES], rest], axis=0).astype(BF16)


def unpack(packed):
    half = TILE // 2
    rest = packed[TILE:]
    turned = jnp.concatenate([rest[:, half:], rest[:, :half]], axis=1)
    return jnp.concatenate(
        [packed[:TILE], jnp.concatenate([rest, turned], axis=0)], axis=1
    )


def group_send(pieces, landing, send, arrive):
    rep, blk = where_am_i()
    for step in range(1, REP):
        other = lax.rem(rep + step, REP)
        remote(
            pieces.at[other], landing.at[rep], send.at[other], arrive.at[rep], (other, blk)
        ).start()


def group_wait(pieces, landing, send, arrive):
    rep, blk = where_am_i()
    for step in range(1, REP):
        other = lax.rem(rep + step, REP)
        copy = remote(
            pieces.at[other], landing.at[other], send.at[other], arrive.at[other], (other, blk)
        )
        copy.wait_recv()
        copy.wait_send()


def group_sum(pieces, landing):
    rep, blk = where_am_i()
    landing[rep] = pieces[rep]
    total = landing[0].astype(F32)
    for index in range(1, REP):
        total = total + landing[index].astype(F32)
    return total


GROUP_SEMS = (pltpu.SemaphoreType.DMA((REP,)), pltpu.SemaphoreType.DMA((REP,)))


def keep_factor(ids):
    columns = lax.broadcasted_iota(jnp.int32, (1, WIDE), 1)
    mixed = ids * 73244475 + columns * 19349663 + 12345
    mixed = mixed ^ jnp.right_shift(mixed, 15)
    mixed = mixed * 40503
    mixed = mixed ^ jnp.right_shift(mixed, 13)
    return jnp.where(jnp.bitwise_and(mixed, 3) != 0, F32(4.0 / 3.0), F32(0.0))


def first_kernel(x, sections, *spread_refs):
    spot = Spot()
    waits = greet_spread(spot)
    pl.semaphore_wait(pltpu.get_barrier_semaphore(), waits)
    spread(spot, x, sections, *spread_refs)


def forward_kernel(place, count, tiles, sections, out, total):
    total[...] = jnp.zeros_like(total)
    for section in range(SEC):
        live = count[section]
        for group in range(SLOTS // 4):
            @pl.when(group * 4 < live)
            def _(section=section, group=group):
                for slot in range(group * 4, group * 4 + 4):
                    spot = place[section, slot]
                    row = spot // SLOTS
                    column = lax.rem(spot, SLOTS)
                    source = sections[section, lax.rem(column, 2), column // 2]
                    if source.shape[0] == PACKED:
                        source = unpack(source)
                    product = jnp.dot(
                        tiles[section, slot], source, preferred_element_type=F32
                    )
                    flag = jnp.where(slot < live, F32(1.0), F32(0.0))
                    total[row] = total[row] + product * flag
    if out.shape[1] == PACKED:
        for row in range(out.shape[0]):
            out[row] = pack(total[row])
    else:
        out[...] = total[...]


def backward_kernel(place, count, tiles, rows, out, total):
    total[...] = jnp.zeros_like(total)
    for section in range(SEC):
        live = count[section]
        for group in range(SLOTS // 4):
            @pl.when(group * 4 < live)
            def _(section=section, group=group):
                for slot in range(group * 4, group * 4 + 4):
                    spot = place[section, slot]
                    row = spot // SLOTS
                    column = lax.rem(spot, SLOTS)
                    product = lax.dot_general(
                        tiles[section, slot],
                        unpack(rows[row]),
                        (((0,), (0,)), ((), ())),
                        preferred_element_type=F32,
                    )
                    flag = jnp.where(slot < live, F32(1.0), F32(0.0))
                    half = lax.rem(column, 2)
                    piece = column // 2
                    total[section, half, piece] = total[section, half, piece] + product * flag
    for section in range(SEC):
        for piece in range(REP):
            for half in range(2):
                out[section, half, piece] = pack(total[section, half, piece])


def hidden_kernel(
    partial,
    ids,
    weight_in,
    weight_out,
    z_out,
    dropped_out,
    slope_factor,
    sections,
    landing,
    shard,
    group_sems_send,
    group_sems_arrive,
    *spread_refs,
):
    spot = Spot()
    waits = greet_group() + greet_spread(spot)
    pl.semaphore_wait(pltpu.get_barrier_semaphore(), waits)
    group_send(partial, landing, group_sems_send, group_sems_arrive)
    group_wait(partial, landing, group_sems_send, group_sems_arrive)
    z_input = group_sum(partial, landing).astype(BF16)
    z_out[...] = z_input
    pre_act = jnp.dot(z_input, weight_in[...], preferred_element_type=F32)
    kept = keep_factor(ids[...])
    dropped = (jnp.maximum(pre_act, 0.0) * kept).astype(BF16)
    dropped_out[...] = dropped
    slope_factor[...] = jnp.where(pre_act > 0, kept, 0.0)
    mapped = jnp.dot(dropped, weight_out[...], preferred_element_type=F32)
    shard[0] = pack(mapped[:TILE])
    shard[1] = pack(mapped[TILE:])
    spread(spot, shard, sections, *spread_refs)


def class_kernel(
    scale,
    partial,
    labels,
    mask,
    bias,
    logits_out,
    slopes,
    landing,
    send,
    arrive,
    slope_send,
    slope_arrive,
):
    waits = greet_group()
    rep, blk = where_am_i()
    pl.semaphore_wait(pltpu.get_barrier_semaphore(), waits)
    group_send(partial, landing, send, arrive)
    group_wait(partial, landing, send, arrive)
    summed = group_sum(partial, landing)
    logits = jnp.concatenate([unpack(summed[:PACKED]), unpack(summed[PACKED:])], axis=0) + bias[...]
    logits_out[...] = logits[:, :CLASSES]
    columns = lax.broadcasted_iota(jnp.int32, logits.shape, 1)
    real = columns < CLASSES
    top = jnp.max(jnp.where(real, logits, -jnp.inf), axis=1, keepdims=True)
    powers = jnp.where(real, jnp.exp(logits - top), 0.0)
    likelihood = powers / jnp.sum(powers, axis=1, keepdims=True)
    onehot = jnp.where(columns == labels[...], 1.0, 0.0)
    slope = (likelihood - onehot) * mask[...].astype(F32) * scale
    slopes[rep] = jnp.concatenate([pack(slope[:TILE]), pack(slope[TILE:])], axis=0)
    for step in range(1, REP):
        other = lax.rem(rep + step, REP)
        remote(
            slopes.at[rep], slopes.at[rep], slope_send.at[other], slope_arrive.at[rep], (other, blk)
        ).start()
    for step in range(1, REP):
        other = lax.rem(rep + step, REP)
        copy = remote(
            slopes.at[rep], slopes.at[other], slope_send.at[other], slope_arrive.at[other], (other, blk)
        )
        copy.wait_recv()
        copy.wait_send()


def last_kernel(
    parts,
    z_input,
    dropped,
    slope_factor,
    weight_out,
    grad_in,
    grad_out,
    terms,
    landing,
    corner,
    corner_in,
    depth_in,
    full_corner,
    full,
    a_send,
    a_arrive,
    b_send,
    b_arrive,
    c_send,
    c_arrive,
    d_send,
    d_arrive,
    e_send,
    e_arrive,
    *fold_refs,
):
    spot = Spot()
    rep, blk, core, depth, part = spot.rep, spot.blk, spot.core, spot.depth, spot.part
    waits = greet_group() + greet_fold(spot)
    corner_me = part * 2 + core
    for step in range(1, 4):
        other = lax.rem(corner_me + step, 4)
        greet((rep, blk_of(other // 2, depth, lax.rem(other, 2))))
    for step in range(1, 8):
        greet((rep, blk_of(part, lax.rem(depth + step, 8), core)))
    pl.semaphore_wait(pltpu.get_barrier_semaphore(), waits + 10)

    low, high = fold(spot, parts, *fold_refs)
    back = jnp.concatenate([unpack(low.astype(BF16)), unpack(high.astype(BF16))], axis=0)
    out_terms = lax.dot_general(
        dropped[...], back, (((0,), (0,)), ((), ())), preferred_element_type=F32
    )
    back_rows = lax.dot_general(
        back, weight_out[...], (((1,), (1,)), ((), ())), preferred_element_type=F32
    )
    pre_slope = (back_rows * slope_factor[...]).astype(BF16)
    in_terms = lax.dot_general(
        z_input[...], pre_slope, (((0,), (0,)), ((), ())), preferred_element_type=F32
    )
    in_rows = in_terms.shape[0]
    chunk = (in_rows + WIDE) // REP
    joined = jnp.concatenate([in_terms, out_terms], axis=0)
    for index in range(REP):
        terms[index] = joined[index * chunk : (index + 1) * chunk]
    group_send(terms, landing, a_send, a_arrive)
    group_wait(terms, landing, a_send, a_arrive)
    total = group_sum(terms, landing)
    for index in range(12):
        corner[index // 3, index % 3] = total[
            (index // 2) * 8 : (index // 2) * 8 + 8, (index % 2) * 128 : (index % 2) * 128 + 128
        ]

    def corner_device(index):
        return (rep, blk_of(index // 2, depth, lax.rem(index, 2)))

    for step in range(1, 4):
        other = lax.rem(corner_me + step, 4)
        remote(
            corner.at[other],
            corner_in.at[corner_me],
            b_send.at[other],
            b_arrive.at[corner_me],
            corner_device(other),
        ).start()
    for step in range(1, 4):
        other = lax.rem(corner_me + step, 4)
        copy = remote(
            corner.at[other],
            corner_in.at[other],
            b_send.at[other],
            b_arrive.at[other],
            corner_device(other),
        )
        copy.wait_recv()
        copy.wait_send()
    corner_in[corner_me] = corner[corner_me]
    total = corner_in[0] + corner_in[1] + corner_in[2] + corner_in[3]
    depth_in[depth] = total
    for step in range(1, 8):
        other = lax.rem(depth + step, 8)
        remote(
            depth_in.at[depth],
            depth_in.at[depth],
            c_send.at[other],
            c_arrive.at[depth],
            (rep, blk_of(part, other, core)),
        ).start()
    for step in range(1, 8):
        other = lax.rem(depth + step, 8)
        copy = remote(
            depth_in.at[depth],
            depth_in.at[other],
            c_send.at[other],
            c_arrive.at[other],
            (rep, blk_of(part, other, core)),
        )
        copy.wait_recv()
        copy.wait_send()
    total = depth_in[0]
    for index in range(1, 8):
        total = total + depth_in[index]
    full_corner[corner_me] = total
    for step in range(1, 4):
        other = lax.rem(corner_me + step, 4)
        remote(
            full_corner.at[corner_me],
            full_corner.at[corner_me],
            d_send.at[other],
            d_arrive.at[corner_me],
            corner_device(other),
        ).start()
    for step in range(1, 4):
        other = lax.rem(corner_me + step, 4)
        copy = remote(
            full_corner.at[corner_me],
            full_corner.at[other],
            d_send.at[other],
            d_arrive.at[other],
            corner_device(other),
        )
        copy.wait_recv()
        copy.wait_send()
    full[rep] = full_corner[...]
    for step in range(1, REP):
        other = lax.rem(rep + step, REP)
        remote(full.at[rep], full.at[rep], e_send.at[other], e_arrive.at[rep], (other, blk)).start()
    for step in range(1, REP):
        other = lax.rem(rep + step, REP)
        copy = remote(
            full.at[rep], full.at[other], e_send.at[other], e_arrive.at[other], (other, blk)
        )
        copy.wait_recv()
        copy.wait_send()
    for index in range(REP * 6):
        group, inner = index // 6, index % 6
        left, right = 2 * inner, 2 * inner + 1
        row = jnp.concatenate(
            [full[group, left // 3, left % 3], full[group, right // 3, right % 3]], axis=1
        )
        if index * 8 < in_rows:
            grad_in[index * 8 : index * 8 + 8, :] = row
        else:
            start_row = index * 8 - in_rows
            grad_out[start_row : start_row + 8, :] = row[:, :CLASSES]


def on_device(
    features,
    node_ids,
    labels,
    train_mask,
    tile_values,
    tile_place,
    tile_count,
    weight_in,
    weight_out,
    class_bias,
):
    width = features.shape[-1]
    own_rows = features.shape[1]
    scale = 1.0 / math.sqrt(own_rows * REP * BLK)
    tiles = tile_values[0, 0]
    place = tile_place[0, 0]
    count = tile_count[0, 0]
    shape = jax.ShapeDtypeStruct
    padded_out = jnp.pad(weight_out, ((0, 0), (0, WIDE - CLASSES)))
    padded_bias = jnp.pad(class_bias, (0, WIDE - CLASSES))[None, :]
    ids = node_ids.reshape(own_rows, 1)
    label_column = labels.reshape(own_rows, 1)
    mask_column = train_mask.reshape(own_rows, 1)

    sections = pl.pallas_call(
        first_kernel,
        out_shape=shape((SEC, 2, REP, TILE, width), BF16),
        in_specs=[whole()],
        out_specs=whole(),
        scratch_shapes=spread_scratch(TILE),
        compiler_params=params(0),
        name="spread_features",
    )(features.reshape(2, TILE, width))
    partial = pl.pallas_call(
        forward_kernel,
        out_shape=shape((2 * REP, TILE, width), F32),
        in_specs=[in_smem(), in_smem(), whole(), whole()],
        out_specs=whole(),
        scratch_shapes=[pltpu.VMEM((2 * REP, TILE, width), F32)],
        compiler_params=params(None),
        name="aggregate_features",
    )(place, count, tiles, sections)
    z_input, dropped, slope_factor, sections = pl.pallas_call(
        hidden_kernel,
        out_shape=(
            shape((own_rows, width), BF16),
            shape((own_rows, WIDE), BF16),
            shape((own_rows, WIDE), F32),
            shape((SEC, 2, REP, PACKED, LANES), BF16),
        ),
        in_specs=[whole()] * 4,
        out_specs=[whole()] * 4,
        scratch_shapes=[
            pltpu.VMEM((REP, own_rows, width), F32),
            pltpu.VMEM((2, PACKED, LANES), BF16),
            *GROUP_SEMS,
            *spread_scratch(PACKED),
        ],
        compiler_params=params(1),
        name="hidden",
    )(partial.reshape(REP, own_rows, width), ids, weight_in, padded_out)
    partial = pl.pallas_call(
        forward_kernel,
        out_shape=shape((2 * REP, PACKED, LANES), BF16),
        in_specs=[in_smem(), in_smem(), whole(), whole()],
        out_specs=whole(),
        scratch_shapes=[pltpu.VMEM((2 * REP, TILE, WIDE), F32)],
        compiler_params=params(None),
        name="aggregate_hidden",
    )(place, count, tiles, sections)
    logits, slopes = pl.pallas_call(
        functools.partial(class_kernel, scale),
        out_shape=(
            shape((own_rows, CLASSES), F32),
            shape((REP, 2 * PACKED, LANES), BF16),
        ),
        in_specs=[whole()] * 4,
        out_specs=[whole()] * 2,
        scratch_shapes=[
            pltpu.VMEM((REP, 2 * PACKED, LANES), BF16),
            *GROUP_SEMS,
            *GROUP_SEMS,
        ],
        compiler_params=params(2),
        name="classes",
    )(partial.reshape(REP, 2 * PACKED, LANES), label_column, mask_column, padded_bias)
    parts = pl.pallas_call(
        backward_kernel,
        out_shape=shape((SEC, 2, REP, PACKED, LANES), BF16),
        in_specs=[in_smem(), in_smem(), whole(), whole()],
        out_specs=whole(),
        scratch_shapes=[pltpu.VMEM((SEC, 2, REP, TILE, WIDE), F32)],
        compiler_params=params(None),
        name="aggregate_back",
    )(place, count, tiles, slopes.reshape(2 * REP, PACKED, LANES))
    chunk = (width + WIDE) // REP
    dma = pltpu.SemaphoreType.DMA
    grad_in, grad_out = pl.pallas_call(
        last_kernel,
        out_shape=(shape((width, WIDE), F32), shape((WIDE, CLASSES), F32)),
        in_specs=[whole()] * 5,
        out_specs=[whole()] * 2,
        scratch_shapes=[
            pltpu.VMEM((REP, chunk, WIDE), F32),
            pltpu.VMEM((REP, chunk, WIDE), F32),
            pltpu.VMEM((4, 3, 8, 128), F32),
            pltpu.VMEM((4, 3, 8, 128), F32),
            pltpu.VMEM((8, 3, 8, 128), F32),
            pltpu.VMEM((4, 3, 8, 128), F32),
            pltpu.VMEM((REP, 4, 3, 8, 128), F32),
            dma((REP,)),
            dma((REP,)),
            dma((4,)),
            dma((4,)),
            dma((8,)),
            dma((8,)),
            dma((4,)),
            dma((4,)),
            dma((REP,)),
            dma((REP,)),
            *fold_scratch(PACKED),
        ],
        compiler_params=params(3),
        name="gradients",
    )(parts, z_input, dropped, slope_factor, padded_out)
    return (logits[None], grad_in, grad_out)


def solution(mesh):
    placed = (
        P("blk", "rep", None),
        P("blk", "rep"),
        P("blk", "rep"),
        P("blk", "rep"),
        P("blk", "rep", None, None, None, None),
        P("blk", "rep", None, None),
        P("blk", "rep", None),
        P(),
        P(),
        P(),
    )
    return jax.shard_map(
        on_device,
        mesh=mesh,
        in_specs=placed,
        out_specs=(P("blk", "rep", None), P(), P()),
        check_vma=False,
    )
```

```python
import math

import jax
import jax.numpy as jnp
from jax import lax
from jax.experimental import pallas as pl
from jax.experimental.pallas import tpu as pltpu
from jax.sharding import PartitionSpec as P

MESH = pl.DeviceIdType.MESH
F32 = jnp.float32
BF16 = jnp.bfloat16
REP = 8
BLK = 32
SEC = 4
TILE = 128
SLOTS = 16
WIDE = 256
CLASSES = 172
LANES = 128
PACKED = 192
DEPTH = 8
NONE = SEC * SLOTS
FORWARD_ORDER = (1, 2, 0, 3)
BACKWARD_ORDER = (3, 0, 2, 1)
VMEM_LIMIT = 60 << 20


def whole():
    return pl.BlockSpec(memory_space=pltpu.VMEM)


def remote(source, target, send, arrive, device):
    return pltpu.make_async_remote_copy(
        src_ref=source,
        dst_ref=target,
        send_sem=send,
        recv_sem=arrive,
        device_id=device,
        device_id_type=MESH,
    )


def landed(target, send, arrive, device):
    remote(target, target, send, arrive, device).wait_recv()


def greet(device):
    pl.semaphore_signal(
        pltpu.get_barrier_semaphore(), inc=1, device_id=device, device_id_type=MESH
    )


def blk_of(part, depth, core):
    return (part * (BLK // 4) + depth) * 2 + core


class Spot:
    def __init__(self):
        self.rep = lax.axis_index("rep")
        self.blk = lax.axis_index("blk")
        self.core = lax.rem(self.blk, 2)
        self.depth = lax.rem(self.blk // 2, DEPTH)
        self.part = self.blk // 16
        self.here = (self.rep, self.blk)
        self.up = (self.rep, lax.rem(self.blk + 1, BLK))
        self.down = (self.rep, lax.rem(self.blk + BLK - 1, BLK))
        low_block = lax.rem(self.blk - SEC * self.rep + BLK, BLK)
        high_block = lax.rem(self.blk - SEC * self.rep - (SEC - 1) + 2 * BLK, BLK)
        self.low_relay = (low_block // 16) * 16 + lax.rem(self.blk, 16)
        self.high_relay = blk_of(high_block // 16, self.depth, 1 - self.core)
        self.own_relay = self.low_relay == self.blk
        self.corner = self.part * 2 + self.core

    def line(self, step):
        return (self.rep, blk_of(self.part, lax.rem(self.depth + step + DEPTH, DEPTH), self.core))

    def corner_device(self, index):
        return (self.rep, blk_of(index // 2, self.depth, lax.rem(index, 2)))

    def local(self, piece):
        return jnp.logical_and(self.own_relay, piece == self.rep)

    def targets(self, half, slot):
        offset = 2 * slot + half * (1 + self.core)
        source = blk_of(self.part, lax.rem(self.depth - offset + 2 * DEPTH, DEPTH), self.core)
        for other in (slot, slot + 4):
            yield other, (other, lax.rem(source + (SEC - 1) * half + SEC * other, BLK))


def greet_everyone(spot):
    for step in range(1, REP):
        greet((lax.rem(spot.rep + step, REP), spot.blk))
    for step in range(1, DEPTH):
        greet(spot.line(step))
    for step in range(1, 4):
        greet(spot.corner_device(lax.rem(spot.corner + step, 4)))
    for other in range(REP):
        @pl.when(jnp.logical_not(spot.local(other)))
        def _(other=other):
            greet((other, spot.low_relay))

        greet((other, spot.high_relay))
    for slot in range(4):
        for half in range(2):
            for other, device in spot.targets(half, slot):
                if half == 0:
                    same = jnp.logical_and(other == spot.rep, device[1] == spot.blk)

                    @pl.when(jnp.logical_not(same))
                    def _(device=device):
                        greet(device)
                else:
                    greet(device)
    greet(spot.up)
    greet(spot.down)
    count = (REP - 1) + (DEPTH - 1) + 3 + 4 * REP + 2
    return count - jnp.where(spot.own_relay, 2, 0)


class Spread:
    def __init__(self, spot, shard, sections, relay, line_send, line_arrive, send, chain_send, arrive):
        self.spot, self.shard, self.sections, self.relay = spot, shard, sections, relay
        self.line_send, self.line_arrive, self.send = line_send, line_arrive, send
        self.chain_send, self.arrive = chain_send, arrive
        self.dummy = chain_send.at[0, 0, 0]

    def line_copy(self, half, source, slot, step):
        return remote(
            source,
            self.relay.at[half, slot],
            self.line_send.at[half, slot],
            self.line_arrive.at[half, slot],
            self.spot.line(step),
        )

    def line_wait(self, half, slot):
        landed(
            self.relay.at[half, slot], self.dummy, self.line_arrive.at[half, slot], self.spot.here
        )

    def hand_on(self, half, slot, source):
        spot = self.spot
        section = (SEC - 1) * half
        for other, device in spot.targets(half, slot):
            copy = remote(
                source,
                self.sections[section].at[half * REP + spot.rep],
                self.send.at[half, other],
                self.arrive.at[section, half, spot.rep],
                device,
            )
            if half == 0:
                same = jnp.logical_and(other == spot.rep, device[1] == spot.blk)

                @pl.when(same)
                def _(source=source):
                    self.sections[0][spot.rep] = source[...]

                @pl.when(jnp.logical_not(same))
                def _(copy=copy):
                    copy.start()
            else:
                copy.start()

    def start_low(self):
        self.low = [
            self.line_copy(0, self.shard.at[0], 1, 2),
            self.line_copy(0, self.shard.at[0], 3, -2),
        ]
        for copy in self.low:
            copy.start()
        self.hand_on(0, 0, self.shard.at[0])

    def start_high(self):
        core = self.spot.core
        self.high = [
            self.line_copy(1, self.shard.at[1], 0, 1 + core),
            self.line_copy(1, self.shard.at[1], 3 - core, -1 - core),
        ]
        for copy in self.high:
            copy.start()

        @pl.when(core == 1)
        def _():
            self.hand_on(1, 3, self.shard.at[1])

    def pass_on(self):
        core, relay = self.spot.core, self.relay
        self.line_wait(0, 1)
        self.onward = self.line_copy(0, relay.at[0, 1], 2, 2)
        self.onward.start()
        self.hand_on(0, 1, relay.at[0, 1])
        self.line_wait(0, 3)
        self.hand_on(0, 3, relay.at[0, 3])
        self.line_wait(1, 3 - core)
        self.back = self.line_copy(1, relay.at[1, 3 - core], 2 - core, -2)
        self.back.start()
        self.line_wait(1, 0)
        self.forth = self.line_copy(1, relay.at[1, 0], 1, 2)

        @pl.when(core == 0)
        def _():
            self.forth.start()

        self.hand_on(1, 0, relay.at[1, 0])
        self.hand_on(1, 3 - core, relay.at[1, 3 - core])
        self.line_wait(0, 2)
        self.hand_on(0, 2, relay.at[0, 2])
        self.line_wait(1, 2 - core)
        self.hand_on(1, 2 - core, relay.at[1, 2 - core])

        @pl.when(core == 0)
        def _():
            self.line_wait(1, 1)
            self.hand_on(1, 1, relay.at[1, 1])

    def arrived(self, section, half, piece):
        landed(
            self.sections[section].at[half * REP + piece],
            self.dummy,
            self.arrive.at[section, half, piece],
            self.spot.here,
        )

    def chains(self):
        spot = self.spot
        for section in range(SEC - 1):
            other_section = SEC - 1 - section

            def hop(step, carry, section=section, other_section=other_section):
                piece = lax.rem(spot.rep + REP - step, REP)
                if section == 0:
                    @pl.when(jnp.logical_not(spot.local(piece)))
                    def _():
                        self.arrived(section, 0, piece)
                else:
                    self.arrived(section, 0, piece)
                remote(
                    self.sections[section].at[piece],
                    self.sections[section + 1].at[piece],
                    self.chain_send.at[0, section, piece],
                    self.arrive.at[section + 1, 0, piece],
                    spot.up,
                ).start()
                self.arrived(other_section, 1, piece)
                remote(
                    self.sections[other_section].at[REP + piece],
                    self.sections[other_section - 1].at[REP + piece],
                    self.chain_send.at[1, section, piece],
                    self.arrive.at[other_section - 1, 1, piece],
                    spot.down,
                ).start()
                return carry

            lax.fori_loop(0, REP, hop, 0)

    def last_arrivals(self):
        def finish(piece, carry):
            self.arrived(SEC - 1, 0, piece)
            self.arrived(0, 1, piece)
            return carry

        lax.fori_loop(0, REP, finish, 0)

    def drain(self):
        spot = self.spot
        sample = self.shard.at[0]

        def sent(semaphore):
            remote(sample, sample, semaphore, self.arrive.at[0, 0, 0], spot.here).wait_send()

        def body(piece, carry):
            for direction in range(2):
                for section in range(SEC - 1):
                    sent(self.chain_send.at[direction, section, piece])

            @pl.when(jnp.logical_not(spot.local(piece)))
            def _():
                sent(self.send.at[0, piece])

            sent(self.send.at[1, piece])
            return carry

        lax.fori_loop(0, REP, body, 0)
        for copy in (*self.low, *self.high, self.back, self.onward):
            copy.wait_send()

        @pl.when(spot.core == 0)
        def _():
            self.forth.wait_send()


def spread_scratch(height):
    dma = pltpu.SemaphoreType.DMA
    return [
        *[pltpu.VMEM((2 * REP, height, LANES), BF16)] * SEC,
        pltpu.VMEM((2, 4, height, LANES), BF16),
        dma((2, 4)),
        dma((2, 4)),
        dma((2, REP)),
        dma((2, SEC - 1, REP)),
        dma((SEC, 2, REP)),
    ]


class Scatter:
    def __init__(self, spot, pieces, landing, send, arrive):
        self.spot, self.pieces, self.landing = spot, pieces, landing
        self.send, self.arrive = send, arrive

    def copy(self, half, other, lands):
        return remote(
            self.pieces.at[half, other],
            self.landing.at[half, lands],
            self.send.at[half, other],
            self.arrive.at[half, lands],
            (other, self.spot.blk),
        )

    def put(self, half, make):
        rep = self.spot.rep

        def one(step, carry):
            other = lax.rem(rep + 1 + step, REP)
            self.pieces[half, other] = make(other)
            self.copy(half, other, rep).start()
            return carry

        lax.fori_loop(0, REP - 1, one, 0)
        self.landing[half, rep] = make(rep)

    def total(self, half):
        rep = self.spot.rep

        def one(step, carry):
            other = lax.rem(rep + 1 + step, REP)
            self.copy(half, other, other).wait_recv()
            return carry

        lax.fori_loop(0, REP - 1, one, 0)
        total = self.landing[half, 0].astype(F32)
        for index in range(1, REP):
            total = total + self.landing[half, index].astype(F32)
        return total

    def drain(self):
        def one(step, carry):
            other = lax.rem(self.spot.rep + 1 + step, REP)
            for half in range(self.pieces.shape[0]):
                self.copy(half, other, other).wait_send()
            return carry

        lax.fori_loop(0, REP - 1, one, 0)


def scatter_scratch(halves, height, width, dtype):
    dma = pltpu.SemaphoreType.DMA
    return [
        pltpu.VMEM((halves, REP, height, width), dtype),
        pltpu.VMEM((halves, REP, height, width), dtype),
        dma((halves, REP)),
        dma((halves, REP)),
    ]


def fold(
    spot,
    fill,
    parts,
    low_in,
    high_in,
    low_out,
    high_out,
    final_out,
    final_in,
    line_out,
    line_in,
    chain_send,
    chain_arrive,
    final_send,
    final_arrive,
    line_send,
    line_arrive,
):
    rep, blk, core, here = spot.rep, spot.blk, spot.core, spot.here
    dummy = chain_send.at[0, 0, 0]

    def send_low(piece):
        remote(
            parts[SEC - 1].at[piece],
            low_in.at[SEC - 2, piece],
            chain_send.at[0, 0, piece],
            chain_arrive.at[0, SEC - 2, piece],
            spot.down,
        ).start()

    def send_high(piece):
        remote(
            parts[0].at[REP + piece],
            high_in.at[0, piece],
            chain_send.at[1, 0, piece],
            chain_arrive.at[1, 0, piece],
            spot.up,
        ).start()

    fill(SEC - 1, send_low, None)
    fill(0, None, send_high)
    fill(SEC - 2, None, None)
    fill(1, None, None)

    for step in range(SEC - 2):
        low_section = SEC - 2 - step

        def hop(piece, carry, step=step, low_section=low_section):
            landed(
                low_in.at[low_section, piece], dummy, chain_arrive.at[0, low_section, piece], here
            )
            low_out[low_section, piece] = (
                low_in[low_section, piece].astype(F32) + parts[low_section][piece].astype(F32)
            ).astype(BF16)
            remote(
                low_out.at[low_section, piece],
                low_in.at[low_section - 1, piece],
                chain_send.at[0, step + 1, piece],
                chain_arrive.at[0, low_section - 1, piece],
                spot.down,
            ).start()
            landed(high_in.at[step, piece], dummy, chain_arrive.at[1, step, piece], here)
            high_out[step, piece] = (
                high_in[step, piece].astype(F32) + parts[step + 1][REP + piece].astype(F32)
            ).astype(BF16)
            remote(
                high_out.at[step, piece],
                high_in.at[step + 1, piece],
                chain_send.at[1, step + 1, piece],
                chain_arrive.at[1, step + 1, piece],
                spot.up,
            ).start()
            return carry

        lax.fori_loop(0, REP, hop, 0)

    def final_copy(half, piece):
        return remote(
            final_out.at[half, piece],
            final_in.at[half, rep],
            final_send.at[half, piece],
            final_arrive.at[half, rep],
            (piece, spot.low_relay if half == 0 else spot.high_relay),
        )

    def final(index, carry):
        piece = lax.rem(index + rep, REP)
        landed(low_in.at[0, piece], dummy, chain_arrive.at[0, 0, piece], here)
        final_out[0, piece] = (
            low_in[0, piece].astype(F32) + parts[0][piece].astype(F32)
        ).astype(BF16)

        @pl.when(spot.local(piece))
        def _():
            final_in[0, rep] = final_out[0, piece]

        @pl.when(jnp.logical_not(spot.local(piece)))
        def _():
            final_copy(0, piece).start()

        landed(high_in.at[SEC - 2, piece], dummy, chain_arrive.at[1, SEC - 2, piece], here)
        final_out[1, piece] = (
            high_in[SEC - 2, piece].astype(F32) + parts[SEC - 1][REP + piece].astype(F32)
        ).astype(BF16)
        final_copy(1, piece).start()
        return carry

    lax.fori_loop(0, REP, final, 0)

    def pair(half, slot):
        for other in (slot, slot + 4):
            if half == 0:
                @pl.when(jnp.logical_not(spot.local(other)))
                def _(other=other):
                    landed(
                        final_in.at[0, other], dummy, final_arrive.at[0, other], here
                    )
            else:
                landed(final_in.at[1, other], dummy, final_arrive.at[1, other], here)
        return final_in[half, slot].astype(F32) + final_in[half, slot + 4].astype(F32)

    def line_copy(half, index, step):
        return remote(
            line_out.at[half, index],
            line_in.at[half, index],
            line_send.at[half, index],
            line_arrive.at[half, index],
            spot.line(step),
        )

    def line_wait(half, index):
        landed(line_in.at[half, index], dummy, line_arrive.at[half, index], here)
        return line_in[half, index].astype(F32)

    low_far = line_copy(0, 0, -2)
    line_out[0, 0] = pair(0, 2).astype(BF16)
    low_far.start()
    high_far = line_copy(1, 0, 2)
    line_out[1, 0] = pair(1, 2 - core).astype(BF16)
    high_far.start()
    high_side = line_copy(1, 1, -2)

    @pl.when(core == 0)
    def _():
        line_out[1, 1] = pair(1, 1).astype(BF16)
        high_side.start()

    low_back = line_copy(0, 1, 2)
    line_out[0, 1] = pair(0, 3).astype(BF16)
    low_back.start()
    low_near = line_copy(0, 2, -2)
    line_out[0, 2] = (pair(0, 1) + line_wait(0, 0)).astype(BF16)
    low_near.start()
    high_up = line_copy(1, 2, 1 + core)
    line_out[1, 2] = (pair(1, 3 - core) + line_wait(1, 0)).astype(BF16)
    high_up.start()
    high_down = line_copy(1, 3, -1 - core)

    @pl.when(core == 0)
    def _():
        line_out[1, 3] = (pair(1, 0) + line_wait(1, 1)).astype(BF16)

    @pl.when(core == 1)
    def _():
        line_out[1, 3] = pair(1, 0).astype(BF16)
        line_in[1, 1] = pair(1, 3).astype(BF16)

    high_down.start()
    low = pair(0, 0) + line_wait(0, 1) + line_wait(0, 2)
    high = line_wait(1, 2) + line_wait(1, 3)
    high = high + jnp.where(core == 1, line_in[1, 1].astype(F32), 0.0)

    def drain_all():
        def drain(piece, carry):
            for direction in range(2):
                for step in range(SEC - 1):
                    remote(
                        low_in.at[0, piece],
                        low_in.at[0, piece],
                        chain_send.at[direction, step, piece],
                        dummy,
                        here,
                    ).wait_send()

            @pl.when(jnp.logical_not(spot.local(piece)))
            def _():
                final_copy(0, piece).wait_send()

            final_copy(1, piece).wait_send()
            return carry

        lax.fori_loop(0, REP, drain, 0)
        for copy in (low_far, high_far, low_back, low_near, high_up, high_down):
            copy.wait_send()

        @pl.when(core == 0)
        def _():
            high_side.wait_send()

    return low, high, drain_all


def fold_scratch(height):
    dma = pltpu.SemaphoreType.DMA
    chain = pltpu.VMEM((SEC - 1, REP, height, LANES), BF16)
    final = pltpu.VMEM((2, REP, height, LANES), BF16)
    line = pltpu.VMEM((2, 4, height, LANES), BF16)
    return [
        *[pltpu.VMEM((2 * REP, height, LANES), BF16)] * SEC,
        chain,
        chain,
        chain,
        chain,
        final,
        final,
        line,
        line,
        dma((2, SEC - 1, REP)),
        dma((2, SEC - 1, REP)),
        dma((2, REP)),
        dma((2, REP)),
        dma((2, 4)),
        dma((2, 4)),
    ]


def pack(values):
    half = TILE // 2
    lanes = lax.broadcasted_iota(jnp.int32, (half, LANES), 1)
    rest = jnp.where(
        lanes < half,
        values[:half, LANES:],
        pltpu.roll(values[half:, LANES:], half, 1),
    )
    return jnp.concatenate([values[:, :LANES], rest], axis=0).astype(BF16)


def unpack(packed):
    half = TILE // 2
    rest = packed[TILE:]
    turned = jnp.concatenate([rest[:, half:], rest[:, :half]], axis=1)
    return jnp.concatenate(
        [packed[:TILE], jnp.concatenate([rest, turned], axis=0)], axis=1
    )


def keep_factor(ids):
    columns = lax.broadcasted_iota(jnp.int32, (1, WIDE), 1)
    mixed = ids * 73244475 + columns * 19349663 + 12345
    mixed = mixed ^ jnp.right_shift(mixed, 15)
    mixed = mixed * 40503
    mixed = mixed ^ jnp.right_shift(mixed, 13)
    return jnp.where(jnp.bitwise_and(mixed, 3) != 0, F32(4.0 / 3.0), F32(0.0))


def column_of(row):
    lanes = lax.broadcasted_iota(jnp.int32, (TILE, LANES), 1)
    rows = lax.broadcasted_iota(jnp.int32, (TILE, LANES), 0)
    spread_out = jnp.broadcast_to(row.astype(F32), (TILE, LANES))
    return jnp.sum(jnp.where(lanes == rows, spread_out, 0.0), axis=1, keepdims=True)


def step_kernel(
    scale,
    tables,
    x,
    ids,
    labels,
    mask,
    tiles,
    weight_in,
    weight_out,
    bias,
    logits_out,
    grad_in,
    grad_out,
    wide_out,
    wide_bias,
    running,
    shard,
    z_input,
    dropped,
    slope_factor,
    slopes,
    slope_send,
    slope_arrive,
    corner,
    corner_in,
    depth_in,
    full_corner,
    full,
    b_send,
    b_arrive,
    c_send,
    c_arrive,
    d_send,
    d_arrive,
    e_send,
    e_arrive,
    *rest,
):
    rest = list(rest)

    def take(count):
        taken = rest[:count]
        del rest[:count]
        return taken

    spot = Spot()
    rep, blk = spot.rep, spot.blk
    first_sections = take(SEC)
    first_spread = Spread(spot, x, first_sections, *take(6))
    second_sections = take(SEC)
    second_spread = Spread(spot, shard, second_sections, *take(6))
    first_scatter = Scatter(spot, *take(4))
    second_scatter = Scatter(spot, *take(4))
    term_scatter = Scatter(spot, *take(4))
    parts = take(SEC)
    fold_refs = take(14)

    waits = greet_everyone(spot)
    running[NONE] = jnp.zeros((TILE, WIDE), F32)
    wide_out[...] = jnp.zeros_like(wide_out)
    wide_out[:, :CLASSES] = weight_out[...]
    wide_bias[...] = jnp.zeros_like(wide_bias)
    wide_bias[:, :CLASSES] = bias[...]
    pl.semaphore_wait(pltpu.get_barrier_semaphore(), waits)

    def products(sections, section, width):
        place = FORWARD_ORDER.index(section)

        def some(group, carry):
            made = []
            for inner in range(4):
                slot = group * 4 + inner
                entry = place * SLOTS + slot
                source = sections[section][tables[0, entry]]
                if width == WIDE:
                    source = unpack(source)
                made.append(
                    jnp.dot(
                        tiles[section * SLOTS + slot], source, preferred_element_type=F32
                    )
                )
            for inner in range(4):
                entry = place * SLOTS + group * 4 + inner
                running[entry, :, :width] = (
                    made[inner] + running[tables[1, entry], :, :width]
                )
            return carry

        lax.fori_loop(0, SLOTS // 4, some, 0)

    def first_sum(half):
        return lambda other: running[tables[2, 2 * other + half], :, :LANES]

    def second_sum(half):
        return lambda other: pack(running[tables[2, 2 * other + half]])

    first_spread.start_low()
    first_spread.start_high()
    first_spread.pass_on()
    first_spread.chains()
    products(first_sections, 1, LANES)
    products(first_sections, 2, LANES)
    first_spread.last_arrivals()
    products(first_sections, 0, LANES)
    products(first_sections, 3, LANES)
    first_scatter.put(0, first_sum(0))
    first_scatter.put(1, first_sum(1))
    first_spread.drain()

    def hidden(half):
        rows = pl.ds(half * TILE, TILE)
        z_half = first_scatter.total(half).astype(BF16)
        z_input[rows, :] = z_half
        pre_act = jnp.dot(z_half, weight_in[...], preferred_element_type=F32)
        kept = keep_factor(column_of(ids[half : half + 1, :]).astype(jnp.int32))
        active = (jnp.maximum(pre_act, 0.0) * kept).astype(BF16)
        dropped[rows, :] = active
        slope_factor[rows, :] = jnp.where(pre_act > 0, kept, 0.0)
        shard[half] = pack(jnp.dot(active, wide_out[...], preferred_element_type=F32))

    hidden(0)
    second_spread.start_low()
    hidden(1)
    second_spread.start_high()
    second_spread.pass_on()
    second_spread.chains()
    products(second_sections, 1, WIDE)
    products(second_sections, 2, WIDE)
    second_spread.last_arrivals()
    products(second_sections, 0, WIDE)
    products(second_sections, 3, WIDE)
    second_scatter.put(0, second_sum(0))
    second_scatter.put(1, second_sum(1))
    second_spread.drain()
    first_scatter.drain()

    def slope_copy(half, other, lands):
        return remote(
            slopes.at[2 * rep + half],
            slopes.at[2 * lands + half],
            slope_send.at[half, other],
            slope_arrive.at[half, lands],
            (other, blk),
        )

    def classes(half):
        logits = unpack(second_scatter.total(half)) + wide_bias[...]
        logits_out[half * TILE : (half + 1) * TILE, :] = logits[:, :CLASSES]
        columns = lax.broadcasted_iota(jnp.int32, logits.shape, 1)
        real = columns < CLASSES
        top = jnp.max(jnp.where(real, logits, -jnp.inf), axis=1, keepdims=True)
        powers = jnp.where(real, jnp.exp(jnp.where(real, logits - top, 0.0)), 0.0)
        likelihood = powers / jnp.sum(powers, axis=1, keepdims=True)
        label = column_of(labels[half : half + 1, :]).astype(jnp.int32)
        onehot = jnp.where(columns == label, 1.0, 0.0)
        chosen = column_of(mask[half : half + 1, :]) * scale
        slopes[2 * rep + half] = pack((likelihood - onehot) * chosen)
        for step in range(1, REP):
            slope_copy(half, lax.rem(rep + step, REP), rep).start()

    classes(0)
    classes(1)
    second_scatter.drain()

    def slope_waits(step, carry):
        other = lax.rem(rep + step, REP)
        for half in range(2):
            copy = remote(
                slopes.at[2 * rep + half],
                slopes.at[2 * other + half],
                slope_send.at[half, other],
                slope_arrive.at[half, other],
                (other, blk),
            )
            copy.wait_recv()
            copy.wait_send()
        return carry

    lax.fori_loop(1, REP, slope_waits, 0)

    def fill(section, send_low, send_high):
        def some(group, carry):
            made = []
            for inner in range(4):
                entry = section * SLOTS + group * 4 + inner
                made.append(
                    lax.dot_general(
                        tiles[entry],
                        unpack(slopes[tables[3, entry]]),
                        (((0,), (0,)), ((), ())),
                        preferred_element_type=F32,
                    )
                )
            for inner in range(4):
                entry = section * SLOTS + group * 4 + inner
                running[entry] = made[inner] + running[tables[4, entry]]
            return carry

        lax.fori_loop(0, SLOTS // 4, some, 0)

        def gather(piece, carry):
            order = ((0, send_low), (1, send_high))
            for half, send in order:
                column = 2 * piece + half
                parts[section][half * REP + piece] = pack(
                    running[tables[5, section * SLOTS + column]]
                )
                if send is not None:
                    send(piece)
            return carry

        lax.fori_loop(0, REP, gather, 0)

    low, high, fold_drain = fold(spot, fill, parts, *fold_refs)
    back = jnp.concatenate([unpack(low.astype(BF16)), unpack(high.astype(BF16))], axis=0)
    out_terms = lax.dot_general(
        dropped[...], back, (((0,), (0,)), ((), ())), preferred_element_type=F32
    )
    back_rows = lax.dot_general(
        back, wide_out[...], (((1,), (1,)), ((), ())), preferred_element_type=F32
    )
    pre_slope = (back_rows * slope_factor[...]).astype(BF16)
    in_terms = lax.dot_general(
        z_input[...], pre_slope, (((0,), (0,)), ((), ())), preferred_element_type=F32
    )
    in_rows = in_terms.shape[0]
    chunk = (in_rows + WIDE) // REP
    joined = jnp.concatenate([in_terms, out_terms], axis=0).astype(BF16)
    for index in range(REP):
        term_scatter.pieces[0, index] = joined[index * chunk : (index + 1) * chunk]
    for step in range(1, REP):
        term_scatter.copy(0, lax.rem(rep + step, REP), rep).start()
    term_scatter.landing[0, rep] = term_scatter.pieces[0, rep]
    fold_drain()
    total = term_scatter.total(0)
    term_scatter.drain()
    for index in range(12):
        corner[index // 3, index % 3] = total[
            (index // 2) * 8 : (index // 2) * 8 + 8, (index % 2) * LANES : (index % 2 + 1) * LANES
        ]
    me = spot.corner
    for step in range(1, 4):
        other = lax.rem(me + step, 4)
        remote(
            corner.at[other],
            corner_in.at[me],
            b_send.at[other],
            b_arrive.at[me],
            spot.corner_device(other),
        ).start()
    for step in range(1, 4):
        other = lax.rem(me + step, 4)
        copy = remote(
            corner.at[other],
            corner_in.at[other],
            b_send.at[other],
            b_arrive.at[other],
            spot.corner_device(other),
        )
        copy.wait_recv()
        copy.wait_send()
    corner_in[me] = corner[me]
    depth = spot.depth
    depth_in[depth] = corner_in[0] + corner_in[1] + corner_in[2] + corner_in[3]
    for step in range(1, DEPTH):
        remote(
            depth_in.at[depth],
            depth_in.at[depth],
            c_send.at[step],
            c_arrive.at[depth],
            spot.line(step),
        ).start()
    for step in range(1, DEPTH):
        other = lax.rem(depth + step, DEPTH)
        copy = remote(
            depth_in.at[depth],
            depth_in.at[other],
            c_send.at[step],
            c_arrive.at[other],
            spot.line(step),
        )
        copy.wait_recv()
        copy.wait_send()
    total = depth_in[0]
    for index in range(1, DEPTH):
        total = total + depth_in[index]
    full_corner[me] = total
    for step in range(1, 4):
        other = lax.rem(me + step, 4)
        remote(
            full_corner.at[me],
            full_corner.at[me],
            d_send.at[other],
            d_arrive.at[me],
            spot.corner_device(other),
        ).start()
    for step in range(1, 4):
        other = lax.rem(me + step, 4)
        copy = remote(
            full_corner.at[me],
            full_corner.at[other],
            d_send.at[other],
            d_arrive.at[other],
            spot.corner_device(other),
        )
        copy.wait_recv()
        copy.wait_send()
    full[rep] = jnp.concatenate(
        [
            jnp.concatenate(
                [
                    full_corner[(2 * row) // 3, (2 * row) % 3],
                    full_corner[(2 * row + 1) // 3, (2 * row + 1) % 3],
                ],
                axis=1,
            )
            for row in range(6)
        ],
        axis=0,
    ).astype(BF16)
    for step in range(1, REP):
        other = lax.rem(rep + step, REP)
        remote(full.at[rep], full.at[rep], e_send.at[other], e_arrive.at[rep], (other, blk)).start()
    for step in range(1, REP):
        other = lax.rem(rep + step, REP)
        copy = remote(
            full.at[rep], full.at[other], e_send.at[other], e_arrive.at[other], (other, blk)
        )
        copy.wait_recv()
        copy.wait_send()
    joined = jnp.concatenate([full[index] for index in range(REP)], axis=0).astype(F32)
    grad_in[...] = joined[:in_rows]
    grad_out[...] = joined[in_rows:, :CLASSES]


def index_tables(tile_place, tile_count):
    entries = jnp.arange(NONE, dtype=jnp.int32)
    live = (jnp.arange(SLOTS, dtype=jnp.int32)[None, :] < tile_count[:, None]).astype(jnp.int32)
    forward = list(FORWARD_ORDER)
    place_f = jnp.concatenate([tile_place[index] for index in forward])
    live_f = jnp.concatenate([live[index] for index in forward])
    place_b = tile_place.reshape(-1)
    live_b = live.reshape(-1)
    row_f, column_f = place_f // SLOTS, place_f % SLOTS
    row_b, column_b = place_b // SLOTS, place_b % SLOTS
    source_f = (column_f % 2) * REP + column_f // 2
    group = entries // SLOTS

    def latest(keys, wanted, before, live_now):
        match = (keys[None, :] == wanted[:, None]) & (live_now[None, :] > 0)
        match = match & (entries[None, :] < before[:, None])
        found = jnp.max(jnp.where(match, entries[None, :], -1), axis=1)
        return jnp.where(found < 0, NONE, found)

    everything = jnp.full((NONE,), NONE, jnp.int32)
    key_b = group * SLOTS + column_b
    return jnp.stack(
        [
            source_f,
            latest(row_f, row_f, entries, live_f),
            latest(row_f, entries, everything, live_f),
            row_b,
            latest(key_b, key_b, entries, live_b),
            latest(key_b, entries, everything, live_b),
        ]
    )


def on_device(
    features,
    node_ids,
    labels,
    train_mask,
    tile_values,
    tile_place,
    tile_count,
    weight_in,
    weight_out,
    class_bias,
):
    width = features.shape[-1]
    own_rows = features.shape[1]
    scale = 1.0 / math.sqrt(own_rows * REP * BLK)
    shape = jax.ShapeDtypeStruct
    dma = pltpu.SemaphoreType.DMA
    vmem = pltpu.VMEM
    chunk = (width + WIDE) // REP
    tables = index_tables(tile_place[0, 0], tile_count[0, 0])
    logits, grad_in, grad_out = pl.pallas_call(
        lambda *refs: step_kernel(scale, *refs),
        out_shape=(
            shape((own_rows, CLASSES), F32),
            shape((width, WIDE), F32),
            shape((WIDE, CLASSES), F32),
        ),
        in_specs=[pl.BlockSpec(memory_space=pltpu.SMEM)] + [whole()] * 8,
        out_specs=[whole()] * 3,
        scratch_shapes=[
            vmem((WIDE, WIDE), BF16),
            vmem((1, WIDE), F32),
            vmem((NONE + 1, TILE, WIDE), F32),
            vmem((2, PACKED, LANES), BF16),
            vmem((own_rows, width), BF16),
            vmem((own_rows, WIDE), BF16),
            vmem((own_rows, WIDE), F32),
            vmem((2 * REP, PACKED, LANES), BF16),
            dma((2, REP)),
            dma((2, REP)),
            vmem((4, 3, 8, LANES), F32),
            vmem((4, 3, 8, LANES), F32),
            vmem((DEPTH, 3, 8, LANES), F32),
            vmem((4, 3, 8, LANES), F32),
            vmem((REP, chunk, WIDE), BF16),
            dma((4,)),
            dma((4,)),
            dma((DEPTH,)),
            dma((DEPTH,)),
            dma((4,)),
            dma((4,)),
            dma((REP,)),
            dma((REP,)),
            *spread_scratch(TILE),
            *spread_scratch(PACKED),
            *scatter_scratch(2, TILE, LANES, F32),
            *scatter_scratch(2, PACKED, LANES, BF16),
            *scatter_scratch(1, chunk, WIDE, BF16),
            *fold_scratch(PACKED),
        ],
        compiler_params=pltpu.CompilerParams(
            collective_id=0, has_side_effects=True, vmem_limit_bytes=VMEM_LIMIT
        ),
        name="training_step",
    )(
        tables,
        features.reshape(2, TILE, width),
        node_ids.reshape(2, TILE),
        labels.reshape(2, TILE),
        train_mask.reshape(2, TILE),
        tile_values.reshape(NONE, TILE, TILE),
        weight_in,
        weight_out,
        class_bias.reshape(1, CLASSES),
    )
    return (logits[None], grad_in, grad_out)


def solution(mesh):
    placed = (
        P("blk", "rep", None),
        P("blk", "rep"),
        P("blk", "rep"),
        P("blk", "rep"),
        P("blk", "rep", None, None, None, None),
        P("blk", "rep", None, None),
        P("blk", "rep", None),
        P(),
        P(),
        P(),
    )
    return jax.shard_map(
        on_device,
        mesh=mesh,
        in_specs=placed,
        out_specs=(P("blk", "rep", None), P(), P()),
        check_vma=False,
    )
```

```python
import math

import jax
import jax.numpy as jnp
from jax import lax
from jax.experimental import pallas as pl
from jax.experimental.pallas import tpu as pltpu
from jax.sharding import PartitionSpec as P

MESH = pl.DeviceIdType.MESH
F32 = jnp.float32
BF16 = jnp.bfloat16
REP = 8
BLK = 32
SEC = 4
TILE = 128
SLOTS = 16
WIDE = 256
CLASSES = 172
LANES = 128
PACKED = 192
DEPTH = 8
NONE = SEC * SLOTS
FORWARD_ORDER = (1, 2, 0, 3)
CODED = 144
KEEP = 4.0 / 3.0
VMEM_LIMIT = 60 << 20


def whole():
    return pl.BlockSpec(memory_space=pltpu.VMEM)


def remote(source, target, send, arrive, device):
    return pltpu.make_async_remote_copy(
        src_ref=source,
        dst_ref=target,
        send_sem=send,
        recv_sem=arrive,
        device_id=device,
        device_id_type=MESH,
    )


def landed(target, send, arrive, device):
    remote(target, target, send, arrive, device).wait_recv()


def greet(device):
    pl.semaphore_signal(
        pltpu.get_barrier_semaphore(), inc=1, device_id=device, device_id_type=MESH
    )


def blk_of(part, depth, core):
    return (part * (BLK // 4) + depth) * 2 + core


class Spot:
    def __init__(self):
        self.rep = lax.axis_index("rep")
        self.blk = lax.axis_index("blk")
        self.core = lax.rem(self.blk, 2)
        self.depth = lax.rem(self.blk // 2, DEPTH)
        self.part = self.blk // 16
        self.here = (self.rep, self.blk)
        self.up = (self.rep, lax.rem(self.blk + 1, BLK))
        self.down = (self.rep, lax.rem(self.blk + BLK - 1, BLK))
        low_block = lax.rem(self.blk - SEC * self.rep + BLK, BLK)
        high_block = lax.rem(self.blk - SEC * self.rep - (SEC - 1) + 2 * BLK, BLK)
        self.low_relay = (low_block // 16) * 16 + lax.rem(self.blk, 16)
        self.high_relay = blk_of(high_block // 16, self.depth, 1 - self.core)
        self.own_relay = self.low_relay == self.blk
        self.corner = self.part * 2 + self.core

    def line(self, step):
        return (self.rep, blk_of(self.part, lax.rem(self.depth + step + DEPTH, DEPTH), self.core))

    def corner_device(self, index):
        return (self.rep, blk_of(index // 2, self.depth, lax.rem(index, 2)))

    def local(self, piece):
        return jnp.logical_and(self.own_relay, piece == self.rep)

    def targets(self, half, slot):
        offset = 2 * slot + half * (1 + self.core)
        source = blk_of(self.part, lax.rem(self.depth - offset + 2 * DEPTH, DEPTH), self.core)
        for other in (slot, slot + 4):
            yield other, (other, lax.rem(source + (SEC - 1) * half + SEC * other, BLK))


def greet_everyone(spot):
    for step in range(1, REP):
        greet((lax.rem(spot.rep + step, REP), spot.blk))
    for step in range(1, DEPTH):
        greet(spot.line(step))
    for step in range(1, 4):
        greet(spot.corner_device(lax.rem(spot.corner + step, 4)))
    for other in range(REP):
        @pl.when(jnp.logical_not(spot.local(other)))
        def _(other=other):
            greet((other, spot.low_relay))

        greet((other, spot.high_relay))
    greet(spot.up)
    greet(spot.down)
    count = (REP - 1) + (DEPTH - 1) + 3 + 2 * REP + 2
    return count - jnp.where(spot.own_relay, 1, 0)


class Spread:
    def __init__(self, spot, shard, sections, relay, line_send, line_arrive, send, chain_send, arrive):
        self.spot, self.shard, self.sections, self.relay = spot, shard, sections, relay
        self.line_send, self.line_arrive, self.send = line_send, line_arrive, send
        self.chain_send, self.arrive = chain_send, arrive
        self.dummy = chain_send.at[0, 0, 0]

    def line_copy(self, half, source, slot, step):
        return remote(
            source,
            self.relay.at[half, slot],
            self.line_send.at[half, slot],
            self.line_arrive.at[half, slot],
            self.spot.line(step),
        )

    def line_wait(self, half, slot):
        landed(
            self.relay.at[half, slot], self.dummy, self.line_arrive.at[half, slot], self.spot.here
        )

    def hand_on(self, half, slot, source):
        spot = self.spot
        section = (SEC - 1) * half
        for other, device in spot.targets(half, slot):
            copy = remote(
                source,
                self.sections[section].at[half * REP + spot.rep],
                self.send.at[half, other],
                self.arrive.at[section, half, spot.rep],
                device,
            )
            if half == 0:
                same = jnp.logical_and(other == spot.rep, device[1] == spot.blk)

                @pl.when(same)
                def _(source=source):
                    self.sections[0][spot.rep] = source[...]

                @pl.when(jnp.logical_not(same))
                def _(copy=copy):
                    copy.start()
            else:
                copy.start()

    def start_low(self):
        self.low = [
            self.line_copy(0, self.shard.at[0], 1, 2),
            self.line_copy(0, self.shard.at[0], 3, -2),
        ]
        for copy in self.low:
            copy.start()
        self.hand_on(0, 0, self.shard.at[0])

    def start_high(self):
        core = self.spot.core
        self.high = [
            self.line_copy(1, self.shard.at[1], 0, 1 + core),
            self.line_copy(1, self.shard.at[1], 3 - core, -1 - core),
        ]
        for copy in self.high:
            copy.start()

        @pl.when(core == 1)
        def _():
            self.hand_on(1, 3, self.shard.at[1])

    def pass_on(self):
        core, relay = self.spot.core, self.relay
        self.line_wait(0, 1)
        self.onward = self.line_copy(0, relay.at[0, 1], 2, 2)
        self.onward.start()
        self.hand_on(0, 1, relay.at[0, 1])
        self.line_wait(0, 3)
        self.hand_on(0, 3, relay.at[0, 3])
        self.line_wait(1, 3 - core)
        self.back = self.line_copy(1, relay.at[1, 3 - core], 2 - core, -2)
        self.back.start()
        self.line_wait(1, 0)
        self.forth = self.line_copy(1, relay.at[1, 0], 1, 2)

        @pl.when(core == 0)
        def _():
            self.forth.start()

        self.hand_on(1, 0, relay.at[1, 0])
        self.hand_on(1, 3 - core, relay.at[1, 3 - core])
        self.line_wait(0, 2)
        self.hand_on(0, 2, relay.at[0, 2])
        self.line_wait(1, 2 - core)
        self.hand_on(1, 2 - core, relay.at[1, 2 - core])

        @pl.when(core == 0)
        def _():
            self.line_wait(1, 1)
            self.hand_on(1, 1, relay.at[1, 1])

    def arrived(self, section, half, piece):
        landed(
            self.sections[section].at[half * REP + piece],
            self.dummy,
            self.arrive.at[section, half, piece],
            self.spot.here,
        )

    def chains(self):
        spot = self.spot
        for section in range(SEC - 1):
            other_section = SEC - 1 - section

            def hop(step, carry, section=section, other_section=other_section):
                piece = lax.rem(spot.rep + REP - step, REP)
                if section == 0:
                    @pl.when(jnp.logical_not(spot.local(piece)))
                    def _():
                        self.arrived(section, 0, piece)
                else:
                    self.arrived(section, 0, piece)
                remote(
                    self.sections[section].at[piece],
                    self.sections[section + 1].at[piece],
                    self.chain_send.at[0, section, piece],
                    self.arrive.at[section + 1, 0, piece],
                    spot.up,
                ).start()
                self.arrived(other_section, 1, piece)
                remote(
                    self.sections[other_section].at[REP + piece],
                    self.sections[other_section - 1].at[REP + piece],
                    self.chain_send.at[1, section, piece],
                    self.arrive.at[other_section - 1, 1, piece],
                    spot.down,
                ).start()
                return carry

            lax.fori_loop(0, REP, hop, 0)

    def last_arrivals(self):
        def finish(piece, carry):
            self.arrived(SEC - 1, 0, piece)
            self.arrived(0, 1, piece)
            return carry

        lax.fori_loop(0, REP, finish, 0)

    def drain(self):
        spot = self.spot
        sample = self.shard.at[0]

        def sent(semaphore):
            remote(sample, sample, semaphore, self.arrive.at[0, 0, 0], spot.here).wait_send()

        def body(piece, carry):
            for direction in range(2):
                for section in range(SEC - 1):
                    sent(self.chain_send.at[direction, section, piece])

            @pl.when(jnp.logical_not(spot.local(piece)))
            def _():
                sent(self.send.at[0, piece])

            sent(self.send.at[1, piece])
            return carry

        lax.fori_loop(0, REP, body, 0)
        for copy in (*self.low, *self.high, self.back, self.onward):
            copy.wait_send()

        @pl.when(spot.core == 0)
        def _():
            self.forth.wait_send()


def spread_scratch(height):
    dma = pltpu.SemaphoreType.DMA
    return [
        *[pltpu.VMEM((2 * REP, height, LANES), BF16)] * SEC,
        pltpu.VMEM((2, 4, height, LANES), BF16),
        dma((2, 4)),
        dma((2, 4)),
        dma((2, REP)),
        dma((2, SEC - 1, REP)),
        dma((SEC, 2, REP)),
    ]


class Scatter:
    def __init__(self, spot, pieces, landing, send, arrive):
        self.spot, self.pieces, self.landing = spot, pieces, landing
        self.send, self.arrive = send, arrive

    def copy(self, half, other, lands):
        return remote(
            self.pieces.at[half, other],
            self.landing.at[half, lands],
            self.send.at[half, other],
            self.arrive.at[half, lands],
            (other, self.spot.blk),
        )

    def put(self, half, make):
        rep = self.spot.rep

        def one(step, carry):
            other = lax.rem(rep + 1 + step, REP)
            self.pieces[half, other] = make(other)
            self.copy(half, other, rep).start()
            return carry

        lax.fori_loop(0, REP - 1, one, 0)
        self.landing[half, rep] = make(rep)

    def total(self, half):
        rep = self.spot.rep

        def one(step, carry):
            other = lax.rem(rep + 1 + step, REP)
            self.copy(half, other, other).wait_recv()
            return carry

        lax.fori_loop(0, REP - 1, one, 0)
        total = self.landing[half, 0].astype(F32)
        for index in range(1, REP):
            total = total + self.landing[half, index].astype(F32)
        return total

    def drain(self):
        def one(step, carry):
            other = lax.rem(self.spot.rep + 1 + step, REP)
            for half in range(self.pieces.shape[0]):
                self.copy(half, other, other).wait_send()
            return carry

        lax.fori_loop(0, REP - 1, one, 0)


def scatter_scratch(halves, height, width, dtype):
    dma = pltpu.SemaphoreType.DMA
    return [
        pltpu.VMEM((halves, REP, height, width), dtype),
        pltpu.VMEM((halves, REP, height, width), dtype),
        dma((halves, REP)),
        dma((halves, REP)),
    ]


def pack(values):
    half = TILE // 2
    lanes = lax.broadcasted_iota(jnp.int32, (half, LANES), 1)
    rest = jnp.where(
        lanes < half,
        values[:half, LANES:],
        pltpu.roll(values[half:, LANES:], half, 1),
    )
    return jnp.concatenate([values[:, :LANES], rest], axis=0).astype(BF16)


def unpack(packed):
    half = TILE // 2
    rest = packed[TILE:]
    turned = jnp.concatenate([rest[:, half:], rest[:, :half]], axis=1)
    return jnp.concatenate(
        [packed[:TILE], jnp.concatenate([rest, turned], axis=0)], axis=1
    )


def keep_factor(ids):
    columns = lax.broadcasted_iota(jnp.int32, (1, WIDE), 1)
    mixed = ids * 73244475 + columns * 19349663 + 12345
    mixed = mixed ^ jnp.right_shift(mixed, 15)
    mixed = mixed * 40503
    mixed = mixed ^ jnp.right_shift(mixed, 13)
    return jnp.bitwise_and(mixed, 3) != 0


def column_of(row):
    lanes = lax.broadcasted_iota(jnp.int32, (TILE, LANES), 1)
    rows = lax.broadcasted_iota(jnp.int32, (TILE, LANES), 0)
    spread_out = jnp.broadcast_to(row.astype(F32), (TILE, LANES))
    return jnp.sum(jnp.where(lanes == rows, spread_out, 0.0), axis=1, keepdims=True)


def step_kernel(
    scale,
    source_table,
    previous_table,
    last_table,
    row_table,
    back_previous_table,
    back_last_table,
    x,
    ids,
    labels,
    mask,
    tiles,
    weight_in,
    weight_out,
    bias,
    logits_out,
    grad_in,
    grad_out,
    wide_out,
    wide_bias,
    running,
    coded,
    shard,
    kept,
    dense,
    back_rows,
    in_sum,
    out_sum,
    slopes,
    slope_send,
    slope_arrive,
    corner,
    corner_in,
    depth_in,
    full_corner,
    full,
    b_send,
    b_arrive,
    c_send,
    c_arrive,
    d_send,
    d_arrive,
    e_send,
    e_arrive,
    *rest,
):
    rest = list(rest)

    def take(count):
        taken = rest[:count]
        del rest[:count]
        return taken

    spot = Spot()
    rep, blk = spot.rep, spot.blk
    first_sections = take(SEC)
    first_spread = Spread(spot, coded, first_sections, *take(6))
    second_sections = take(SEC)
    second_spread = Spread(spot, shard, second_sections, *take(6))
    first_scatter = Scatter(spot, *take(4))
    second_scatter = Scatter(spot, *take(4))
    term_scatter = Scatter(spot, *take(4))
    waits = greet_everyone(spot)
    running[NONE] = jnp.zeros((TILE, WIDE), F32)
    wide_out[...] = jnp.zeros_like(wide_out)
    wide_out[:CLASSES, :] = weight_out[...]
    wide_bias[...] = jnp.zeros_like(wide_bias)
    wide_bias[:, :CLASSES] = bias[...]
    code_rows = lax.broadcasted_iota(jnp.int32, (CODED - TILE, LANES), 0)
    for half in range(2):
        coded[half, :TILE] = x[half]
        number = ids[half : half + 1, :]
        code = jnp.zeros((CODED - TILE, LANES), F32)
        for byte in range(3):
            value = jnp.bitwise_and(jnp.right_shift(number, 8 * byte), 255).astype(F32)
            code = jnp.where(code_rows == byte, jnp.broadcast_to(value, code.shape), code)
        coded[half, TILE:] = code.astype(BF16)
    pl.semaphore_wait(pltpu.get_barrier_semaphore(), waits)

    def products(section, width, source_of):
        place = FORWARD_ORDER.index(section)

        def some(group, carry):
            made = []
            for inner in range(4):
                slot = group * 4 + inner
                made.append(
                    jnp.dot(
                        tiles[section * SLOTS + slot],
                        source_of(source_table[section, slot]),
                        preferred_element_type=F32,
                    )
                )
            for inner in range(4):
                slot = group * 4 + inner
                running[place * SLOTS + slot, :, :width] = (
                    made[inner] + running[previous_table[section, slot], :, :width]
                )
            return carry

        lax.fori_loop(0, SLOTS // 4, some, 0)

    def first_products(section):
        products(section, LANES, lambda index: first_sections[section][index, :TILE])

    def second_products(section):
        products(section, WIDE, lambda index: dense[section * SLOTS + index])

    def first_sum(half):
        return lambda other: running[last_table[2 * other + half], :, :LANES]

    def second_sum(half):
        def one(other):
            part = running[last_table[2 * other + half]].astype(BF16)
            return pack(
                lax.dot_general(
                    part, wide_out[...], (((1,), (1,)), ((), ())), preferred_element_type=F32
                )
            )

        return one

    def find_kept(section):
        lanes = lax.broadcasted_iota(jnp.int32, (TILE, LANES), 1)
        rows = lax.broadcasted_iota(jnp.int32, (TILE, LANES), 0)
        unit = jnp.where(lanes == rows, 1.0, 0.0).astype(BF16)

        def one(index, carry):
            code = lax.dot_general(
                unit,
                first_sections[section][index, TILE:],
                (((1,), (1,)), ((), ())),
                preferred_element_type=F32,
            )
            number = code[:, 0:1] + 256.0 * code[:, 1:2] + 65536.0 * code[:, 2:3]
            kept[section * SLOTS + index] = jnp.where(
                keep_factor(number.astype(jnp.int32)), 1.0, 0.0
            ).astype(BF16)
            return carry

        lax.fori_loop(0, SLOTS, one, 0)

    def activate(section):
        def one(index, carry):
            pre_act = jnp.dot(
                second_sections[section][index], weight_in[...], preferred_element_type=F32
            )
            active = jnp.maximum(pre_act, 0.0) * F32(KEEP)
            flag = kept[section * SLOTS + index].astype(F32)
            dense[section * SLOTS + index] = jnp.where(flag > 0.0, active, 0.0).astype(BF16)
            return carry

        lax.fori_loop(0, SLOTS, one, 0)

    first_spread.start_low()
    first_spread.start_high()
    first_spread.pass_on()
    first_spread.chains()
    first_products(1)
    first_products(2)
    first_spread.last_arrivals()
    first_products(0)
    first_products(3)
    first_scatter.put(0, first_sum(0))
    first_scatter.put(1, first_sum(1))
    for section in range(SEC):
        find_kept(section)
    shard[0] = first_scatter.total(0).astype(BF16)
    second_spread.start_low()
    shard[1] = first_scatter.total(1).astype(BF16)
    second_spread.start_high()
    second_spread.pass_on()
    second_spread.chains()
    activate(1)
    activate(2)
    second_products(1)
    second_products(2)
    second_spread.last_arrivals()
    activate(0)
    activate(3)
    second_products(0)
    second_products(3)
    second_scatter.put(0, second_sum(0))
    second_scatter.put(1, second_sum(1))
    first_spread.drain()
    second_spread.drain()
    first_scatter.drain()

    def slope_copy(half, other, lands):
        return remote(
            slopes.at[2 * rep + half],
            slopes.at[2 * lands + half],
            slope_send.at[half, other],
            slope_arrive.at[half, lands],
            (other, blk),
        )

    def classes(half):
        logits = unpack(second_scatter.total(half)) + wide_bias[...]
        logits_out[half * TILE : (half + 1) * TILE, :] = logits[:, :CLASSES]
        columns = lax.broadcasted_iota(jnp.int32, logits.shape, 1)
        real = columns < CLASSES
        top = jnp.max(jnp.where(real, logits, -jnp.inf), axis=1, keepdims=True)
        powers = jnp.where(real, jnp.exp(jnp.where(real, logits - top, 0.0)), 0.0)
        likelihood = powers / jnp.sum(powers, axis=1, keepdims=True)
        label = column_of(labels[half : half + 1, :]).astype(jnp.int32)
        onehot = jnp.where(columns == label, 1.0, 0.0)
        chosen = column_of(mask[half : half + 1, :]) * scale
        slopes[2 * rep + half] = pack((likelihood - onehot) * chosen)
        for step in range(1, REP):
            slope_copy(half, lax.rem(rep + step, REP), rep).start()

    classes(0)
    classes(1)
    second_scatter.drain()

    def slope_waits(step, carry):
        other = lax.rem(rep + step, REP)
        for half in range(2):
            copy = remote(
                slopes.at[2 * rep + half],
                slopes.at[2 * other + half],
                slope_send.at[half, other],
                slope_arrive.at[half, other],
                (other, blk),
            )
            copy.wait_recv()
            copy.wait_send()
        return carry

    lax.fori_loop(1, REP, slope_waits, 0)

    def back_products(section):
        def some(group, carry):
            made = []
            for inner in range(4):
                slot = group * 4 + inner
                made.append(
                    lax.dot_general(
                        tiles[section * SLOTS + slot],
                        unpack(slopes[row_table[section, slot]]),
                        (((0,), (0,)), ((), ())),
                        preferred_element_type=F32,
                    )
                )
            for inner in range(4):
                slot = group * 4 + inner
                running[section * SLOTS + slot] = (
                    made[inner] + running[back_previous_table[section, slot]]
                )
            return carry

        lax.fori_loop(0, SLOTS // 4, some, 0)

        def gather(piece, carry):
            for half in range(2):
                back_rows[section * SLOTS + half * REP + piece] = running[
                    back_last_table[section, 2 * piece + half]
                ].astype(BF16)
            return carry

        lax.fori_loop(0, REP, gather, 0)

    in_sum[...] = jnp.zeros_like(in_sum)
    out_sum[...] = jnp.zeros_like(out_sum)

    def terms(section):
        for half in range(2):
            inside = pl.ds(section * SLOTS + half * REP, REP)
            back = back_rows[inside].reshape(REP * TILE, WIDE)
            active = dense[inside].reshape(REP * TILE, WIDE)
            z_rows = second_sections[section][half * REP : (half + 1) * REP].reshape(
                REP * TILE, LANES
            )
            out_sum[...] += lax.dot_general(
                back, active, (((0,), (0,)), ((), ())), preferred_element_type=F32
            )
            hidden_rows = jnp.dot(back, wide_out[...], preferred_element_type=F32)
            pre_slope = jnp.where(
                active.astype(F32) > 0.0, hidden_rows * F32(KEEP), 0.0
            ).astype(BF16)
            in_sum[...] += lax.dot_general(
                z_rows, pre_slope, (((0,), (0,)), ((), ())), preferred_element_type=F32
            )

    for section in range(SEC):
        back_products(section)
        terms(section)
    in_rows = in_sum.shape[0]
    chunk = (in_rows + WIDE) // REP
    joined = jnp.concatenate([in_sum[...], out_sum[...]], axis=0).astype(BF16)
    for index in range(REP):
        term_scatter.pieces[0, index] = joined[index * chunk : (index + 1) * chunk]
    for step in range(1, REP):
        term_scatter.copy(0, lax.rem(rep + step, REP), rep).start()
    term_scatter.landing[0, rep] = term_scatter.pieces[0, rep]
    total = term_scatter.total(0)
    term_scatter.drain()
    for index in range(12):
        corner[index // 3, index % 3] = total[
            (index // 2) * 8 : (index // 2) * 8 + 8, (index % 2) * LANES : (index % 2 + 1) * LANES
        ]
    me = spot.corner
    for step in range(1, 4):
        other = lax.rem(me + step, 4)
        remote(
            corner.at[other],
            corner_in.at[me],
            b_send.at[other],
            b_arrive.at[me],
            spot.corner_device(other),
        ).start()
    for step in range(1, 4):
        other = lax.rem(me + step, 4)
        copy = remote(
            corner.at[other],
            corner_in.at[other],
            b_send.at[other],
            b_arrive.at[other],
            spot.corner_device(other),
        )
        copy.wait_recv()
        copy.wait_send()
    corner_in[me] = corner[me]
    depth = spot.depth
    depth_in[depth] = corner_in[0] + corner_in[1] + corner_in[2] + corner_in[3]
    for step in range(1, DEPTH):
        remote(
            depth_in.at[depth],
            depth_in.at[depth],
            c_send.at[step],
            c_arrive.at[depth],
            spot.line(step),
        ).start()
    for step in range(1, DEPTH):
        other = lax.rem(depth + step, DEPTH)
        copy = remote(
            depth_in.at[depth],
            depth_in.at[other],
            c_send.at[step],
            c_arrive.at[other],
            spot.line(step),
        )
        copy.wait_recv()
        copy.wait_send()
    total = depth_in[0]
    for index in range(1, DEPTH):
        total = total + depth_in[index]
    full_corner[me] = total
    for step in range(1, 4):
        other = lax.rem(me + step, 4)
        remote(
            full_corner.at[me],
            full_corner.at[me],
            d_send.at[other],
            d_arrive.at[me],
            spot.corner_device(other),
        ).start()
    for step in range(1, 4):
        other = lax.rem(me + step, 4)
        copy = remote(
            full_corner.at[me],
            full_corner.at[other],
            d_send.at[other],
            d_arrive.at[other],
            spot.corner_device(other),
        )
        copy.wait_recv()
        copy.wait_send()
    full[rep] = jnp.concatenate(
        [
            jnp.concatenate(
                [
                    full_corner[(2 * row) // 3, (2 * row) % 3],
                    full_corner[(2 * row + 1) // 3, (2 * row + 1) % 3],
                ],
                axis=1,
            )
            for row in range(6)
        ],
        axis=0,
    ).astype(BF16)
    for step in range(1, REP):
        other = lax.rem(rep + step, REP)
        remote(full.at[rep], full.at[rep], e_send.at[other], e_arrive.at[rep], (other, blk)).start()
    for step in range(1, REP):
        other = lax.rem(rep + step, REP)
        copy = remote(
            full.at[rep], full.at[other], e_send.at[other], e_arrive.at[other], (other, blk)
        )
        copy.wait_recv()
        copy.wait_send()
    joined = jnp.concatenate([full[index] for index in range(REP)], axis=0).astype(F32)
    grad_in[...] = joined[:in_rows]
    grad_out[...] = joined[in_rows : in_rows + CLASSES]


def index_tables(place, count):
    section = lax.broadcasted_iota(jnp.int32, (SEC, SLOTS), 0)
    slot = lax.broadcasted_iota(jnp.int32, (SEC, SLOTS), 1)
    live = slot < count[:, None]
    row, column = place // SLOTS, place % SLOTS
    turn = jnp.where(section == SEC - 1, SEC - 1, (section + 2) % (SEC - 1))
    entry = turn * SLOTS + slot
    back_entry = section * SLOTS + slot

    def found(match, entries, axes):
        latest = jnp.max(jnp.where(match, entries, -1), axis=axes)
        return jnp.where(latest < 0, NONE, latest)

    entries = entry[None, None]
    same_row = (row[None, None] == row[:, :, None, None]) & live[None, None]
    previous = found(same_row & (entries < entry[:, :, None, None]), entries, (2, 3))
    numbers = jnp.arange(SLOTS, dtype=jnp.int32)
    of_row = (row[None] == numbers[:, None, None]) & live[None]
    last = found(of_row, entry[None], (1, 2))
    back_entries = back_entry[:, None, :]
    same_column = (column[:, None, :] == column[:, :, None]) & live[:, None, :]
    back_previous = found(
        same_column & (back_entries < back_entry[:, :, None]), back_entries, 2
    )
    of_column = (column[:, None, :] == numbers[None, :, None]) & live[:, None, :]
    back_last = found(of_column, back_entries, 2)
    source = (column % 2) * REP + column // 2
    return source, previous, last, row, back_previous, back_last


def on_device(
    features,
    node_ids,
    labels,
    train_mask,
    tile_values,
    tile_place,
    tile_count,
    weight_in,
    weight_out,
    class_bias,
):
    width = features.shape[-1]
    own_rows = features.shape[1]
    scale = 1.0 / math.sqrt(own_rows * REP * BLK)
    shape = jax.ShapeDtypeStruct
    dma = pltpu.SemaphoreType.DMA
    vmem = pltpu.VMEM
    chunk = (width + WIDE) // REP
    tables = index_tables(tile_place[0, 0], tile_count[0, 0])
    logits, grad_in, grad_out = pl.pallas_call(
        lambda *refs: step_kernel(scale, *refs),
        out_shape=(
            shape((own_rows, CLASSES), F32),
            shape((width, WIDE), F32),
            shape((CLASSES, WIDE), F32),
        ),
        in_specs=[pl.BlockSpec(memory_space=pltpu.SMEM)] * 6 + [whole()] * 8,
        out_specs=[whole()] * 3,
        scratch_shapes=[
            vmem((WIDE, WIDE), BF16),
            vmem((1, WIDE), F32),
            vmem((NONE + 1, TILE, WIDE), F32),
            vmem((2, CODED, LANES), BF16),
            vmem((2, TILE, LANES), BF16),
            vmem((NONE, TILE, WIDE), BF16),
            vmem((NONE, TILE, WIDE), BF16),
            vmem((NONE, TILE, WIDE), BF16),
            vmem((width, WIDE), F32),
            vmem((WIDE, WIDE), F32),
            vmem((2 * REP, PACKED, LANES), BF16),
            dma((2, REP)),
            dma((2, REP)),
            vmem((4, 3, 8, LANES), F32),
            vmem((4, 3, 8, LANES), F32),
            vmem((DEPTH, 3, 8, LANES), F32),
            vmem((4, 3, 8, LANES), F32),
            vmem((REP, chunk, WIDE), BF16),
            dma((4,)),
            dma((4,)),
            dma((DEPTH,)),
            dma((DEPTH,)),
            dma((4,)),
            dma((4,)),
            dma((REP,)),
            dma((REP,)),
            *spread_scratch(CODED),
            *spread_scratch(TILE),
            *scatter_scratch(2, TILE, LANES, F32),
            *scatter_scratch(2, PACKED, LANES, BF16),
            *scatter_scratch(1, chunk, WIDE, BF16),
        ],
        compiler_params=pltpu.CompilerParams(
            collective_id=0, has_side_effects=True, vmem_limit_bytes=VMEM_LIMIT
        ),
        name="training_step",
    )(
        *tables,
        features.reshape(2, TILE, width),
        node_ids.reshape(2, TILE),
        labels.reshape(2, TILE),
        train_mask.reshape(2, TILE),
        tile_values.reshape(NONE, TILE, TILE),
        weight_in,
        weight_out.T,
        class_bias.reshape(1, CLASSES),
    )
    return (logits[None], grad_in, grad_out.T)


def solution(mesh):
    placed = (
        P("blk", "rep", None),
        P("blk", "rep"),
        P("blk", "rep"),
        P("blk", "rep"),
        P("blk", "rep", None, None, None, None),
        P("blk", "rep", None, None),
        P("blk", "rep", None),
        P(),
        P(),
        P(),
    )
    return jax.shard_map(
        on_device,
        mesh=mesh,
        in_specs=placed,
        out_specs=(P("blk", "rep", None), P(), P()),
        check_vma=False,
    )
```

```python
import math

import jax
import jax.numpy as jnp
from jax import lax
from jax.experimental import pallas as pl
from jax.experimental.pallas import tpu as pltpu
from jax.sharding import PartitionSpec as P

MESH = pl.DeviceIdType.MESH
F32 = jnp.float32
BF16 = jnp.bfloat16
REP = 8
BLK = 32
SEC = 4
TILE = 128
SLOTS = 16
WIDE = 256
CLASSES = 172
LANES = 128
PACKED = 192
DEPTH = 8
NONE = SEC * SLOTS
FORWARD_ORDER = (1, 2, 0, 3)
CODED = 144
KEEP = 4.0 / 3.0
SOURCE, PREVIOUS, ROW, BACK_PREVIOUS, BACK_LAST, LAST = 0, 4, 8, 12, 16, 20
VMEM_LIMIT = 60 << 20


def whole():
    return pl.BlockSpec(memory_space=pltpu.VMEM)


def remote(source, target, send, arrive, device):
    return pltpu.make_async_remote_copy(
        src_ref=source,
        dst_ref=target,
        send_sem=send,
        recv_sem=arrive,
        device_id=device,
        device_id_type=MESH,
    )


def landed(target, send, arrive, device):
    remote(target, target, send, arrive, device).wait_recv()


def greet(device):
    pl.semaphore_signal(
        pltpu.get_barrier_semaphore(), inc=1, device_id=device, device_id_type=MESH
    )


def blk_of(part, depth, core):
    return (part * (BLK // 4) + depth) * 2 + core


class Spot:
    def __init__(self):
        self.rep = lax.axis_index("rep")
        self.blk = lax.axis_index("blk")
        self.core = lax.rem(self.blk, 2)
        self.depth = lax.rem(self.blk // 2, DEPTH)
        self.part = self.blk // 16
        self.here = (self.rep, self.blk)
        self.up = (self.rep, lax.rem(self.blk + 1, BLK))
        self.down = (self.rep, lax.rem(self.blk + BLK - 1, BLK))
        low_block = lax.rem(self.blk - SEC * self.rep + BLK, BLK)
        high_block = lax.rem(self.blk - SEC * self.rep - (SEC - 1) + 2 * BLK, BLK)
        self.low_relay = (low_block // 16) * 16 + lax.rem(self.blk, 16)
        self.high_relay = blk_of(high_block // 16, self.depth, 1 - self.core)
        self.own_relay = self.low_relay == self.blk
        self.corner = self.part * 2 + self.core

    def line(self, step):
        return (self.rep, blk_of(self.part, lax.rem(self.depth + step + DEPTH, DEPTH), self.core))

    def corner_device(self, index):
        return (self.rep, blk_of(index // 2, self.depth, lax.rem(index, 2)))

    def local(self, piece):
        return jnp.logical_and(self.own_relay, piece == self.rep)

    def targets(self, half, slot):
        offset = 2 * slot + half * (1 + self.core)
        source = blk_of(self.part, lax.rem(self.depth - offset + 2 * DEPTH, DEPTH), self.core)
        for other in (slot, slot + 4):
            yield other, (other, lax.rem(source + (SEC - 1) * half + SEC * other, BLK))


def greet_everyone(spot):
    for step in range(1, REP):
        greet((lax.rem(spot.rep + step, REP), spot.blk))
    for step in range(1, DEPTH):
        greet(spot.line(step))
    for step in range(1, 4):
        greet(spot.corner_device(lax.rem(spot.corner + step, 4)))
    for other in range(REP):
        @pl.when(jnp.logical_not(spot.local(other)))
        def _(other=other):
            greet((other, spot.low_relay))

        greet((other, spot.high_relay))
    greet(spot.up)
    greet(spot.down)
    count = (REP - 1) + (DEPTH - 1) + 3 + 2 * REP + 2
    return count - jnp.where(spot.own_relay, 1, 0)


class Spread:
    def __init__(self, spot, shard, sections, relay, line_send, line_arrive, send, chain_send, arrive):
        self.spot, self.shard, self.sections, self.relay = spot, shard, sections, relay
        self.line_send, self.line_arrive, self.send = line_send, line_arrive, send
        self.chain_send, self.arrive = chain_send, arrive
        self.dummy = chain_send.at[0, 0, 0]

    def line_copy(self, half, source, slot, step):
        return remote(
            source,
            self.relay.at[half, slot],
            self.line_send.at[half, slot],
            self.line_arrive.at[half, slot],
            self.spot.line(step),
        )

    def line_wait(self, half, slot):
        landed(
            self.relay.at[half, slot], self.dummy, self.line_arrive.at[half, slot], self.spot.here
        )

    def hand_on(self, half, slot, source):
        spot = self.spot
        section = (SEC - 1) * half
        for other, device in spot.targets(half, slot):
            copy = remote(
                source,
                self.sections[section].at[half * REP + spot.rep],
                self.send.at[half, other],
                self.arrive.at[section, half, spot.rep],
                device,
            )
            if half == 0:
                same = jnp.logical_and(other == spot.rep, device[1] == spot.blk)

                @pl.when(same)
                def _(source=source):
                    self.sections[0][spot.rep] = source[...]

                @pl.when(jnp.logical_not(same))
                def _(copy=copy):
                    copy.start()
            else:
                copy.start()

    def start_low(self):
        self.low = [
            self.line_copy(0, self.shard.at[0], 1, 2),
            self.line_copy(0, self.shard.at[0], 3, -2),
        ]
        for copy in self.low:
            copy.start()
        self.hand_on(0, 0, self.shard.at[0])

    def start_high(self):
        core = self.spot.core
        self.high = [
            self.line_copy(1, self.shard.at[1], 0, 1 + core),
            self.line_copy(1, self.shard.at[1], 3 - core, -1 - core),
        ]
        for copy in self.high:
            copy.start()

        @pl.when(core == 1)
        def _():
            self.hand_on(1, 3, self.shard.at[1])

    def pass_on(self):
        core, relay = self.spot.core, self.relay
        self.line_wait(0, 1)
        self.onward = self.line_copy(0, relay.at[0, 1], 2, 2)
        self.onward.start()
        self.hand_on(0, 1, relay.at[0, 1])
        self.line_wait(0, 3)
        self.hand_on(0, 3, relay.at[0, 3])
        self.line_wait(1, 3 - core)
        self.back = self.line_copy(1, relay.at[1, 3 - core], 2 - core, -2)
        self.back.start()
        self.line_wait(1, 0)
        self.forth = self.line_copy(1, relay.at[1, 0], 1, 2)

        @pl.when(core == 0)
        def _():
            self.forth.start()

        self.hand_on(1, 0, relay.at[1, 0])
        self.hand_on(1, 3 - core, relay.at[1, 3 - core])
        self.line_wait(0, 2)
        self.hand_on(0, 2, relay.at[0, 2])
        self.line_wait(1, 2 - core)
        self.hand_on(1, 2 - core, relay.at[1, 2 - core])

        @pl.when(core == 0)
        def _():
            self.line_wait(1, 1)
            self.hand_on(1, 1, relay.at[1, 1])

    def arrived(self, section, half, piece):
        landed(
            self.sections[section].at[half * REP + piece],
            self.dummy,
            self.arrive.at[section, half, piece],
            self.spot.here,
        )

    def chains(self):
        spot = self.spot
        for section in range(SEC - 1):
            other_section = SEC - 1 - section

            def hop(step, carry, section=section, other_section=other_section):
                piece = lax.rem(spot.rep + REP - step, REP)
                if section == 0:
                    @pl.when(jnp.logical_not(spot.local(piece)))
                    def _():
                        self.arrived(section, 0, piece)
                else:
                    self.arrived(section, 0, piece)
                remote(
                    self.sections[section].at[piece],
                    self.sections[section + 1].at[piece],
                    self.chain_send.at[0, section, piece],
                    self.arrive.at[section + 1, 0, piece],
                    spot.up,
                ).start()
                self.arrived(other_section, 1, piece)
                remote(
                    self.sections[other_section].at[REP + piece],
                    self.sections[other_section - 1].at[REP + piece],
                    self.chain_send.at[1, section, piece],
                    self.arrive.at[other_section - 1, 1, piece],
                    spot.down,
                ).start()
                return carry

            lax.fori_loop(0, REP, hop, 0)

    def last_arrivals(self):
        def finish(piece, carry):
            self.arrived(SEC - 1, 0, piece)
            self.arrived(0, 1, piece)
            return carry

        lax.fori_loop(0, REP, finish, 0)

    def drain(self):
        spot = self.spot
        sample = self.shard.at[0]

        def sent(semaphore):
            remote(sample, sample, semaphore, self.arrive.at[0, 0, 0], spot.here).wait_send()

        def body(piece, carry):
            for direction in range(2):
                for section in range(SEC - 1):
                    sent(self.chain_send.at[direction, section, piece])

            @pl.when(jnp.logical_not(spot.local(piece)))
            def _():
                sent(self.send.at[0, piece])

            sent(self.send.at[1, piece])
            return carry

        lax.fori_loop(0, REP, body, 0)
        for copy in (*self.low, *self.high, self.back, self.onward):
            copy.wait_send()

        @pl.when(spot.core == 0)
        def _():
            self.forth.wait_send()


def spread_scratch(height):
    dma = pltpu.SemaphoreType.DMA
    return [
        *[pltpu.VMEM((2 * REP, height, LANES), BF16)] * SEC,
        pltpu.VMEM((2, 4, height, LANES), BF16),
        dma((2, 4)),
        dma((2, 4)),
        dma((2, REP)),
        dma((2, SEC - 1, REP)),
        dma((SEC, 2, REP)),
    ]


class Scatter:
    def __init__(self, spot, pieces, landing, send, arrive):
        self.spot, self.pieces, self.landing = spot, pieces, landing
        self.send, self.arrive = send, arrive

    def copy(self, half, other, lands):
        return remote(
            self.pieces.at[half, other],
            self.landing.at[half, lands],
            self.send.at[half, other],
            self.arrive.at[half, lands],
            (other, self.spot.blk),
        )

    def put(self, half, make):
        rep = self.spot.rep

        def one(step, carry):
            other = lax.rem(rep + 1 + step, REP)
            self.pieces[half, other] = make(other)
            self.copy(half, other, rep).start()
            return carry

        lax.fori_loop(0, REP - 1, one, 0)
        self.landing[half, rep] = make(rep)

    def total(self, half):
        rep = self.spot.rep

        def one(step, carry):
            other = lax.rem(rep + 1 + step, REP)
            self.copy(half, other, other).wait_recv()
            return carry

        lax.fori_loop(0, REP - 1, one, 0)
        total = self.landing[half, 0].astype(F32)
        for index in range(1, REP):
            total = total + self.landing[half, index].astype(F32)
        return total

    def drain(self):
        def one(step, carry):
            other = lax.rem(self.spot.rep + 1 + step, REP)
            for half in range(self.pieces.shape[0]):
                self.copy(half, other, other).wait_send()
            return carry

        lax.fori_loop(0, REP - 1, one, 0)


def scatter_scratch(halves, height, width, dtype):
    dma = pltpu.SemaphoreType.DMA
    return [
        pltpu.VMEM((halves, REP, height, width), dtype),
        pltpu.VMEM((halves, REP, height, width), dtype),
        dma((halves, REP)),
        dma((halves, REP)),
    ]


def pack(values):
    half = TILE // 2
    lanes = lax.broadcasted_iota(jnp.int32, (half, LANES), 1)
    rest = jnp.where(
        lanes < half,
        values[:half, LANES:],
        pltpu.roll(values[half:, LANES:], half, 1),
    )
    return jnp.concatenate([values[:, :LANES], rest], axis=0).astype(BF16)


def unpack(packed):
    half = TILE // 2
    rest = packed[TILE:]
    turned = jnp.concatenate([rest[:, half:], rest[:, :half]], axis=1)
    return jnp.concatenate(
        [packed[:TILE], jnp.concatenate([rest, turned], axis=0)], axis=1
    )


def is_kept(ids):
    columns = lax.broadcasted_iota(jnp.int32, (1, WIDE), 1)
    mixed = (ids * 73244475 + 12345) + columns * 19349663
    mixed = jnp.bitwise_and(mixed ^ jnp.right_shift(mixed, 15), 32767) * (40503 % 32768)
    mixed = mixed ^ jnp.right_shift(mixed, 13)
    return jnp.bitwise_and(mixed, 3) != 0


def column_of(row):
    lanes = lax.broadcasted_iota(jnp.int32, (TILE, LANES), 1)
    rows = lax.broadcasted_iota(jnp.int32, (TILE, LANES), 0)
    spread_out = jnp.broadcast_to(row.astype(F32), (TILE, LANES))
    return jnp.sum(jnp.where(lanes == rows, spread_out, 0.0), axis=1, keepdims=True)


def step_kernel(
    scale,
    count,
    place,
    x_hbm,
    ids,
    labels,
    mask,
    tiles_hbm,
    weight_in_hbm,
    weight_out_hbm,
    bias,
    logits_out,
    full,
    x,
    tiles,
    weight_in,
    weight_out,
    input_sems,
    table_values,
    table,
    wide_out,
    wide_bias,
    running,
    coded,
    shard,
    kept,
    dense,
    back_rows,
    in_sum,
    out_sum,
    slopes,
    slope_send,
    slope_arrive,
    corner,
    corner_in,
    depth_in,
    full_corner,
    b_send,
    b_arrive,
    c_send,
    c_arrive,
    d_send,
    d_arrive,
    e_send,
    e_arrive,
    *rest,
):
    rest = list(rest)

    def take(count):
        taken = rest[:count]
        del rest[:count]
        return taken

    spot = Spot()
    rep, blk = spot.rep, spot.blk
    first_sections = take(SEC)
    first_spread = Spread(spot, coded, first_sections, *take(6))
    second_sections = take(SEC)
    second_spread = Spread(spot, shard, second_sections, *take(6))
    first_scatter = Scatter(spot, *take(4))
    second_scatter = Scatter(spot, *take(4))
    term_scatter = Scatter(spot, *take(4))
    waits = greet_everyone(spot)
    input_copies = [
        pltpu.make_async_copy(source, target, input_sems.at[index])
        for index, (source, target) in enumerate(
            (
                (x_hbm, x),
                (weight_out_hbm, weight_out),
                (weight_in_hbm, weight_in),
                (tiles_hbm, tiles),
            )
        )
    ]
    for copy in input_copies:
        copy.start()
    fill_tables(place, count, table_values)
    table_copy = pltpu.make_async_copy(table_values, table, input_sems.at[len(input_copies)])
    table_copy.start()
    running[NONE] = jnp.zeros((TILE, WIDE), F32)
    wide_out[...] = jnp.zeros_like(wide_out)
    wide_bias[...] = jnp.zeros_like(wide_bias)
    wide_bias[:, :CLASSES] = bias[...]
    input_copies[0].wait()
    input_copies[1].wait()
    wide_out[:CLASSES, :] = weight_out[...]
    code_rows = lax.broadcasted_iota(jnp.int32, (CODED - TILE, LANES), 0)
    for half in range(2):
        coded[half, :TILE] = x[half]
        number = ids[half : half + 1, :]
        code = jnp.zeros((CODED - TILE, LANES), F32)
        for byte in range(3):
            value = jnp.bitwise_and(jnp.right_shift(number, 8 * byte), 255).astype(F32)
            code = jnp.where(code_rows == byte, jnp.broadcast_to(value, code.shape), code)
        coded[half, TILE:] = code.astype(BF16)
    pl.semaphore_wait(pltpu.get_barrier_semaphore(), waits)

    def products(section, width, source_of):
        place = FORWARD_ORDER.index(section)

        def some(group, carry):
            made = []
            for inner in range(4):
                slot = group * 4 + inner
                made.append(
                    jnp.dot(
                        tiles[section * SLOTS + slot],
                        source_of(table[SOURCE + section, slot]),
                        preferred_element_type=F32,
                    )
                )
            for inner in range(4):
                slot = group * 4 + inner
                running[place * SLOTS + slot, :, :width] = (
                    made[inner] + running[table[PREVIOUS + section, slot], :, :width]
                )
            return carry

        lax.fori_loop(0, SLOTS // 4, some, 0)

    def first_products(section):
        products(section, LANES, lambda index: first_sections[section][index, :TILE])

    def second_products(section):
        products(section, WIDE, lambda index: dense[section * SLOTS + index])

    def first_sum(half):
        return lambda other: running[table[LAST, 2 * other + half], :, :LANES]

    def second_sum(half):
        def one(other):
            part = running[table[LAST, 2 * other + half]].astype(BF16)
            return pack(
                lax.dot_general(
                    part, wide_out[...], (((1,), (1,)), ((), ())), preferred_element_type=F32
                )
            )

        return one

    def find_kept(section):
        lanes = lax.broadcasted_iota(jnp.int32, (TILE, LANES), 1)
        rows = lax.broadcasted_iota(jnp.int32, (TILE, LANES), 0)
        unit = jnp.where(lanes == rows, 1.0, 0.0).astype(BF16)

        def one(index, carry):
            code = lax.dot_general(
                unit,
                first_sections[section][index, TILE:],
                (((1,), (1,)), ((), ())),
                preferred_element_type=F32,
            )
            number = code[:, 0:1] + 256.0 * code[:, 1:2] + 65536.0 * code[:, 2:3]
            kept[section * SLOTS + index] = jnp.where(
                is_kept(number.astype(jnp.int32)), 1.0, 0.0
            ).astype(BF16)
            return carry

        lax.fori_loop(0, SLOTS, one, 0, unroll=4)

    def activate(section):
        def one(index, carry):
            pre_act = jnp.dot(
                second_sections[section][index], weight_in[...], preferred_element_type=F32
            )
            active = jnp.maximum(pre_act, 0.0) * F32(KEEP)
            flag = kept[section * SLOTS + index].astype(F32)
            dense[section * SLOTS + index] = jnp.where(flag > 0.0, active, 0.0).astype(BF16)
            return carry

        lax.fori_loop(0, SLOTS, one, 0, unroll=4)

    first_spread.start_low()
    first_spread.start_high()
    first_spread.pass_on()
    first_spread.chains()
    input_copies[2].wait()
    input_copies[3].wait()
    table_copy.wait()
    first_products(1)
    first_products(2)
    first_spread.last_arrivals()
    first_products(0)
    first_products(3)
    first_scatter.put(0, first_sum(0))
    first_scatter.put(1, first_sum(1))
    for section in range(SEC):
        find_kept(section)
    shard[0] = first_scatter.total(0).astype(BF16)
    second_spread.start_low()
    shard[1] = first_scatter.total(1).astype(BF16)
    second_spread.start_high()
    second_spread.pass_on()
    second_spread.chains()
    activate(1)
    activate(2)
    second_products(1)
    second_products(2)
    second_spread.last_arrivals()
    activate(0)
    activate(3)
    second_products(0)
    second_products(3)
    second_scatter.put(0, second_sum(0))
    second_scatter.put(1, second_sum(1))
    first_spread.drain()
    second_spread.drain()
    first_scatter.drain()

    def slope_copy(half, other, lands):
        return remote(
            slopes.at[2 * rep + half],
            slopes.at[2 * lands + half],
            slope_send.at[half, other],
            slope_arrive.at[half, lands],
            (other, blk),
        )

    def classes(half):
        logits = unpack(second_scatter.total(half)) + wide_bias[...]
        columns = lax.broadcasted_iota(jnp.int32, logits.shape, 1)
        real = columns < CLASSES
        top = jnp.max(jnp.where(real, logits, -jnp.inf), axis=1, keepdims=True)
        powers = jnp.where(real, jnp.exp(jnp.where(real, logits - top, 0.0)), 0.0)
        likelihood = powers / jnp.sum(powers, axis=1, keepdims=True)
        label = column_of(labels[half : half + 1, :]).astype(jnp.int32)
        onehot = jnp.where(columns == label, 1.0, 0.0)
        chosen = column_of(mask[half : half + 1, :]) * scale
        slopes[2 * rep + half] = pack((likelihood - onehot) * chosen)
        for step in range(1, REP):
            slope_copy(half, lax.rem(rep + step, REP), rep).start()
        return logits

    low_logits = classes(0)
    high_logits = classes(1)
    logits_out[:, :TILE] = low_logits.T[:CLASSES]
    logits_out[:, TILE:] = high_logits.T[:CLASSES]
    second_scatter.drain()

    def slope_waits(step, carry):
        other = lax.rem(rep + step, REP)
        for half in range(2):
            copy = remote(
                slopes.at[2 * rep + half],
                slopes.at[2 * other + half],
                slope_send.at[half, other],
                slope_arrive.at[half, other],
                (other, blk),
            )
            copy.wait_recv()
            copy.wait_send()
        return carry

    lax.fori_loop(1, REP, slope_waits, 0)

    def back_products(section):
        def some(group, carry):
            made = []
            for inner in range(4):
                slot = group * 4 + inner
                made.append(
                    lax.dot_general(
                        tiles[section * SLOTS + slot],
                        unpack(slopes[table[ROW + section, slot]]),
                        (((0,), (0,)), ((), ())),
                        preferred_element_type=F32,
                    )
                )
            for inner in range(4):
                slot = group * 4 + inner
                running[section * SLOTS + slot] = (
                    made[inner] + running[table[BACK_PREVIOUS + section, slot]]
                )
            return carry

        lax.fori_loop(0, SLOTS // 4, some, 0)

        def gather(piece, carry):
            for half in range(2):
                back_rows[section * SLOTS + half * REP + piece] = running[
                    table[BACK_LAST + section, 2 * piece + half]
                ].astype(BF16)
            return carry

        lax.fori_loop(0, REP, gather, 0, unroll=2)

    in_sum[...] = jnp.zeros_like(in_sum)
    out_sum[...] = jnp.zeros_like(out_sum)

    def terms(section):
        for half in range(2):
            inside = pl.ds(section * SLOTS + half * REP, REP)
            back = back_rows[inside].reshape(REP * TILE, WIDE)
            active = dense[inside].reshape(REP * TILE, WIDE)
            z_rows = second_sections[section][half * REP : (half + 1) * REP].reshape(
                REP * TILE, LANES
            )
            out_sum[...] += lax.dot_general(
                back, active, (((0,), (0,)), ((), ())), preferred_element_type=F32
            )
            hidden_rows = jnp.dot(back, wide_out[...], preferred_element_type=F32)
            pre_slope = jnp.where(
                active.astype(F32) > 0.0, hidden_rows * F32(KEEP), 0.0
            ).astype(BF16)
            in_sum[...] += lax.dot_general(
                z_rows, pre_slope, (((0,), (0,)), ((), ())), preferred_element_type=F32
            )

    for section in range(SEC):
        back_products(section)
        terms(section)
    in_rows = in_sum.shape[0]
    chunk = (in_rows + WIDE) // REP
    joined = jnp.concatenate([in_sum[...], out_sum[...]], axis=0).astype(BF16)
    for index in range(REP):
        term_scatter.pieces[0, index] = joined[index * chunk : (index + 1) * chunk]
    for step in range(1, REP):
        term_scatter.copy(0, lax.rem(rep + step, REP), rep).start()
    term_scatter.landing[0, rep] = term_scatter.pieces[0, rep]
    total = term_scatter.total(0)
    term_scatter.drain()
    for index in range(12):
        corner[index // 3, index % 3] = total[
            (index // 2) * 8 : (index // 2) * 8 + 8, (index % 2) * LANES : (index % 2 + 1) * LANES
        ]
    me = spot.corner
    for step in range(1, 4):
        other = lax.rem(me + step, 4)
        remote(
            corner.at[other],
            corner_in.at[me],
            b_send.at[other],
            b_arrive.at[me],
            spot.corner_device(other),
        ).start()
    for step in range(1, 4):
        other = lax.rem(me + step, 4)
        copy = remote(
            corner.at[other],
            corner_in.at[other],
            b_send.at[other],
            b_arrive.at[other],
            spot.corner_device(other),
        )
        copy.wait_recv()
        copy.wait_send()
    corner_in[me] = corner[me]
    depth = spot.depth
    depth_in[depth] = corner_in[0] + corner_in[1] + corner_in[2] + corner_in[3]
    for step in range(1, DEPTH):
        remote(
            depth_in.at[depth],
            depth_in.at[depth],
            c_send.at[step],
            c_arrive.at[depth],
            spot.line(step),
        ).start()
    for step in range(1, DEPTH):
        other = lax.rem(depth + step, DEPTH)
        copy = remote(
            depth_in.at[depth],
            depth_in.at[other],
            c_send.at[step],
            c_arrive.at[other],
            spot.line(step),
        )
        copy.wait_recv()
        copy.wait_send()
    total = depth_in[0]
    for index in range(1, DEPTH):
        total = total + depth_in[index]
    full_corner[me] = total
    for step in range(1, 4):
        other = lax.rem(me + step, 4)
        remote(
            full_corner.at[me],
            full_corner.at[me],
            d_send.at[other],
            d_arrive.at[me],
            spot.corner_device(other),
        ).start()
    for step in range(1, 4):
        other = lax.rem(me + step, 4)
        copy = remote(
            full_corner.at[me],
            full_corner.at[other],
            d_send.at[other],
            d_arrive.at[other],
            spot.corner_device(other),
        )
        copy.wait_recv()
        copy.wait_send()
    full[rep] = jnp.concatenate(
        [
            jnp.concatenate(
                [
                    full_corner[(2 * row) // 3, (2 * row) % 3],
                    full_corner[(2 * row + 1) // 3, (2 * row + 1) % 3],
                ],
                axis=1,
            )
            for row in range(6)
        ],
        axis=0,
    ).astype(BF16)
    for step in range(1, REP):
        other = lax.rem(rep + step, REP)
        remote(full.at[rep], full.at[rep], e_send.at[other], e_arrive.at[rep], (other, blk)).start()
    for step in range(1, REP):
        other = lax.rem(rep + step, REP)
        copy = remote(
            full.at[rep], full.at[other], e_send.at[other], e_arrive.at[other], (other, blk)
        )
        copy.wait_recv()
        copy.wait_send()


def result_kernel(in_rows, logits, full, logits_out, grad_in, grad_out):
    logits_out[:, 0, :] = logits[...]
    joined = jnp.concatenate([full[index] for index in range(REP)], axis=0).astype(F32)
    grad_in[...] = joined[:in_rows]
    grad_out[...] = joined[in_rows : in_rows + CLASSES]


def fill_tables(place, count, out):
    slots = lax.broadcasted_iota(jnp.int32, (SLOTS, SLOTS), 1)
    others = lax.broadcasted_iota(jnp.int32, (SLOTS, SLOTS), 0)
    before = others < slots

    def turned(line):
        flat = jnp.broadcast_to(line.astype(F32), (SLOTS, SLOTS))
        column = jnp.sum(jnp.where(slots == others, flat, 0.0), axis=1, keepdims=True)
        return column.astype(jnp.int32)

    def top(match, entries):
        return jnp.max(jnp.where(match, entries, -1), axis=0, keepdims=True)

    def put(row, values):
        out[row : row + 1, :SLOTS] = values

    def settled(values):
        return jnp.where(values < 0, NONE, values)

    rows, columns, row_turned, column_turned, live = [], [], [], [], []
    for section in range(SEC):
        line = place[section : section + 1, :]
        rows.append(jnp.right_shift(line, 4))
        columns.append(jnp.bitwise_and(line, SLOTS - 1))
        row_turned.append(turned(rows[section]))
        column_turned.append(turned(columns[section]))
        live.append(others < count[section])
    numbers = slots[:1]
    last = jnp.full((1, SLOTS), -1, jnp.int32)
    for section in range(SEC):
        turn = FORWARD_ORDER.index(section)
        entries = others + turn * SLOTS
        latest = jnp.full((1, SLOTS), -1, jnp.int32)
        for earlier in FORWARD_ORDER[: turn + 1]:
            match = (row_turned[earlier] == rows[section]) & live[earlier]
            if earlier == section:
                match = match & before
            latest = jnp.maximum(
                latest, top(match, others + FORWARD_ORDER.index(earlier) * SLOTS)
            )
        last = jnp.maximum(last, top((row_turned[section] == numbers) & live[section], entries))
        put(SOURCE + section, jnp.bitwise_and(columns[section], 1) * REP + jnp.right_shift(columns[section], 1))
        put(PREVIOUS + section, settled(latest))
        put(ROW + section, rows[section])
        own = others + section * SLOTS
        match = (column_turned[section] == columns[section]) & live[section]
        put(BACK_PREVIOUS + section, settled(top(match & before, own)))
        match = (column_turned[section] == numbers) & live[section]
        put(BACK_LAST + section, settled(top(match, own)))
    put(LAST, settled(last))


def on_device(
    features,
    node_ids,
    labels,
    train_mask,
    tile_values,
    tile_place,
    tile_count,
    weight_in,
    weight_out,
    class_bias,
):
    width = features.shape[-1]
    own_rows = features.shape[1]
    scale = 1.0 / math.sqrt(own_rows * REP * BLK)
    shape = jax.ShapeDtypeStruct
    dma = pltpu.SemaphoreType.DMA
    vmem = pltpu.VMEM
    chunk = (width + WIDE) // REP
    anywhere = pl.BlockSpec(memory_space=pl.ANY)
    logits, full = pl.pallas_call(
        lambda *refs: step_kernel(scale, *refs),
        out_shape=(shape((CLASSES, own_rows), F32), shape((REP, chunk, WIDE), BF16)),
        in_specs=[
            pl.BlockSpec(memory_space=pltpu.SMEM),
            whole(),
            anywhere,
            whole(),
            whole(),
            whole(),
            anywhere,
            anywhere,
            anywhere,
            whole(),
        ],
        out_specs=[whole()] * 2,
        scratch_shapes=[
            vmem((2, TILE, width), BF16),
            vmem((NONE, TILE, TILE), BF16),
            vmem((width, WIDE), BF16),
            vmem((CLASSES, WIDE), BF16),
            dma((5,)),
            vmem((24, LANES), jnp.int32),
            pltpu.SMEM((24, LANES), jnp.int32),
            vmem((WIDE, WIDE), BF16),
            vmem((1, WIDE), F32),
            vmem((NONE + 1, TILE, WIDE), F32),
            vmem((2, CODED, LANES), BF16),
            vmem((2, TILE, LANES), BF16),
            vmem((NONE, TILE, WIDE), BF16),
            vmem((NONE, TILE, WIDE), BF16),
            vmem((NONE, TILE, WIDE), BF16),
            vmem((width, WIDE), F32),
            vmem((WIDE, WIDE), F32),
            vmem((2 * REP, PACKED, LANES), BF16),
            dma((2, REP)),
            dma((2, REP)),
            vmem((4, 3, 8, LANES), F32),
            vmem((4, 3, 8, LANES), F32),
            vmem((DEPTH, 3, 8, LANES), F32),
            vmem((4, 3, 8, LANES), F32),
            dma((4,)),
            dma((4,)),
            dma((DEPTH,)),
            dma((DEPTH,)),
            dma((4,)),
            dma((4,)),
            dma((REP,)),
            dma((REP,)),
            *spread_scratch(CODED),
            *spread_scratch(TILE),
            *scatter_scratch(2, TILE, LANES, F32),
            *scatter_scratch(2, PACKED, LANES, BF16),
            *scatter_scratch(1, chunk, WIDE, BF16),
        ],
        compiler_params=pltpu.CompilerParams(
            collective_id=0, has_side_effects=True, vmem_limit_bytes=VMEM_LIMIT
        ),
        name="training_step",
    )(
        tile_count.reshape(SEC),
        tile_place.reshape(SEC, SLOTS),
        features.reshape(2, TILE, width),
        node_ids.reshape(2, TILE),
        labels.reshape(2, TILE),
        train_mask.reshape(2, TILE),
        tile_values.reshape(NONE, TILE, TILE),
        weight_in,
        weight_out.T,
        class_bias.reshape(1, CLASSES),
    )
    logits, grad_in, grad_out = pl.pallas_call(
        lambda *refs: result_kernel(width, *refs),
        out_shape=(
            shape((CLASSES, 1, own_rows), F32),
            shape((width, WIDE), F32),
            shape((CLASSES, WIDE), F32),
        ),
        in_specs=[whole()] * 2,
        out_specs=[whole()] * 3,
        name="results",
    )(logits, full)
    return (logits.transpose(1, 2, 0), grad_in, grad_out.T)


def solution(mesh):
    placed = (
        P("blk", "rep", None),
        P("blk", "rep"),
        P("blk", "rep"),
        P("blk", "rep"),
        P("blk", "rep", None, None, None, None),
        P("blk", "rep", None, None),
        P("blk", "rep", None),
        P(),
        P(),
        P(),
    )
    return jax.shard_map(
        on_device,
        mesh=mesh,
        in_specs=placed,
        out_specs=(P("blk", "rep", None), P(), P()),
        check_vma=False,
    )
```

```python
import math

import jax
import jax.numpy as jnp
from jax import lax
from jax.experimental import pallas as pl
from jax.experimental.pallas import tpu as pltpu
from jax.sharding import PartitionSpec as P

MESH = pl.DeviceIdType.MESH
F32 = jnp.float32
BF16 = jnp.bfloat16
REP = 8
BLK = 32
SEC = 4
TILE = 128
SLOTS = 16
WIDE = 256
CLASSES = 172
LANES = 128
PACKED = 192
DEPTH = 8
NONE = SEC * SLOTS
FORWARD_ORDER = (1, 2, 0, 3)
CODED = 144
CREW = 32
KEEP = 4.0 / 3.0
CHUNK = 24
SOURCE, PREVIOUS, ROW, BACK_PREVIOUS, BACK_LAST, LAST = 0, 4, 8, 12, 16, 20
VMEM_LIMIT = 60 << 20


def whole():
    return pl.BlockSpec(memory_space=pltpu.VMEM)


def remote(source, target, send, arrive, device):
    return pltpu.make_async_remote_copy(
        src_ref=source,
        dst_ref=target,
        send_sem=send,
        recv_sem=arrive,
        device_id=device,
        device_id_type=MESH,
    )


def landed(target, send, arrive, device):
    remote(target, target, send, arrive, device).wait_recv()


def greet(device):
    pl.semaphore_signal(
        pltpu.get_barrier_semaphore(), inc=1, device_id=device, device_id_type=MESH
    )


def blk_of(part, depth, core):
    return (part * (BLK // 4) + depth) * 2 + core


class Spot:
    def __init__(self):
        self.rep = lax.axis_index("rep")
        self.blk = lax.axis_index("blk")
        self.core = lax.rem(self.blk, 2)
        self.depth = lax.rem(self.blk // 2, DEPTH)
        self.part = self.blk // 16
        self.here = (self.rep, self.blk)
        self.up = (self.rep, lax.rem(self.blk + 1, BLK))
        self.down = (self.rep, lax.rem(self.blk + BLK - 1, BLK))
        low_block = lax.rem(self.blk - SEC * self.rep + BLK, BLK)
        high_block = lax.rem(self.blk - SEC * self.rep - (SEC - 1) + 2 * BLK, BLK)
        self.low_relay = (low_block // 16) * 16 + lax.rem(self.blk, 16)
        self.high_relay = blk_of(high_block // 16, self.depth, 1 - self.core)
        self.own_relay = self.low_relay == self.blk
        self.member = self.rep * 4 + self.part * 2 + self.core

    def line(self, step):
        return (self.rep, blk_of(self.part, lax.rem(self.depth + step + DEPTH, DEPTH), self.core))

    def crew(self, index):
        corner = lax.rem(index, 4)
        return (index // 4, blk_of(corner // 2, self.depth, lax.rem(corner, 2)))

    def local(self, piece):
        return jnp.logical_and(self.own_relay, piece == self.rep)

    def targets(self, half, slot):
        offset = 2 * slot + half * (1 + self.core)
        source = blk_of(self.part, lax.rem(self.depth - offset + 2 * DEPTH, DEPTH), self.core)
        for other in (slot, slot + 4):
            yield other, (other, lax.rem(source + (SEC - 1) * half + SEC * other, BLK))


def greet_everyone(spot):
    for step in range(1, CREW):
        greet(spot.crew(lax.rem(spot.member + step, CREW)))
    for step in range(1, DEPTH):
        greet(spot.line(step))
    for other in range(REP):
        @pl.when(jnp.logical_not(spot.local(other)))
        def _(other=other):
            greet((other, spot.low_relay))

        greet((other, spot.high_relay))
    greet(spot.up)
    greet(spot.down)
    count = (CREW - 1) + (DEPTH - 1) + 2 * REP + 2
    return count - jnp.where(spot.own_relay, 1, 0)


class Spread:
    def __init__(self, spot, shard, sections, relay, line_send, line_arrive, send, chain_send, arrive):
        self.spot, self.shard, self.sections, self.relay = spot, shard, sections, relay
        self.line_send, self.line_arrive, self.send = line_send, line_arrive, send
        self.chain_send, self.arrive = chain_send, arrive
        self.dummy = chain_send.at[0, 0, 0]

    def line_copy(self, half, source, slot, step):
        return remote(
            source,
            self.relay.at[half, slot],
            self.line_send.at[half, slot],
            self.line_arrive.at[half, slot],
            self.spot.line(step),
        )

    def line_wait(self, half, slot):
        landed(
            self.relay.at[half, slot], self.dummy, self.line_arrive.at[half, slot], self.spot.here
        )

    def hand_on(self, half, slot, source):
        spot = self.spot
        section = (SEC - 1) * half
        for other, device in spot.targets(half, slot):
            copy = remote(
                source,
                self.sections[section].at[half * REP + spot.rep],
                self.send.at[half, other],
                self.arrive.at[section, half, spot.rep],
                device,
            )
            if half == 0:
                same = jnp.logical_and(other == spot.rep, device[1] == spot.blk)

                @pl.when(same)
                def _(source=source):
                    self.sections[0][spot.rep] = source[...]

                @pl.when(jnp.logical_not(same))
                def _(copy=copy):
                    copy.start()
            else:
                copy.start()

    def start_low(self):
        self.low = [
            self.line_copy(0, self.shard.at[0], 1, 2),
            self.line_copy(0, self.shard.at[0], 3, -2),
        ]
        for copy in self.low:
            copy.start()
        self.hand_on(0, 0, self.shard.at[0])

    def start_high(self):
        core = self.spot.core
        self.high = [
            self.line_copy(1, self.shard.at[1], 0, 1 + core),
            self.line_copy(1, self.shard.at[1], 3 - core, -1 - core),
        ]
        for copy in self.high:
            copy.start()

        @pl.when(core == 1)
        def _():
            self.hand_on(1, 3, self.shard.at[1])

    def pass_on(self):
        core, relay = self.spot.core, self.relay
        self.line_wait(0, 1)
        self.onward = self.line_copy(0, relay.at[0, 1], 2, 2)
        self.onward.start()
        self.hand_on(0, 1, relay.at[0, 1])
        self.line_wait(0, 3)
        self.hand_on(0, 3, relay.at[0, 3])
        self.line_wait(1, 3 - core)
        self.back = self.line_copy(1, relay.at[1, 3 - core], 2 - core, -2)
        self.back.start()
        self.line_wait(1, 0)
        self.forth = self.line_copy(1, relay.at[1, 0], 1, 2)

        @pl.when(core == 0)
        def _():
            self.forth.start()

        self.hand_on(1, 0, relay.at[1, 0])
        self.hand_on(1, 3 - core, relay.at[1, 3 - core])
        self.line_wait(0, 2)
        self.hand_on(0, 2, relay.at[0, 2])
        self.line_wait(1, 2 - core)
        self.hand_on(1, 2 - core, relay.at[1, 2 - core])

        @pl.when(core == 0)
        def _():
            self.line_wait(1, 1)
            self.hand_on(1, 1, relay.at[1, 1])

    def arrived(self, section, half, piece):
        landed(
            self.sections[section].at[half * REP + piece],
            self.dummy,
            self.arrive.at[section, half, piece],
            self.spot.here,
        )

    def chains(self, meanwhile=None):
        spot = self.spot
        for section in range(SEC - 1):
            other_section = SEC - 1 - section

            def hop(step, carry, section=section, other_section=other_section):
                piece = lax.rem(spot.rep + REP - step, REP)
                if section == 0:
                    @pl.when(jnp.logical_not(spot.local(piece)))
                    def _():
                        self.arrived(section, 0, piece)
                else:
                    self.arrived(section, 0, piece)
                remote(
                    self.sections[section].at[piece],
                    self.sections[section + 1].at[piece],
                    self.chain_send.at[0, section, piece],
                    self.arrive.at[section + 1, 0, piece],
                    spot.up,
                ).start()
                self.arrived(other_section, 1, piece)
                remote(
                    self.sections[other_section].at[REP + piece],
                    self.sections[other_section - 1].at[REP + piece],
                    self.chain_send.at[1, section, piece],
                    self.arrive.at[other_section - 1, 1, piece],
                    spot.down,
                ).start()
                return carry

            lax.fori_loop(0, REP, hop, 0)
            if meanwhile is not None:
                meanwhile(section)

    def last_arrivals(self):
        def finish(piece, carry):
            self.arrived(SEC - 1, 0, piece)
            self.arrived(0, 1, piece)
            return carry

        lax.fori_loop(0, REP, finish, 0)

    def drain(self):
        spot = self.spot
        sample = self.shard.at[0]

        def sent(semaphore):
            remote(sample, sample, semaphore, self.arrive.at[0, 0, 0], spot.here).wait_send()

        def body(piece, carry):
            for direction in range(2):
                for section in range(SEC - 1):
                    sent(self.chain_send.at[direction, section, piece])

            @pl.when(jnp.logical_not(spot.local(piece)))
            def _():
                sent(self.send.at[0, piece])

            sent(self.send.at[1, piece])
            return carry

        lax.fori_loop(0, REP, body, 0)
        for copy in (*self.low, *self.high, self.back, self.onward):
            copy.wait_send()

        @pl.when(spot.core == 0)
        def _():
            self.forth.wait_send()


def spread_scratch(height):
    dma = pltpu.SemaphoreType.DMA
    return [
        *[pltpu.VMEM((2 * REP, height, LANES), BF16)] * SEC,
        pltpu.VMEM((2, 4, height, LANES), BF16),
        dma((2, 4)),
        dma((2, 4)),
        dma((2, REP)),
        dma((2, SEC - 1, REP)),
        dma((SEC, 2, REP)),
    ]


class Scatter:
    def __init__(self, spot, pieces, landing, send, arrive):
        self.spot, self.pieces, self.landing = spot, pieces, landing
        self.send, self.arrive = send, arrive

    def copy(self, half, other, lands):
        return remote(
            self.pieces.at[half, other],
            self.landing.at[half, lands],
            self.send.at[half, other],
            self.arrive.at[half, lands],
            (other, self.spot.blk),
        )

    def put(self, half, make):
        rep = self.spot.rep

        def one(step, carry):
            other = lax.rem(rep + 1 + step, REP)
            self.pieces[half, other] = make(other)
            self.copy(half, other, rep).start()
            return carry

        lax.fori_loop(0, REP - 1, one, 0)
        self.landing[half, rep] = make(rep)

    def total(self, half):
        rep = self.spot.rep

        def one(step, carry):
            other = lax.rem(rep + 1 + step, REP)
            self.copy(half, other, other).wait_recv()
            return carry

        lax.fori_loop(0, REP - 1, one, 0)
        total = self.landing[half, 0].astype(F32)
        for index in range(1, REP):
            total = total + self.landing[half, index].astype(F32)
        return total

    def drain(self):
        def one(step, carry):
            other = lax.rem(self.spot.rep + 1 + step, REP)
            for half in range(self.pieces.shape[0]):
                self.copy(half, other, other).wait_send()
            return carry

        lax.fori_loop(0, REP - 1, one, 0)


def scatter_scratch(halves, height, width, dtype):
    dma = pltpu.SemaphoreType.DMA
    return [
        pltpu.VMEM((halves, REP, height, width), dtype),
        pltpu.VMEM((halves, REP, height, width), dtype),
        dma((halves, REP)),
        dma((halves, REP)),
    ]


def pack(values):
    half = TILE // 2
    lanes = lax.broadcasted_iota(jnp.int32, (half, LANES), 1)
    rest = jnp.where(
        lanes < half,
        values[:half, LANES:],
        pltpu.roll(values[half:, LANES:], half, 1),
    )
    return jnp.concatenate([values[:, :LANES], rest], axis=0).astype(BF16)


def unpack(packed):
    half = TILE // 2
    rest = packed[TILE:]
    turned = jnp.concatenate([rest[:, half:], rest[:, :half]], axis=1)
    return jnp.concatenate(
        [packed[:TILE], jnp.concatenate([rest, turned], axis=0)], axis=1
    )


def is_kept(ids):
    columns = lax.broadcasted_iota(jnp.int32, (1, WIDE), 1)
    mixed = (ids * 73244475 + 12345) + columns * 19349663
    mixed = jnp.bitwise_and(mixed ^ jnp.right_shift(mixed, 15), 32767) * (40503 % 32768)
    mixed = mixed ^ jnp.right_shift(mixed, 13)
    return jnp.bitwise_and(mixed, 3) != 0


def column_of(row):
    lanes = lax.broadcasted_iota(jnp.int32, (TILE, LANES), 1)
    rows = lax.broadcasted_iota(jnp.int32, (TILE, LANES), 0)
    spread_out = jnp.broadcast_to(row.astype(F32), (TILE, LANES))
    return jnp.sum(jnp.where(lanes == rows, spread_out, 0.0), axis=1, keepdims=True)


def step_kernel(
    scale,
    count,
    place,
    x_hbm,
    ids,
    labels,
    mask,
    tiles_hbm,
    weight_in_hbm,
    weight_out_hbm,
    bias,
    logits_out,
    full,
    x,
    tiles,
    weight_in,
    weight_out,
    input_sems,
    table_values,
    table,
    wide_out,
    wide_bias,
    running,
    coded,
    shard,
    kept,
    dense,
    back_rows,
    in_sum,
    out_sum,
    slopes,
    slope_send,
    slope_arrive,
    depth_in,
    pieces,
    pieces_in,
    b_send,
    b_arrive,
    c_send,
    c_arrive,
    d_send,
    d_arrive,
    *rest,
):
    rest = list(rest)

    def take(count):
        taken = rest[:count]
        del rest[:count]
        return taken

    spot = Spot()
    rep, blk = spot.rep, spot.blk
    first_sections = take(SEC)
    first_spread = Spread(spot, coded, first_sections, *take(6))
    second_sections = take(SEC)
    second_spread = Spread(spot, shard, second_sections, *take(6))
    first_scatter = Scatter(spot, *take(4))
    second_scatter = Scatter(spot, *take(4))
    waits = greet_everyone(spot)
    input_copies = [
        pltpu.make_async_copy(source, target, input_sems.at[index])
        for index, (source, target) in enumerate(
            (
                (x_hbm, x),
                (weight_out_hbm, weight_out),
                (weight_in_hbm, weight_in),
                (tiles_hbm, tiles),
            )
        )
    ]
    for copy in input_copies:
        copy.start()
    fill_tables(place, count, table_values)
    table_copy = pltpu.make_async_copy(table_values, table, input_sems.at[len(input_copies)])
    table_copy.start()
    running[NONE] = jnp.zeros((TILE, WIDE), F32)
    wide_out[...] = jnp.zeros_like(wide_out)
    wide_bias[...] = jnp.zeros_like(wide_bias)
    wide_bias[:, :CLASSES] = bias[...]
    input_copies[0].wait()
    input_copies[1].wait()
    wide_out[:CLASSES, :] = weight_out[...]
    code_rows = lax.broadcasted_iota(jnp.int32, (CODED - TILE, LANES), 0)
    for half in range(2):
        coded[half, :TILE] = x[half]
        number = ids[half : half + 1, :]
        code = jnp.zeros((CODED - TILE, LANES), F32)
        for byte in range(3):
            value = jnp.bitwise_and(jnp.right_shift(number, 8 * byte), 255).astype(F32)
            code = jnp.where(code_rows == byte, jnp.broadcast_to(value, code.shape), code)
        coded[half, TILE:] = code.astype(BF16)
    pl.semaphore_wait(pltpu.get_barrier_semaphore(), waits)

    def products(section, width, source_of):
        place = FORWARD_ORDER.index(section)

        def some(group, carry):
            made = []
            for inner in range(4):
                slot = group * 4 + inner
                made.append(
                    jnp.dot(
                        tiles[section * SLOTS + slot],
                        source_of(table[SOURCE + section, slot]),
                        preferred_element_type=F32,
                    )
                )
            for inner in range(4):
                slot = group * 4 + inner
                running[place * SLOTS + slot, :, :width] = (
                    made[inner] + running[table[PREVIOUS + section, slot], :, :width]
                )
            return carry

        lax.fori_loop(0, SLOTS // 4, some, 0)

    def first_products(section):
        products(section, LANES, lambda index: first_sections[section][index, :TILE])

    def second_products(section):
        products(section, WIDE, lambda index: dense[section * SLOTS + index])

    def first_sum(half):
        return lambda other: running[table[LAST, 2 * other + half], :, :LANES]

    def second_sum(half):
        def one(other):
            part = running[table[LAST, 2 * other + half]].astype(BF16)
            return pack(
                lax.dot_general(
                    part, wide_out[...], (((1,), (1,)), ((), ())), preferred_element_type=F32
                )
            )

        return one

    def find_kept(section):
        lanes = lax.broadcasted_iota(jnp.int32, (TILE, LANES), 1)
        rows = lax.broadcasted_iota(jnp.int32, (TILE, LANES), 0)
        unit = jnp.where(lanes == rows, 1.0, 0.0).astype(BF16)

        def one(index, carry):
            code = lax.dot_general(
                unit,
                first_sections[section][index, TILE:],
                (((1,), (1,)), ((), ())),
                preferred_element_type=F32,
            )
            number = code[:, 0:1] + 256.0 * code[:, 1:2] + 65536.0 * code[:, 2:3]
            kept[section * SLOTS + index] = jnp.where(
                is_kept(number.astype(jnp.int32)), 1.0, 0.0
            ).astype(BF16)
            return carry

        lax.fori_loop(0, SLOTS, one, 0, unroll=4)

    def activate(section, half):
        def one(index, carry):
            pre_act = jnp.dot(
                second_sections[section][index], weight_in[...], preferred_element_type=F32
            )
            active = jnp.maximum(pre_act, 0.0) * F32(KEEP)
            flag = kept[section * SLOTS + index].astype(F32)
            dense[section * SLOTS + index] = jnp.where(flag > 0.0, active, 0.0).astype(BF16)
            return carry

        lax.fori_loop(half * REP, (half + 1) * REP, one, 0, unroll=4)

    def activate_arrived(section):
        activate(section, 0)
        activate(SEC - 1 - section, 1)

    first_spread.start_low()
    first_spread.start_high()
    first_spread.pass_on()
    first_spread.chains()
    input_copies[2].wait()
    input_copies[3].wait()
    table_copy.wait()
    first_products(1)
    first_products(2)
    first_spread.last_arrivals()
    first_products(0)
    first_products(3)
    first_scatter.put(0, first_sum(0))
    first_scatter.put(1, first_sum(1))
    for section in range(SEC):
        find_kept(section)
    shard[0] = first_scatter.total(0).astype(BF16)
    second_spread.start_low()
    shard[1] = first_scatter.total(1).astype(BF16)
    second_spread.start_high()
    second_spread.pass_on()
    second_spread.chains(activate_arrived)
    second_products(1)
    second_products(2)
    second_spread.last_arrivals()
    activate_arrived(SEC - 1)
    second_products(0)
    second_products(3)
    second_scatter.put(0, second_sum(0))
    second_scatter.put(1, second_sum(1))
    first_spread.drain()
    second_spread.drain()
    first_scatter.drain()

    def slope_copy(half, other, lands):
        return remote(
            slopes.at[2 * rep + half],
            slopes.at[2 * lands + half],
            slope_send.at[half, other],
            slope_arrive.at[half, lands],
            (other, blk),
        )

    def classes(half):
        logits = unpack(second_scatter.total(half)) + wide_bias[...]
        columns = lax.broadcasted_iota(jnp.int32, logits.shape, 1)
        real = columns < CLASSES
        top = jnp.max(jnp.where(real, logits, -jnp.inf), axis=1, keepdims=True)
        powers = jnp.where(real, jnp.exp(jnp.where(real, logits - top, 0.0)), 0.0)
        likelihood = powers / jnp.sum(powers, axis=1, keepdims=True)
        label = column_of(labels[half : half + 1, :]).astype(jnp.int32)
        onehot = jnp.where(columns == label, 1.0, 0.0)
        chosen = column_of(mask[half : half + 1, :]) * scale
        slopes[2 * rep + half] = pack((likelihood - onehot) * chosen)
        for step in range(1, REP):
            slope_copy(half, lax.rem(rep + step, REP), rep).start()
        return logits

    low_logits = classes(0)
    high_logits = classes(1)
    logits_out[:, :TILE] = low_logits.T[:CLASSES]
    logits_out[:, TILE:] = high_logits.T[:CLASSES]
    second_scatter.drain()

    def slope_waits(step, carry):
        other = lax.rem(rep + step, REP)
        for half in range(2):
            copy = remote(
                slopes.at[2 * rep + half],
                slopes.at[2 * other + half],
                slope_send.at[half, other],
                slope_arrive.at[half, other],
                (other, blk),
            )
            copy.wait_recv()
            copy.wait_send()
        return carry

    lax.fori_loop(1, REP, slope_waits, 0)

    def back_products(section):
        def some(group, carry):
            made = []
            for inner in range(4):
                slot = group * 4 + inner
                made.append(
                    lax.dot_general(
                        tiles[section * SLOTS + slot],
                        unpack(slopes[table[ROW + section, slot]]),
                        (((0,), (0,)), ((), ())),
                        preferred_element_type=F32,
                    )
                )
            for inner in range(4):
                slot = group * 4 + inner
                running[section * SLOTS + slot] = (
                    made[inner] + running[table[BACK_PREVIOUS + section, slot]]
                )
            return carry

        lax.fori_loop(0, SLOTS // 4, some, 0)

        def gather(piece, carry):
            for half in range(2):
                back_rows[section * SLOTS + half * REP + piece] = running[
                    table[BACK_LAST + section, 2 * piece + half]
                ].astype(BF16)
            return carry

        lax.fori_loop(0, REP, gather, 0, unroll=2)

    in_sum[...] = jnp.zeros_like(in_sum)
    out_sum[...] = jnp.zeros_like(out_sum)

    def terms(section):
        for half in range(2):
            inside = pl.ds(section * SLOTS + half * REP, REP)
            back = back_rows[inside].reshape(REP * TILE, WIDE)
            active = dense[inside].reshape(REP * TILE, WIDE)
            z_rows = second_sections[section][half * REP : (half + 1) * REP].reshape(
                REP * TILE, LANES
            )
            out_sum[...] += lax.dot_general(
                back, active, (((0,), (0,)), ((), ())), preferred_element_type=F32
            )
            hidden_rows = jnp.dot(back, wide_out[...], preferred_element_type=F32)
            pre_slope = jnp.where(
                active.astype(F32) > 0.0, hidden_rows * F32(KEEP), 0.0
            ).astype(BF16)
            in_sum[...] += lax.dot_general(
                z_rows, pre_slope, (((0,), (0,)), ((), ())), preferred_element_type=F32
            )

    for section in range(SEC):
        back_products(section)
        terms(section)
    joined = jnp.concatenate([in_sum[...], out_sum[...]], axis=0)
    for index in range(CREW):
        row = index % (CREW // 2) * CHUNK
        lane = index // (CREW // 2) * LANES
        pieces[index] = joined[row : row + CHUNK, lane : lane + LANES].astype(BF16)
    me, depth = spot.member, spot.depth

    def reduce_copy(other, lands):
        return remote(
            pieces.at[other],
            pieces_in.at[lands],
            b_send.at[other],
            b_arrive.at[lands],
            spot.crew(other),
        )

    def gather_copy(other, lands):
        return remote(
            full.at[me], full.at[lands], d_send.at[other], d_arrive.at[lands], spot.crew(other)
        )

    def start_all(copy):
        def one(step, carry):
            copy(lax.rem(me + step, CREW), me).start()
            return carry

        lax.fori_loop(1, CREW, one, 0)

    def wait_all(copy):
        def one(step, carry):
            other = lax.rem(me + step, CREW)
            both = copy(other, other)
            both.wait_recv()
            both.wait_send()
            return carry

        lax.fori_loop(1, CREW, one, 0)

    start_all(reduce_copy)
    pieces_in[me] = pieces[me]
    wait_all(reduce_copy)
    total = pieces_in[0].astype(F32)
    for index in range(1, CREW):
        total = total + pieces_in[index].astype(F32)
    depth_in[depth] = total
    for step in range(1, DEPTH):
        remote(
            depth_in.at[depth],
            depth_in.at[depth],
            c_send.at[step],
            c_arrive.at[depth],
            spot.line(step),
        ).start()
    for step in range(1, DEPTH):
        other = lax.rem(depth + step, DEPTH)
        copy = remote(
            depth_in.at[depth],
            depth_in.at[other],
            c_send.at[step],
            c_arrive.at[other],
            spot.line(step),
        )
        copy.wait_recv()
        copy.wait_send()
    total = depth_in[0]
    for index in range(1, DEPTH):
        total = total + depth_in[index]
    full[me] = total.astype(BF16)
    start_all(gather_copy)
    wait_all(gather_copy)


def result_kernel(in_rows, logits, full, logits_out, grad_in, grad_out):
    logits_out[:, 0, :] = logits[...]
    joined = jnp.concatenate(
        [
            jnp.concatenate(
                [full[start + index].astype(F32) for index in range(CREW // 2)], axis=0
            )
            for start in (0, CREW // 2)
        ],
        axis=1,
    )
    grad_in[...] = joined[:in_rows]
    grad_out[...] = joined[in_rows : in_rows + CLASSES]


def fill_tables(place, count, out):
    slots = lax.broadcasted_iota(jnp.int32, (SLOTS, SLOTS), 1)
    others = lax.broadcasted_iota(jnp.int32, (SLOTS, SLOTS), 0)
    before = others < slots

    def turned(line):
        flat = jnp.broadcast_to(line.astype(F32), (SLOTS, SLOTS))
        column = jnp.sum(jnp.where(slots == others, flat, 0.0), axis=1, keepdims=True)
        return column.astype(jnp.int32)

    def top(match, entries):
        return jnp.max(jnp.where(match, entries, -1), axis=0, keepdims=True)

    def put(row, values):
        out[row : row + 1, :SLOTS] = values

    def settled(values):
        return jnp.where(values < 0, NONE, values)

    rows, columns, row_turned, column_turned, live = [], [], [], [], []
    for section in range(SEC):
        line = place[section : section + 1, :]
        rows.append(jnp.right_shift(line, 4))
        columns.append(jnp.bitwise_and(line, SLOTS - 1))
        row_turned.append(turned(rows[section]))
        column_turned.append(turned(columns[section]))
        live.append(others < count[section])
    numbers = slots[:1]
    last = jnp.full((1, SLOTS), -1, jnp.int32)
    for section in range(SEC):
        turn = FORWARD_ORDER.index(section)
        entries = others + turn * SLOTS
        latest = jnp.full((1, SLOTS), -1, jnp.int32)
        for earlier in FORWARD_ORDER[: turn + 1]:
            match = (row_turned[earlier] == rows[section]) & live[earlier]
            if earlier == section:
                match = match & before
            latest = jnp.maximum(
                latest, top(match, others + FORWARD_ORDER.index(earlier) * SLOTS)
            )
        last = jnp.maximum(last, top((row_turned[section] == numbers) & live[section], entries))
        put(SOURCE + section, jnp.bitwise_and(columns[section], 1) * REP + jnp.right_shift(columns[section], 1))
        put(PREVIOUS + section, settled(latest))
        put(ROW + section, rows[section])
        own = others + section * SLOTS
        match = (column_turned[section] == columns[section]) & live[section]
        put(BACK_PREVIOUS + section, settled(top(match & before, own)))
        match = (column_turned[section] == numbers) & live[section]
        put(BACK_LAST + section, settled(top(match, own)))
    put(LAST, settled(last))


def on_device(
    features,
    node_ids,
    labels,
    train_mask,
    tile_values,
    tile_place,
    tile_count,
    weight_in,
    weight_out,
    class_bias,
):
    width = features.shape[-1]
    own_rows = features.shape[1]
    scale = 1.0 / math.sqrt(own_rows * REP * BLK)
    shape = jax.ShapeDtypeStruct
    dma = pltpu.SemaphoreType.DMA
    vmem = pltpu.VMEM
    anywhere = pl.BlockSpec(memory_space=pl.ANY)
    logits, full = pl.pallas_call(
        lambda *refs: step_kernel(scale, *refs),
        out_shape=(shape((CLASSES, own_rows), F32), shape((CREW, CHUNK, LANES), BF16)),
        in_specs=[
            pl.BlockSpec(memory_space=pltpu.SMEM),
            whole(),
            anywhere,
            whole(),
            whole(),
            whole(),
            anywhere,
            anywhere,
            anywhere,
            whole(),
        ],
        out_specs=[whole()] * 2,
        scratch_shapes=[
            vmem((2, TILE, width), BF16),
            vmem((NONE, TILE, TILE), BF16),
            vmem((width, WIDE), BF16),
            vmem((CLASSES, WIDE), BF16),
            dma((5,)),
            vmem((24, LANES), jnp.int32),
            pltpu.SMEM((24, LANES), jnp.int32),
            vmem((WIDE, WIDE), BF16),
            vmem((1, WIDE), F32),
            vmem((NONE + 1, TILE, WIDE), F32),
            vmem((2, CODED, LANES), BF16),
            vmem((2, TILE, LANES), BF16),
            vmem((NONE, TILE, WIDE), BF16),
            vmem((NONE, TILE, WIDE), BF16),
            vmem((NONE, TILE, WIDE), BF16),
            vmem((width, WIDE), F32),
            vmem((WIDE, WIDE), F32),
            vmem((2 * REP, PACKED, LANES), BF16),
            dma((2, REP)),
            dma((2, REP)),
            vmem((DEPTH, CHUNK, LANES), F32),
            vmem((CREW, CHUNK, LANES), BF16),
            vmem((CREW, CHUNK, LANES), BF16),
            dma((CREW,)),
            dma((CREW,)),
            dma((DEPTH,)),
            dma((DEPTH,)),
            dma((CREW,)),
            dma((CREW,)),
            *spread_scratch(CODED),
            *spread_scratch(TILE),
            *scatter_scratch(2, TILE, LANES, F32),
            *scatter_scratch(2, PACKED, LANES, BF16),
        ],
        compiler_params=pltpu.CompilerParams(
            collective_id=0, has_side_effects=True, vmem_limit_bytes=VMEM_LIMIT
        ),
        name="training_step",
    )(
        tile_count.reshape(SEC),
        tile_place.reshape(SEC, SLOTS),
        features.reshape(2, TILE, width),
        node_ids.reshape(2, TILE),
        labels.reshape(2, TILE),
        train_mask.reshape(2, TILE),
        tile_values.reshape(NONE, TILE, TILE),
        weight_in,
        weight_out.T,
        class_bias.reshape(1, CLASSES),
    )
    logits, grad_in, grad_out = pl.pallas_call(
        lambda *refs: result_kernel(width, *refs),
        out_shape=(
            shape((CLASSES, 1, own_rows), F32),
            shape((width, WIDE), F32),
            shape((CLASSES, WIDE), F32),
        ),
        in_specs=[whole()] * 2,
        out_specs=[whole()] * 3,
        name="results",
    )(logits, full)
    return (logits.transpose(1, 2, 0), grad_in, grad_out.T)


def solution(mesh):
    placed = (
        P("blk", "rep", None),
        P("blk", "rep"),
        P("blk", "rep"),
        P("blk", "rep"),
        P("blk", "rep", None, None, None, None),
        P("blk", "rep", None, None),
        P("blk", "rep", None),
        P(),
        P(),
        P(),
    )
    return jax.shard_map(
        on_device,
        mesh=mesh,
        in_specs=placed,
        out_specs=(P("blk", "rep", None), P(), P()),
        check_vma=False,
    )
```

```python
import math

import jax
import jax.numpy as jnp
from jax import lax
from jax.experimental import pallas as pl
from jax.experimental.pallas import tpu as pltpu
from jax.sharding import PartitionSpec as P

MESH = pl.DeviceIdType.MESH
F32 = jnp.float32
BF16 = jnp.bfloat16
REP = 8
BLK = 32
SEC = 4
TILE = 128
SLOTS = 16
WIDE = 256
CLASSES = 172
LANES = 128
PACKED = 192
DEPTH = 8
NONE = SEC * SLOTS
FORWARD_ORDER = (1, 2, 0, 3)
CODED = 144
CREW = 32
KEEP = 4.0 / 3.0
CHUNK = 24
SOURCE, PREVIOUS, ROW, BACK_PREVIOUS, BACK_LAST, LAST = 0, 4, 8, 12, 16, 20
VMEM_LIMIT = 60 << 20


def whole():
    return pl.BlockSpec(memory_space=pltpu.VMEM)


def remote(source, target, send, arrive, device):
    return pltpu.make_async_remote_copy(
        src_ref=source,
        dst_ref=target,
        send_sem=send,
        recv_sem=arrive,
        device_id=device,
        device_id_type=MESH,
    )


def landed(target, send, arrive, device):
    remote(target, target, send, arrive, device).wait_recv()


def greet(device):
    pl.semaphore_signal(
        pltpu.get_barrier_semaphore(), inc=1, device_id=device, device_id_type=MESH
    )


def blk_of(part, depth, core):
    return (part * (BLK // 4) + depth) * 2 + core


class Spot:
    def __init__(self):
        self.rep = lax.axis_index("rep")
        self.blk = lax.axis_index("blk")
        self.core = lax.rem(self.blk, 2)
        self.depth = lax.rem(self.blk // 2, DEPTH)
        self.part = self.blk // 16
        self.here = (self.rep, self.blk)
        self.up = (self.rep, lax.rem(self.blk + 1, BLK))
        self.down = (self.rep, lax.rem(self.blk + BLK - 1, BLK))
        low_block = lax.rem(self.blk - SEC * self.rep + BLK, BLK)
        high_block = lax.rem(self.blk - SEC * self.rep - (SEC - 1) + 2 * BLK, BLK)
        self.low_relay = (low_block // 16) * 16 + lax.rem(self.blk, 16)
        self.high_relay = blk_of(high_block // 16, self.depth, 1 - self.core)
        self.own_relay = self.low_relay == self.blk
        self.member = self.rep * 4 + self.part * 2 + self.core

    def line(self, step):
        return (self.rep, blk_of(self.part, lax.rem(self.depth + step + DEPTH, DEPTH), self.core))

    def crew(self, index):
        corner = lax.rem(index, 4)
        return (index // 4, blk_of(corner // 2, self.depth, lax.rem(corner, 2)))

    def local(self, piece):
        return jnp.logical_and(self.own_relay, piece == self.rep)

    def targets(self, half, slot):
        offset = 2 * slot + half * (1 + self.core)
        source = blk_of(self.part, lax.rem(self.depth - offset + 2 * DEPTH, DEPTH), self.core)
        for other in (slot, slot + 4):
            yield other, (other, lax.rem(source + (SEC - 1) * half + SEC * other, BLK))


def greet_everyone(spot):
    for step in range(1, CREW):
        greet(spot.crew(lax.rem(spot.member + step, CREW)))
    for step in range(1, DEPTH):
        greet(spot.line(step))
    for other in range(REP):
        @pl.when(jnp.logical_not(spot.local(other)))
        def _(other=other):
            greet((other, spot.low_relay))

        greet((other, spot.high_relay))
    greet(spot.up)
    greet(spot.down)
    count = (CREW - 1) + (DEPTH - 1) + 2 * REP + 2
    return count - jnp.where(spot.own_relay, 1, 0)


class Spread:
    def __init__(self, spot, shard, sections, relay, line_send, line_arrive, send, chain_send, arrive):
        self.spot, self.shard, self.sections, self.relay = spot, shard, sections, relay
        self.line_send, self.line_arrive, self.send = line_send, line_arrive, send
        self.chain_send, self.arrive = chain_send, arrive
        self.dummy = chain_send.at[0, 0, 0]

    def line_copy(self, half, source, slot, step):
        return remote(
            source,
            self.relay.at[half, slot],
            self.line_send.at[half, slot],
            self.line_arrive.at[half, slot],
            self.spot.line(step),
        )

    def line_wait(self, half, slot):
        landed(
            self.relay.at[half, slot], self.dummy, self.line_arrive.at[half, slot], self.spot.here
        )

    def hand_on(self, half, slot, source):
        spot = self.spot
        section = (SEC - 1) * half
        for other, device in spot.targets(half, slot):
            copy = remote(
                source,
                self.sections[section].at[half * REP + spot.rep],
                self.send.at[half, other],
                self.arrive.at[section, half, spot.rep],
                device,
            )
            if half == 0:
                same = jnp.logical_and(other == spot.rep, device[1] == spot.blk)

                @pl.when(same)
                def _(source=source):
                    self.sections[0][spot.rep] = source[...]

                @pl.when(jnp.logical_not(same))
                def _(copy=copy):
                    copy.start()
            else:
                copy.start()

    def start_low(self):
        self.low = [
            self.line_copy(0, self.shard.at[0], 1, 2),
            self.line_copy(0, self.shard.at[0], 3, -2),
        ]
        for copy in self.low:
            copy.start()
        self.hand_on(0, 0, self.shard.at[0])

    def start_high(self):
        core = self.spot.core
        self.high = [
            self.line_copy(1, self.shard.at[1], 0, 1 + core),
            self.line_copy(1, self.shard.at[1], 3 - core, -1 - core),
        ]
        for copy in self.high:
            copy.start()

        @pl.when(core == 1)
        def _():
            self.hand_on(1, 3, self.shard.at[1])

    def pass_on(self):
        core, relay = self.spot.core, self.relay
        self.line_wait(0, 1)
        self.onward = self.line_copy(0, relay.at[0, 1], 2, 2)
        self.onward.start()
        self.hand_on(0, 1, relay.at[0, 1])
        self.line_wait(0, 3)
        self.hand_on(0, 3, relay.at[0, 3])
        self.line_wait(1, 3 - core)
        self.back = self.line_copy(1, relay.at[1, 3 - core], 2 - core, -2)
        self.back.start()
        self.line_wait(1, 0)
        self.forth = self.line_copy(1, relay.at[1, 0], 1, 2)

        @pl.when(core == 0)
        def _():
            self.forth.start()

        self.hand_on(1, 0, relay.at[1, 0])
        self.hand_on(1, 3 - core, relay.at[1, 3 - core])
        self.line_wait(0, 2)
        self.hand_on(0, 2, relay.at[0, 2])
        self.line_wait(1, 2 - core)
        self.hand_on(1, 2 - core, relay.at[1, 2 - core])

        @pl.when(core == 0)
        def _():
            self.line_wait(1, 1)
            self.hand_on(1, 1, relay.at[1, 1])

    def arrived(self, section, half, piece):
        landed(
            self.sections[section].at[half * REP + piece],
            self.dummy,
            self.arrive.at[section, half, piece],
            self.spot.here,
        )

    def chains(self, meanwhile=None):
        spot = self.spot
        for section in range(SEC - 1):
            other_section = SEC - 1 - section

            def hop(step, carry, section=section, other_section=other_section):
                piece = lax.rem(spot.rep + REP - step, REP)
                if section == 0:
                    @pl.when(jnp.logical_not(spot.local(piece)))
                    def _():
                        self.arrived(section, 0, piece)
                else:
                    self.arrived(section, 0, piece)
                remote(
                    self.sections[section].at[piece],
                    self.sections[section + 1].at[piece],
                    self.chain_send.at[0, section, piece],
                    self.arrive.at[section + 1, 0, piece],
                    spot.up,
                ).start()
                self.arrived(other_section, 1, piece)
                remote(
                    self.sections[other_section].at[REP + piece],
                    self.sections[other_section - 1].at[REP + piece],
                    self.chain_send.at[1, section, piece],
                    self.arrive.at[other_section - 1, 1, piece],
                    spot.down,
                ).start()
                return carry

            lax.fori_loop(0, REP, hop, 0)
            if meanwhile is not None:
                meanwhile(section)

    def last_arrivals(self):
        def finish(piece, carry):
            self.arrived(SEC - 1, 0, piece)
            self.arrived(0, 1, piece)
            return carry

        lax.fori_loop(0, REP, finish, 0)

    def drain(self):
        spot = self.spot
        sample = self.shard.at[0]

        def sent(semaphore):
            remote(sample, sample, semaphore, self.arrive.at[0, 0, 0], spot.here).wait_send()

        def body(piece, carry):
            for direction in range(2):
                for section in range(SEC - 1):
                    sent(self.chain_send.at[direction, section, piece])

            @pl.when(jnp.logical_not(spot.local(piece)))
            def _():
                sent(self.send.at[0, piece])

            sent(self.send.at[1, piece])
            return carry

        lax.fori_loop(0, REP, body, 0)
        for copy in (*self.low, *self.high, self.back, self.onward):
            copy.wait_send()

        @pl.when(spot.core == 0)
        def _():
            self.forth.wait_send()


def spread_scratch(height):
    dma = pltpu.SemaphoreType.DMA
    return [
        *[pltpu.VMEM((2 * REP, height, LANES), BF16)] * SEC,
        pltpu.VMEM((2, 4, height, LANES), BF16),
        dma((2, 4)),
        dma((2, 4)),
        dma((2, REP)),
        dma((2, SEC - 1, REP)),
        dma((SEC, 2, REP)),
    ]


class Scatter:
    def __init__(self, spot, pieces, landing, send, arrive):
        self.spot, self.pieces, self.landing = spot, pieces, landing
        self.send, self.arrive = send, arrive

    def copy(self, half, other, lands):
        return remote(
            self.pieces.at[half, other],
            self.landing.at[half, lands],
            self.send.at[half, other],
            self.arrive.at[half, lands],
            (other, self.spot.blk),
        )

    def put(self, half, make):
        rep = self.spot.rep

        def one(step, carry):
            other = lax.rem(rep + 1 + step, REP)
            self.pieces[half, other] = make(other)
            self.copy(half, other, rep).start()
            return carry

        lax.fori_loop(0, REP - 1, one, 0)
        self.landing[half, rep] = make(rep)

    def total(self, half):
        rep = self.spot.rep

        def one(step, carry):
            other = lax.rem(rep + 1 + step, REP)
            self.copy(half, other, other).wait_recv()
            return carry

        lax.fori_loop(0, REP - 1, one, 0)
        total = self.landing[half, 0].astype(F32)
        for index in range(1, REP):
            total = total + self.landing[half, index].astype(F32)
        return total

    def drain(self):
        def one(step, carry):
            other = lax.rem(self.spot.rep + 1 + step, REP)
            for half in range(self.pieces.shape[0]):
                self.copy(half, other, other).wait_send()
            return carry

        lax.fori_loop(0, REP - 1, one, 0)


def scatter_scratch(halves, height, width, dtype):
    dma = pltpu.SemaphoreType.DMA
    return [
        pltpu.VMEM((halves, REP, height, width), dtype),
        pltpu.VMEM((halves, REP, height, width), dtype),
        dma((halves, REP)),
        dma((halves, REP)),
    ]


def pack(values):
    half = TILE // 2
    lanes = lax.broadcasted_iota(jnp.int32, (half, LANES), 1)
    rest = jnp.where(
        lanes < half,
        values[:half, LANES:],
        pltpu.roll(values[half:, LANES:], half, 1),
    )
    return jnp.concatenate([values[:, :LANES], rest], axis=0).astype(BF16)


def unpack(packed):
    half = TILE // 2
    rest = packed[TILE:]
    turned = jnp.concatenate([rest[:, half:], rest[:, :half]], axis=1)
    return jnp.concatenate(
        [packed[:TILE], jnp.concatenate([rest, turned], axis=0)], axis=1
    )


def is_kept(ids):
    columns = lax.broadcasted_iota(jnp.int32, (1, WIDE), 1)
    mixed = (ids * 73244475 + 12345) + columns * 19349663
    mixed = jnp.bitwise_and(mixed ^ jnp.right_shift(mixed, 15), 32767) * (40503 % 32768)
    mixed = mixed ^ jnp.right_shift(mixed, 13)
    return jnp.bitwise_and(mixed, 3) != 0


def column_of(row):
    lanes = lax.broadcasted_iota(jnp.int32, (TILE, LANES), 1)
    rows = lax.broadcasted_iota(jnp.int32, (TILE, LANES), 0)
    spread_out = jnp.broadcast_to(row.astype(F32), (TILE, LANES))
    return jnp.sum(jnp.where(lanes == rows, spread_out, 0.0), axis=1, keepdims=True)


def step_kernel(
    scale,
    count,
    place,
    x_hbm,
    ids,
    labels,
    mask,
    tiles_hbm,
    weight_in_hbm,
    weight_out_hbm,
    bias,
    logits_out,
    full,
    x,
    tiles,
    weight_in,
    weight_out,
    input_sems,
    table_values,
    table,
    wide_out,
    wide_bias,
    running,
    coded,
    shard,
    kept,
    dense,
    back_rows,
    in_sum,
    out_sum,
    slopes,
    wide_slopes,
    slope_send,
    slope_arrive,
    depth_in,
    pieces,
    pieces_in,
    b_send,
    b_arrive,
    c_send,
    c_arrive,
    d_send,
    d_arrive,
    *rest,
):
    rest = list(rest)

    def take(count):
        taken = rest[:count]
        del rest[:count]
        return taken

    spot = Spot()
    rep, blk = spot.rep, spot.blk
    first_sections = take(SEC)
    first_spread = Spread(spot, coded, first_sections, *take(6))
    second_sections = take(SEC)
    second_spread = Spread(spot, shard, second_sections, *take(6))
    first_scatter = Scatter(spot, *take(4))
    second_scatter = Scatter(spot, *take(4))
    waits = greet_everyone(spot)
    input_copies = [
        pltpu.make_async_copy(source, target, input_sems.at[index])
        for index, (source, target) in enumerate(
            (
                (x_hbm, x),
                (weight_out_hbm, weight_out),
                (weight_in_hbm, weight_in),
                (tiles_hbm, tiles),
            )
        )
    ]
    for copy in input_copies:
        copy.start()
    table_copy = pltpu.make_async_copy(table_values, table, input_sems.at[len(input_copies)])

    def prepare(section):
        if section == 0:
            fill_tables(place, count, table_values)
            table_copy.start()
        elif section == 1:
            running[NONE] = jnp.zeros((TILE, WIDE), F32)
            wide_out[...] = jnp.zeros_like(wide_out)
            wide_bias[...] = jnp.zeros_like(wide_bias)
            wide_bias[:, :CLASSES] = bias[...]
            input_copies[1].wait()
            wide_out[:CLASSES, :] = weight_out[...]
            input_copies[2].wait()
            input_copies[3].wait()
            table_copy.wait()

    input_copies[0].wait()
    code_rows = lax.broadcasted_iota(jnp.int32, (CODED - TILE, LANES), 0)
    for half in range(2):
        coded[half, :TILE] = x[half]
        number = ids[half : half + 1, :]
        code = jnp.zeros((CODED - TILE, LANES), F32)
        for byte in range(3):
            value = jnp.bitwise_and(jnp.right_shift(number, 8 * byte), 255).astype(F32)
            code = jnp.where(code_rows == byte, jnp.broadcast_to(value, code.shape), code)
        coded[half, TILE:] = code.astype(BF16)
    pl.semaphore_wait(pltpu.get_barrier_semaphore(), waits)

    def products(section, width, source_of):
        place = FORWARD_ORDER.index(section)

        def some(group, carry):
            made = []
            for inner in range(4):
                slot = group * 4 + inner
                made.append(
                    jnp.dot(
                        tiles[section * SLOTS + slot],
                        source_of(table[SOURCE + section, slot]),
                        preferred_element_type=F32,
                    )
                )
            for inner in range(4):
                slot = group * 4 + inner
                running[place * SLOTS + slot, :, :width] = (
                    made[inner] + running[table[PREVIOUS + section, slot], :, :width]
                )
            return carry

        lax.fori_loop(0, SLOTS // 4, some, 0, unroll=2)

    def first_products(section):
        products(section, LANES, lambda index: first_sections[section][index, :TILE])

    def second_products(section):
        products(section, WIDE, lambda index: dense[section * SLOTS + index])

    def first_sum(half):
        return lambda other: running[table[LAST, 2 * other + half], :, :LANES]

    def second_sum(half):
        def one(other):
            part = running[table[LAST, 2 * other + half]].astype(BF16)
            return pack(
                lax.dot_general(
                    part, wide_out[...], (((1,), (1,)), ((), ())), preferred_element_type=F32
                )
            )

        return one

    def find_kept(section):
        lanes = lax.broadcasted_iota(jnp.int32, (TILE, LANES), 1)
        rows = lax.broadcasted_iota(jnp.int32, (TILE, LANES), 0)
        unit = jnp.where(lanes == rows, 1.0, 0.0).astype(BF16)

        def one(index, carry):
            code = lax.dot_general(
                unit,
                first_sections[section][index, TILE:],
                (((1,), (1,)), ((), ())),
                preferred_element_type=F32,
            )
            number = code[:, 0:1] + 256.0 * code[:, 1:2] + 65536.0 * code[:, 2:3]
            kept[section * SLOTS + index] = jnp.where(
                is_kept(number.astype(jnp.int32)), 1.0, 0.0
            ).astype(BF16)
            return carry

        lax.fori_loop(0, SLOTS, one, 0, unroll=4)

    def activate(section, half):
        def one(index, carry):
            pre_act = jnp.dot(
                second_sections[section][index], weight_in[...], preferred_element_type=F32
            )
            active = jnp.maximum(pre_act, 0.0) * F32(KEEP)
            flag = kept[section * SLOTS + index].astype(F32)
            dense[section * SLOTS + index] = jnp.where(flag > 0.0, active, 0.0).astype(BF16)
            return carry

        lax.fori_loop(half * REP, (half + 1) * REP, one, 0, unroll=4)

    def activate_arrived(section):
        activate(section, 0)
        activate(SEC - 1 - section, 1)

    first_spread.start_low()
    first_spread.start_high()
    first_spread.pass_on()
    first_spread.chains(prepare)
    first_products(1)
    first_products(2)
    first_spread.last_arrivals()
    first_products(0)
    first_products(3)
    first_scatter.put(0, first_sum(0))
    first_scatter.put(1, first_sum(1))
    for section in range(SEC):
        find_kept(section)
    shard[0] = first_scatter.total(0).astype(BF16)
    second_spread.start_low()
    shard[1] = first_scatter.total(1).astype(BF16)
    second_spread.start_high()
    second_spread.pass_on()
    second_spread.chains(activate_arrived)
    second_products(1)
    second_products(2)
    second_spread.last_arrivals()
    activate_arrived(SEC - 1)
    second_products(0)
    second_products(3)
    second_scatter.put(0, second_sum(0))
    second_scatter.put(1, second_sum(1))
    first_spread.drain()
    second_spread.drain()
    first_scatter.drain()

    def slope_copy(half, other, lands):
        return remote(
            slopes.at[2 * rep + half],
            slopes.at[2 * lands + half],
            slope_send.at[half, other],
            slope_arrive.at[half, lands],
            (other, blk),
        )

    def classes(half):
        logits = unpack(second_scatter.total(half)) + wide_bias[...]
        columns = lax.broadcasted_iota(jnp.int32, logits.shape, 1)
        real = columns < CLASSES
        top = jnp.max(jnp.where(real, logits, -jnp.inf), axis=1, keepdims=True)
        powers = jnp.where(real, jnp.exp(jnp.where(real, logits - top, 0.0)), 0.0)
        likelihood = powers / jnp.sum(powers, axis=1, keepdims=True)
        label = column_of(labels[half : half + 1, :]).astype(jnp.int32)
        onehot = jnp.where(columns == label, 1.0, 0.0)
        chosen = column_of(mask[half : half + 1, :]) * scale
        slopes[2 * rep + half] = pack((likelihood - onehot) * chosen)
        for step in range(1, REP):
            slope_copy(half, lax.rem(rep + step, REP), rep).start()
        return logits

    low_logits = classes(0)
    high_logits = classes(1)
    logits_out[:, :TILE] = low_logits.T[:CLASSES]
    logits_out[:, TILE:] = high_logits.T[:CLASSES]
    second_scatter.drain()

    def slope_waits(step, carry):
        other = lax.rem(rep + step, REP)
        for half in range(2):
            copy = remote(
                slopes.at[2 * rep + half],
                slopes.at[2 * other + half],
                slope_send.at[half, other],
                slope_arrive.at[half, other],
                (other, blk),
            )
            copy.wait_recv()
            copy.wait_send()
        return carry

    lax.fori_loop(1, REP, slope_waits, 0)

    def widen(index, carry):
        wide_slopes[index] = unpack(slopes[index])
        return carry

    lax.fori_loop(0, 2 * REP, widen, 0, unroll=4)

    def back_products(section):
        def some(group, carry):
            made = []
            for inner in range(4):
                slot = group * 4 + inner
                made.append(
                    lax.dot_general(
                        tiles[section * SLOTS + slot],
                        wide_slopes[table[ROW + section, slot]],
                        (((0,), (0,)), ((), ())),
                        preferred_element_type=F32,
                    )
                )
            for inner in range(4):
                slot = group * 4 + inner
                running[section * SLOTS + slot] = (
                    made[inner] + running[table[BACK_PREVIOUS + section, slot]]
                )
            return carry

        lax.fori_loop(0, SLOTS // 4, some, 0, unroll=2)

        def gather(piece, carry):
            for half in range(2):
                back_rows[section * SLOTS + half * REP + piece] = running[
                    table[BACK_LAST + section, 2 * piece + half]
                ].astype(BF16)
            return carry

        lax.fori_loop(0, REP, gather, 0, unroll=2)

    in_sum[...] = jnp.zeros_like(in_sum)
    out_sum[...] = jnp.zeros_like(out_sum)

    def terms(section):
        for half in range(2):
            inside = pl.ds(section * SLOTS + half * REP, REP)
            back = back_rows[inside].reshape(REP * TILE, WIDE)
            active = dense[inside].reshape(REP * TILE, WIDE)
            z_rows = second_sections[section][half * REP : (half + 1) * REP].reshape(
                REP * TILE, LANES
            )
            out_sum[...] += lax.dot_general(
                back, active, (((0,), (0,)), ((), ())), preferred_element_type=F32
            )
            hidden_rows = jnp.dot(back, wide_out[...], preferred_element_type=F32)
            pre_slope = jnp.where(
                active.astype(F32) > 0.0, hidden_rows * F32(KEEP), 0.0
            ).astype(BF16)
            in_sum[...] += lax.dot_general(
                z_rows, pre_slope, (((0,), (0,)), ((), ())), preferred_element_type=F32
            )

    for section in range(SEC):
        back_products(section)
        terms(section)
    joined = jnp.concatenate([in_sum[...], out_sum[...]], axis=0)
    for index in range(CREW):
        row = index % (CREW // 2) * CHUNK
        lane = index // (CREW // 2) * LANES
        pieces[index] = joined[row : row + CHUNK, lane : lane + LANES].astype(BF16)
    me, depth = spot.member, spot.depth

    def reduce_copy(other, lands):
        return remote(
            pieces.at[other],
            pieces_in.at[lands],
            b_send.at[other],
            b_arrive.at[lands],
            spot.crew(other),
        )

    def gather_copy(other, lands):
        return remote(
            full.at[me], full.at[lands], d_send.at[other], d_arrive.at[lands], spot.crew(other)
        )

    def start_all(copy):
        def one(step, carry):
            copy(lax.rem(me + step, CREW), me).start()
            return carry

        lax.fori_loop(1, CREW, one, 0)

    def wait_all(copy):
        def one(step, carry):
            other = lax.rem(me + step, CREW)
            both = copy(other, other)
            both.wait_recv()
            both.wait_send()
            return carry

        lax.fori_loop(1, CREW, one, 0)

    start_all(reduce_copy)
    pieces_in[me] = pieces[me]
    wait_all(reduce_copy)
    total = pieces_in[0].astype(F32)
    for index in range(1, CREW):
        total = total + pieces_in[index].astype(F32)
    depth_in[depth] = total
    for step in range(1, DEPTH):
        remote(
            depth_in.at[depth],
            depth_in.at[depth],
            c_send.at[step],
            c_arrive.at[depth],
            spot.line(step),
        ).start()
    for step in range(1, DEPTH):
        other = lax.rem(depth + step, DEPTH)
        copy = remote(
            depth_in.at[depth],
            depth_in.at[other],
            c_send.at[step],
            c_arrive.at[other],
            spot.line(step),
        )
        copy.wait_recv()
        copy.wait_send()
    total = depth_in[0]
    for index in range(1, DEPTH):
        total = total + depth_in[index]
    full[me] = total.astype(BF16)
    start_all(gather_copy)
    wait_all(gather_copy)


def result_kernel(in_rows, logits, full, logits_out, grad_in, grad_out):
    logits_out[:, 0, :] = logits[...]
    joined = jnp.concatenate(
        [
            jnp.concatenate(
                [full[start + index].astype(F32) for index in range(CREW // 2)], axis=0
            )
            for start in (0, CREW // 2)
        ],
        axis=1,
    )
    grad_in[...] = joined[:in_rows]
    grad_out[...] = joined[in_rows : in_rows + CLASSES]


def fill_tables(place, count, out):
    slots = lax.broadcasted_iota(jnp.int32, (SLOTS, SLOTS), 1)
    others = lax.broadcasted_iota(jnp.int32, (SLOTS, SLOTS), 0)
    before = others < slots

    def turned(line):
        flat = jnp.broadcast_to(line.astype(F32), (SLOTS, SLOTS))
        column = jnp.sum(jnp.where(slots == others, flat, 0.0), axis=1, keepdims=True)
        return column.astype(jnp.int32)

    def top(match, entries):
        return jnp.max(jnp.where(match, entries, -1), axis=0, keepdims=True)

    def put(row, values):
        out[row : row + 1, :SLOTS] = values

    def settled(values):
        return jnp.where(values < 0, NONE, values)

    rows, columns, row_turned, column_turned, live = [], [], [], [], []
    for section in range(SEC):
        line = place[section : section + 1, :]
        rows.append(jnp.right_shift(line, 4))
        columns.append(jnp.bitwise_and(line, SLOTS - 1))
        row_turned.append(turned(rows[section]))
        column_turned.append(turned(columns[section]))
        live.append(others < count[section])
    numbers = slots[:1]
    last = jnp.full((1, SLOTS), -1, jnp.int32)
    for section in range(SEC):
        turn = FORWARD_ORDER.index(section)
        entries = others + turn * SLOTS
        latest = jnp.full((1, SLOTS), -1, jnp.int32)
        for earlier in FORWARD_ORDER[: turn + 1]:
            match = (row_turned[earlier] == rows[section]) & live[earlier]
            if earlier == section:
                match = match & before
            latest = jnp.maximum(
                latest, top(match, others + FORWARD_ORDER.index(earlier) * SLOTS)
            )
        last = jnp.maximum(last, top((row_turned[section] == numbers) & live[section], entries))
        put(SOURCE + section, jnp.bitwise_and(columns[section], 1) * REP + jnp.right_shift(columns[section], 1))
        put(PREVIOUS + section, settled(latest))
        put(ROW + section, rows[section])
        own = others + section * SLOTS
        match = (column_turned[section] == columns[section]) & live[section]
        put(BACK_PREVIOUS + section, settled(top(match & before, own)))
        match = (column_turned[section] == numbers) & live[section]
        put(BACK_LAST + section, settled(top(match, own)))
    put(LAST, settled(last))


def on_device(
    features,
    node_ids,
    labels,
    train_mask,
    tile_values,
    tile_place,
    tile_count,
    weight_in,
    weight_out,
    class_bias,
):
    width = features.shape[-1]
    own_rows = features.shape[1]
    scale = 1.0 / math.sqrt(own_rows * REP * BLK)
    shape = jax.ShapeDtypeStruct
    dma = pltpu.SemaphoreType.DMA
    vmem = pltpu.VMEM
    anywhere = pl.BlockSpec(memory_space=pl.ANY)
    logits, full = pl.pallas_call(
        lambda *refs: step_kernel(scale, *refs),
        out_shape=(shape((CLASSES, own_rows), F32), shape((CREW, CHUNK, LANES), BF16)),
        in_specs=[
            pl.BlockSpec(memory_space=pltpu.SMEM),
            whole(),
            anywhere,
            whole(),
            whole(),
            whole(),
            anywhere,
            anywhere,
            anywhere,
            whole(),
        ],
        out_specs=[whole()] * 2,
        scratch_shapes=[
            vmem((2, TILE, width), BF16),
            vmem((NONE, TILE, TILE), BF16),
            vmem((width, WIDE), BF16),
            vmem((CLASSES, WIDE), BF16),
            dma((5,)),
            vmem((24, LANES), jnp.int32),
            pltpu.SMEM((24, LANES), jnp.int32),
            vmem((WIDE, WIDE), BF16),
            vmem((1, WIDE), F32),
            vmem((NONE + 1, TILE, WIDE), F32),
            vmem((2, CODED, LANES), BF16),
            vmem((2, TILE, LANES), BF16),
            vmem((NONE, TILE, WIDE), BF16),
            vmem((NONE, TILE, WIDE), BF16),
            vmem((NONE, TILE, WIDE), BF16),
            vmem((width, WIDE), F32),
            vmem((WIDE, WIDE), F32),
            vmem((2 * REP, PACKED, LANES), BF16),
            vmem((2 * REP, TILE, WIDE), BF16),
            dma((2, REP)),
            dma((2, REP)),
            vmem((DEPTH, CHUNK, LANES), F32),
            vmem((CREW, CHUNK, LANES), BF16),
            vmem((CREW, CHUNK, LANES), BF16),
            dma((CREW,)),
            dma((CREW,)),
            dma((DEPTH,)),
            dma((DEPTH,)),
            dma((CREW,)),
            dma((CREW,)),
            *spread_scratch(CODED),
            *spread_scratch(TILE),
            *scatter_scratch(2, TILE, LANES, F32),
            *scatter_scratch(2, PACKED, LANES, BF16),
        ],
        compiler_params=pltpu.CompilerParams(
            collective_id=0, has_side_effects=True, vmem_limit_bytes=VMEM_LIMIT
        ),
        name="training_step",
    )(
        tile_count.reshape(SEC),
        tile_place.reshape(SEC, SLOTS),
        features.reshape(2, TILE, width),
        node_ids.reshape(2, TILE),
        labels.reshape(2, TILE),
        train_mask.reshape(2, TILE),
        tile_values.reshape(NONE, TILE, TILE),
        weight_in,
        weight_out.T,
        class_bias.reshape(1, CLASSES),
    )
    logits, grad_in, grad_out = pl.pallas_call(
        lambda *refs: result_kernel(width, *refs),
        out_shape=(
            shape((CLASSES, 1, own_rows), F32),
            shape((width, WIDE), F32),
            shape((CLASSES, WIDE), F32),
        ),
        in_specs=[whole()] * 2,
        out_specs=[whole()] * 3,
        name="results",
    )(logits, full)
    return (logits.transpose(1, 2, 0), grad_in, grad_out.T)


def solution(mesh):
    placed = (
        P("blk", "rep", None),
        P("blk", "rep"),
        P("blk", "rep"),
        P("blk", "rep"),
        P("blk", "rep", None, None, None, None),
        P("blk", "rep", None, None),
        P("blk", "rep", None),
        P(),
        P(),
        P(),
    )
    return jax.shard_map(
        on_device,
        mesh=mesh,
        in_specs=placed,
        out_specs=(P("blk", "rep", None), P(), P()),
        check_vma=False,
    )
```

```python
import math

import jax
import jax.numpy as jnp
from jax import lax
from jax.experimental import pallas as pl
from jax.experimental.pallas import tpu as pltpu
from jax.sharding import PartitionSpec as P

MESH = pl.DeviceIdType.MESH
F32 = jnp.float32
BF16 = jnp.bfloat16
REP = 8
BLK = 32
SEC = 4
TILE = 128
SLOTS = 16
WIDE = 256
CLASSES = 172
LANES = 128
PACKED = 192
DEPTH = 8
NONE = SEC * SLOTS
FORWARD_ORDER = (1, 2, 0, 3)
CODED = 144
CREW = 32
KEEP = 4.0 / 3.0
CHUNK = 24
SOURCE, PREVIOUS, ROW, BACK_PREVIOUS, BACK_LAST, LAST = 0, 4, 8, 12, 16, 20
VMEM_LIMIT = 60 << 20


def whole():
    return pl.BlockSpec(memory_space=pltpu.VMEM)


def remote(source, target, send, arrive, device):
    return pltpu.make_async_remote_copy(
        src_ref=source,
        dst_ref=target,
        send_sem=send,
        recv_sem=arrive,
        device_id=device,
        device_id_type=MESH,
    )


def landed(target, send, arrive, device):
    remote(target, target, send, arrive, device).wait_recv()


def greet(device):
    pl.semaphore_signal(
        pltpu.get_barrier_semaphore(), inc=1, device_id=device, device_id_type=MESH
    )


def blk_of(part, depth, core):
    return (part * (BLK // 4) + depth) * 2 + core


class Spot:
    def __init__(self):
        self.rep = lax.axis_index("rep")
        self.blk = lax.axis_index("blk")
        self.core = lax.rem(self.blk, 2)
        self.depth = lax.rem(self.blk // 2, DEPTH)
        self.part = self.blk // 16
        self.here = (self.rep, self.blk)
        self.up = (self.rep, lax.rem(self.blk + 1, BLK))
        self.down = (self.rep, lax.rem(self.blk + BLK - 1, BLK))
        low_block = lax.rem(self.blk - SEC * self.rep + BLK, BLK)
        high_block = lax.rem(self.blk - SEC * self.rep - (SEC - 1) + 2 * BLK, BLK)
        self.low_relay = (low_block // 16) * 16 + lax.rem(self.blk, 16)
        self.high_relay = blk_of(high_block // 16, self.depth, 1 - self.core)
        self.own_relay = self.low_relay == self.blk
        self.member = self.rep * 4 + self.part * 2 + self.core

    def line(self, step):
        return (self.rep, blk_of(self.part, lax.rem(self.depth + step + DEPTH, DEPTH), self.core))

    def crew(self, index):
        corner = lax.rem(index, 4)
        return (index // 4, blk_of(corner // 2, self.depth, lax.rem(corner, 2)))

    def local(self, piece):
        return jnp.logical_and(self.own_relay, piece == self.rep)

    def targets(self, half, slot):
        offset = 2 * slot + half * (1 + self.core)
        source = blk_of(self.part, lax.rem(self.depth - offset + 2 * DEPTH, DEPTH), self.core)
        for other in (slot, slot + 4):
            yield other, (other, lax.rem(source + (SEC - 1) * half + SEC * other, BLK))


def greet_everyone(spot):
    for step in range(1, CREW):
        greet(spot.crew(lax.rem(spot.member + step, CREW)))
    for step in range(1, DEPTH):
        greet(spot.line(step))
    for other in range(REP):
        @pl.when(jnp.logical_not(spot.local(other)))
        def _(other=other):
            greet((other, spot.low_relay))

        greet((other, spot.high_relay))
    greet(spot.up)
    greet(spot.down)
    count = (CREW - 1) + (DEPTH - 1) + 2 * REP + 2
    return count - jnp.where(spot.own_relay, 1, 0)


class Spread:
    def __init__(self, spot, shard, sections, relay, line_send, line_arrive, send, chain_send, arrive):
        self.spot, self.shard, self.sections, self.relay = spot, shard, sections, relay
        self.line_send, self.line_arrive, self.send = line_send, line_arrive, send
        self.chain_send, self.arrive = chain_send, arrive
        self.dummy = chain_send.at[0, 0, 0]

    def line_copy(self, half, source, slot, step):
        return remote(
            source,
            self.relay.at[half, slot],
            self.line_send.at[half, slot],
            self.line_arrive.at[half, slot],
            self.spot.line(step),
        )

    def line_wait(self, half, slot):
        landed(
            self.relay.at[half, slot], self.dummy, self.line_arrive.at[half, slot], self.spot.here
        )

    def hand_on(self, half, slot, source):
        spot = self.spot
        section = (SEC - 1) * half
        for other, device in spot.targets(half, slot):
            copy = remote(
                source,
                self.sections[section].at[half * REP + spot.rep],
                self.send.at[half, other],
                self.arrive.at[section, half, spot.rep],
                device,
            )
            if half == 0:
                same = jnp.logical_and(other == spot.rep, device[1] == spot.blk)

                @pl.when(same)
                def _(source=source):
                    self.sections[0][spot.rep] = source[...]

                @pl.when(jnp.logical_not(same))
                def _(copy=copy):
                    copy.start()
            else:
                copy.start()

    def start_low(self):
        self.low = [
            self.line_copy(0, self.shard.at[0], 1, 2),
            self.line_copy(0, self.shard.at[0], 3, -2),
        ]
        for copy in self.low:
            copy.start()
        self.hand_on(0, 0, self.shard.at[0])

    def start_high(self):
        core = self.spot.core
        self.high = [
            self.line_copy(1, self.shard.at[1], 0, 1 + core),
            self.line_copy(1, self.shard.at[1], 3 - core, -1 - core),
        ]
        for copy in self.high:
            copy.start()

        @pl.when(core == 1)
        def _():
            self.hand_on(1, 3, self.shard.at[1])

    def pass_on(self):
        core, relay = self.spot.core, self.relay
        self.line_wait(0, 1)
        self.onward = self.line_copy(0, relay.at[0, 1], 2, 2)
        self.onward.start()
        self.hand_on(0, 1, relay.at[0, 1])
        self.line_wait(0, 3)
        self.hand_on(0, 3, relay.at[0, 3])
        self.line_wait(1, 3 - core)
        self.back = self.line_copy(1, relay.at[1, 3 - core], 2 - core, -2)
        self.back.start()
        self.line_wait(1, 0)
        self.forth = self.line_copy(1, relay.at[1, 0], 1, 2)

        @pl.when(core == 0)
        def _():
            self.forth.start()

        self.hand_on(1, 0, relay.at[1, 0])
        self.hand_on(1, 3 - core, relay.at[1, 3 - core])
        self.line_wait(0, 2)
        self.hand_on(0, 2, relay.at[0, 2])
        self.line_wait(1, 2 - core)
        self.hand_on(1, 2 - core, relay.at[1, 2 - core])

        @pl.when(core == 0)
        def _():
            self.line_wait(1, 1)
            self.hand_on(1, 1, relay.at[1, 1])

    def arrived(self, section, half, piece):
        landed(
            self.sections[section].at[half * REP + piece],
            self.dummy,
            self.arrive.at[section, half, piece],
            self.spot.here,
        )

    def chains(self, meanwhile=None):
        spot = self.spot
        for section in range(SEC - 1):
            other_section = SEC - 1 - section

            def hop(step, carry, section=section, other_section=other_section):
                pair = step // 2
                far = pair + pair // 2 - 2 * (pair // 3)
                piece = 2 * lax.rem(spot.rep // 2 + far, 4) + lax.rem(spot.rep + step, 2)
                if section == 0:
                    @pl.when(jnp.logical_not(spot.local(piece)))
                    def _():
                        self.arrived(section, 0, piece)
                else:
                    self.arrived(section, 0, piece)
                remote(
                    self.sections[section].at[piece],
                    self.sections[section + 1].at[piece],
                    self.chain_send.at[0, section, piece],
                    self.arrive.at[section + 1, 0, piece],
                    spot.up,
                ).start()
                self.arrived(other_section, 1, piece)
                remote(
                    self.sections[other_section].at[REP + piece],
                    self.sections[other_section - 1].at[REP + piece],
                    self.chain_send.at[1, section, piece],
                    self.arrive.at[other_section - 1, 1, piece],
                    spot.down,
                ).start()
                return carry

            lax.fori_loop(0, REP, hop, 0)
            if meanwhile is not None:
                meanwhile(section)

    def last_arrivals(self):
        def finish(piece, carry):
            self.arrived(SEC - 1, 0, piece)
            self.arrived(0, 1, piece)
            return carry

        lax.fori_loop(0, REP, finish, 0)

    def drain(self):
        spot = self.spot
        sample = self.shard.at[0]

        def sent(semaphore):
            remote(sample, sample, semaphore, self.arrive.at[0, 0, 0], spot.here).wait_send()

        def body(piece, carry):
            for direction in range(2):
                for section in range(SEC - 1):
                    sent(self.chain_send.at[direction, section, piece])

            @pl.when(jnp.logical_not(spot.local(piece)))
            def _():
                sent(self.send.at[0, piece])

            sent(self.send.at[1, piece])
            return carry

        lax.fori_loop(0, REP, body, 0)
        for copy in (*self.low, *self.high, self.back, self.onward):
            copy.wait_send()

        @pl.when(spot.core == 0)
        def _():
            self.forth.wait_send()


def spread_scratch(height):
    dma = pltpu.SemaphoreType.DMA
    return [
        *[pltpu.VMEM((2 * REP, height, LANES), BF16)] * SEC,
        pltpu.VMEM((2, 4, height, LANES), BF16),
        dma((2, 4)),
        dma((2, 4)),
        dma((2, REP)),
        dma((2, SEC - 1, REP)),
        dma((SEC, 2, REP)),
    ]


class Scatter:
    def __init__(self, spot, pieces, landing, send, arrive):
        self.spot, self.pieces, self.landing = spot, pieces, landing
        self.send, self.arrive = send, arrive

    def copy(self, half, other, lands):
        return remote(
            self.pieces.at[half, other],
            self.landing.at[half, lands],
            self.send.at[half, other],
            self.arrive.at[half, lands],
            (other, self.spot.blk),
        )

    def put(self, half, make):
        rep = self.spot.rep

        def one(step, carry):
            other = lax.rem(rep + 1 + step, REP)
            self.pieces[half, other] = make(other)
            self.copy(half, other, rep).start()
            return carry

        lax.fori_loop(0, REP - 1, one, 0)
        self.landing[half, rep] = make(rep)

    def total(self, half):
        rep = self.spot.rep

        def one(step, carry):
            other = lax.rem(rep + 1 + step, REP)
            self.copy(half, other, other).wait_recv()
            return carry

        lax.fori_loop(0, REP - 1, one, 0)
        total = self.landing[half, 0].astype(F32)
        for index in range(1, REP):
            total = total + self.landing[half, index].astype(F32)
        return total

    def drain(self):
        def one(step, carry):
            other = lax.rem(self.spot.rep + 1 + step, REP)
            for half in range(self.pieces.shape[0]):
                self.copy(half, other, other).wait_send()
            return carry

        lax.fori_loop(0, REP - 1, one, 0)


def scatter_scratch(halves, height, width, dtype):
    dma = pltpu.SemaphoreType.DMA
    return [
        pltpu.VMEM((halves, REP, height, width), dtype),
        pltpu.VMEM((halves, REP, height, width), dtype),
        dma((halves, REP)),
        dma((halves, REP)),
    ]


def pack(values):
    half = TILE // 2
    lanes = lax.broadcasted_iota(jnp.int32, (half, LANES), 1)
    rest = jnp.where(
        lanes < half,
        values[:half, LANES:],
        pltpu.roll(values[half:, LANES:], half, 1),
    )
    return jnp.concatenate([values[:, :LANES], rest], axis=0).astype(BF16)


def unpack(packed):
    half = TILE // 2
    rest = packed[TILE:]
    turned = jnp.concatenate([rest[:, half:], rest[:, :half]], axis=1)
    return jnp.concatenate(
        [packed[:TILE], jnp.concatenate([rest, turned], axis=0)], axis=1
    )


def is_kept(ids):
    columns = lax.broadcasted_iota(jnp.int32, (1, WIDE), 1)
    mixed = (ids * 73244475 + 12345) + columns * 19349663
    mixed = jnp.bitwise_and(mixed ^ jnp.right_shift(mixed, 15), 32767) * (40503 % 32768)
    mixed = mixed ^ jnp.right_shift(mixed, 13)
    return jnp.bitwise_and(mixed, 3) != 0


def column_of(row):
    lanes = lax.broadcasted_iota(jnp.int32, (TILE, LANES), 1)
    rows = lax.broadcasted_iota(jnp.int32, (TILE, LANES), 0)
    spread_out = jnp.broadcast_to(row.astype(F32), (TILE, LANES))
    return jnp.sum(jnp.where(lanes == rows, spread_out, 0.0), axis=1, keepdims=True)


def step_kernel(
    scale,
    count,
    place,
    x_hbm,
    ids,
    labels,
    mask,
    tiles_hbm,
    weight_in_hbm,
    weight_out_hbm,
    bias,
    logits_out,
    full,
    x,
    tiles,
    weight_in,
    weight_out,
    input_sems,
    table_values,
    table,
    wide_out,
    wide_bias,
    running,
    coded,
    shard,
    kept,
    dense,
    back_rows,
    in_sum,
    out_sum,
    slopes,
    wide_slopes,
    slope_send,
    slope_arrive,
    depth_in,
    pieces,
    pieces_in,
    b_send,
    b_arrive,
    c_send,
    c_arrive,
    d_send,
    d_arrive,
    *rest,
):
    rest = list(rest)

    def take(count):
        taken = rest[:count]
        del rest[:count]
        return taken

    spot = Spot()
    rep, blk = spot.rep, spot.blk
    first_sections = take(SEC)
    first_spread = Spread(spot, coded, first_sections, *take(6))
    second_sections = take(SEC)
    second_spread = Spread(spot, shard, second_sections, *take(6))
    first_scatter = Scatter(spot, *take(4))
    second_scatter = Scatter(spot, *take(4))
    waits = greet_everyone(spot)
    input_copies = [
        pltpu.make_async_copy(source, target, input_sems.at[index])
        for index, (source, target) in enumerate(
            (
                (x_hbm, x),
                (weight_out_hbm, weight_out),
                (weight_in_hbm, weight_in),
                (tiles_hbm, tiles),
            )
        )
    ]
    for copy in input_copies:
        copy.start()
    table_copy = pltpu.make_async_copy(table_values, table, input_sems.at[len(input_copies)])

    def prepare(section):
        if section == 0:
            fill_tables(place, count, table_values)
            table_copy.start()
        elif section == 1:
            running[NONE] = jnp.zeros((TILE, WIDE), F32)
            wide_out[...] = jnp.zeros_like(wide_out)
            wide_bias[...] = jnp.zeros_like(wide_bias)
            wide_bias[:, :CLASSES] = bias[...]
            input_copies[1].wait()
            wide_out[:CLASSES, :] = weight_out[...]
            input_copies[2].wait()
            input_copies[3].wait()
            table_copy.wait()

    input_copies[0].wait()
    code_rows = lax.broadcasted_iota(jnp.int32, (CODED - TILE, LANES), 0)
    for half in range(2):
        coded[half, :TILE] = x[half]
        number = ids[half : half + 1, :]
        code = jnp.zeros((CODED - TILE, LANES), F32)
        for byte in range(3):
            value = jnp.bitwise_and(jnp.right_shift(number, 8 * byte), 255).astype(F32)
            code = jnp.where(code_rows == byte, jnp.broadcast_to(value, code.shape), code)
        coded[half, TILE:] = code.astype(BF16)
    pl.semaphore_wait(pltpu.get_barrier_semaphore(), waits)

    def products(section, width, source_of):
        place = FORWARD_ORDER.index(section)

        def some(group, carry):
            made = []
            for inner in range(4):
                slot = group * 4 + inner
                made.append(
                    jnp.dot(
                        tiles[section * SLOTS + slot],
                        source_of(table[SOURCE + section, slot]),
                        preferred_element_type=F32,
                    )
                )
            for inner in range(4):
                slot = group * 4 + inner
                running[place * SLOTS + slot, :, :width] = (
                    made[inner] + running[table[PREVIOUS + section, slot], :, :width]
                )
            return carry

        lax.fori_loop(0, SLOTS // 4, some, 0, unroll=2)

    def first_products(section):
        products(section, LANES, lambda index: first_sections[section][index, :TILE])

    def second_products(section):
        products(section, WIDE, lambda index: dense[section * SLOTS + index])

    def first_sum(half):
        return lambda other: running[table[LAST, 2 * other + half], :, :LANES]

    def second_sum(half):
        def one(other):
            part = running[table[LAST, 2 * other + half]].astype(BF16)
            return pack(
                lax.dot_general(
                    part, wide_out[...], (((1,), (1,)), ((), ())), preferred_element_type=F32
                )
            )

        return one

    def find_kept(section):
        lanes = lax.broadcasted_iota(jnp.int32, (TILE, LANES), 1)
        rows = lax.broadcasted_iota(jnp.int32, (TILE, LANES), 0)
        unit = jnp.where(lanes == rows, 1.0, 0.0).astype(BF16)

        def one(index, carry):
            code = lax.dot_general(
                unit,
                first_sections[section][index, TILE:],
                (((1,), (1,)), ((), ())),
                preferred_element_type=F32,
            )
            number = code[:, 0:1] + 256.0 * code[:, 1:2] + 65536.0 * code[:, 2:3]
            kept[section * SLOTS + index] = jnp.where(
                is_kept(number.astype(jnp.int32)), 1.0, 0.0
            ).astype(BF16)
            return carry

        lax.fori_loop(0, SLOTS, one, 0, unroll=4)

    def activate(section, half):
        def one(index, carry):
            pre_act = jnp.dot(
                second_sections[section][index], weight_in[...], preferred_element_type=F32
            )
            active = jnp.maximum(pre_act, 0.0) * F32(KEEP)
            flag = kept[section * SLOTS + index].astype(F32)
            dense[section * SLOTS + index] = jnp.where(flag > 0.0, active, 0.0).astype(BF16)
            return carry

        lax.fori_loop(half * REP, (half + 1) * REP, one, 0, unroll=4)

    def activate_arrived(section):
        activate(section, 0)
        activate(SEC - 1 - section, 1)

    first_spread.start_low()
    first_spread.start_high()
    first_spread.pass_on()
    first_spread.chains(prepare)
    first_products(1)
    first_products(2)
    first_spread.last_arrivals()
    first_products(0)
    first_products(3)
    first_scatter.put(0, first_sum(0))
    first_scatter.put(1, first_sum(1))
    for section in range(SEC):
        find_kept(section)
    shard[0] = first_scatter.total(0).astype(BF16)
    second_spread.start_low()
    shard[1] = first_scatter.total(1).astype(BF16)
    second_spread.start_high()
    second_spread.pass_on()
    second_spread.chains(activate_arrived)
    second_products(1)
    second_products(2)
    second_spread.last_arrivals()
    activate_arrived(SEC - 1)
    second_products(0)
    second_products(3)
    second_scatter.put(0, second_sum(0))
    second_scatter.put(1, second_sum(1))
    first_spread.drain()
    second_spread.drain()
    first_scatter.drain()

    def slope_copy(half, other, lands):
        return remote(
            slopes.at[2 * rep + half],
            slopes.at[2 * lands + half],
            slope_send.at[half, other],
            slope_arrive.at[half, lands],
            (other, blk),
        )

    def classes(half):
        logits = unpack(second_scatter.total(half)) + wide_bias[...]
        columns = lax.broadcasted_iota(jnp.int32, logits.shape, 1)
        real = columns < CLASSES
        top = jnp.max(jnp.where(real, logits, -jnp.inf), axis=1, keepdims=True)
        powers = jnp.where(real, jnp.exp(jnp.where(real, logits - top, 0.0)), 0.0)
        likelihood = powers / jnp.sum(powers, axis=1, keepdims=True)
        label = column_of(labels[half : half + 1, :]).astype(jnp.int32)
        onehot = jnp.where(columns == label, 1.0, 0.0)
        chosen = column_of(mask[half : half + 1, :]) * scale
        slopes[2 * rep + half] = pack((likelihood - onehot) * chosen)
        for step in range(1, REP):
            slope_copy(half, lax.rem(rep + step, REP), rep).start()
        return logits

    low_logits = classes(0)
    high_logits = classes(1)
    logits_out[:, :TILE] = low_logits.T[:CLASSES]
    logits_out[:, TILE:] = high_logits.T[:CLASSES]
    second_scatter.drain()

    def slope_waits(step, carry):
        other = lax.rem(rep + step, REP)
        for half in range(2):
            copy = remote(
                slopes.at[2 * rep + half],
                slopes.at[2 * other + half],
                slope_send.at[half, other],
                slope_arrive.at[half, other],
                (other, blk),
            )
            copy.wait_recv()
            copy.wait_send()
        return carry

    lax.fori_loop(1, REP, slope_waits, 0)

    def widen(index, carry):
        wide_slopes[index] = unpack(slopes[index])
        return carry

    lax.fori_loop(0, 2 * REP, widen, 0, unroll=4)

    def back_products(section):
        def some(group, carry):
            made = []
            for inner in range(4):
                slot = group * 4 + inner
                made.append(
                    lax.dot_general(
                        tiles[section * SLOTS + slot],
                        wide_slopes[table[ROW + section, slot]],
                        (((0,), (0,)), ((), ())),
                        preferred_element_type=F32,
                    )
                )
            for inner in range(4):
                slot = group * 4 + inner
                running[section * SLOTS + slot] = (
                    made[inner] + running[table[BACK_PREVIOUS + section, slot]]
                )
            return carry

        lax.fori_loop(0, SLOTS // 4, some, 0, unroll=2)

        def gather(piece, carry):
            for half in range(2):
                back_rows[section * SLOTS + half * REP + piece] = running[
                    table[BACK_LAST + section, 2 * piece + half]
                ].astype(BF16)
            return carry

        lax.fori_loop(0, REP, gather, 0, unroll=2)

    in_sum[...] = jnp.zeros_like(in_sum)
    out_sum[...] = jnp.zeros_like(out_sum)

    def terms(section):
        for half in range(2):
            inside = pl.ds(section * SLOTS + half * REP, REP)
            back = back_rows[inside].reshape(REP * TILE, WIDE)
            active = dense[inside].reshape(REP * TILE, WIDE)
            z_rows = second_sections[section][half * REP : (half + 1) * REP].reshape(
                REP * TILE, LANES
            )
            out_sum[...] += lax.dot_general(
                back, active, (((0,), (0,)), ((), ())), preferred_element_type=F32
            )
            hidden_rows = jnp.dot(back, wide_out[...], preferred_element_type=F32)
            pre_slope = jnp.where(
                active.astype(F32) > 0.0, hidden_rows * F32(KEEP), 0.0
            ).astype(BF16)
            in_sum[...] += lax.dot_general(
                z_rows, pre_slope, (((0,), (0,)), ((), ())), preferred_element_type=F32
            )

    for section in range(SEC):
        back_products(section)
        terms(section)
    joined = jnp.concatenate([in_sum[...], out_sum[...]], axis=0)
    for index in range(CREW):
        row = index % (CREW // 2) * CHUNK
        lane = index // (CREW // 2) * LANES
        pieces[index] = joined[row : row + CHUNK, lane : lane + LANES].astype(BF16)
    me, depth = spot.member, spot.depth

    def reduce_copy(other, lands):
        return remote(
            pieces.at[other],
            pieces_in.at[lands],
            b_send.at[other],
            b_arrive.at[lands],
            spot.crew(other),
        )

    def gather_copy(other, lands):
        return remote(
            full.at[me], full.at[lands], d_send.at[other], d_arrive.at[lands], spot.crew(other)
        )

    def start_all(copy):
        def one(step, carry):
            copy(lax.rem(me + step, CREW), me).start()
            return carry

        lax.fori_loop(1, CREW, one, 0, unroll=8)

    def wait_all(copy):
        def one(step, carry):
            other = lax.rem(me + step, CREW)
            both = copy(other, other)
            both.wait_recv()
            both.wait_send()
            return carry

        lax.fori_loop(1, CREW, one, 0, unroll=8)

    start_all(reduce_copy)
    pieces_in[me] = pieces[me]
    wait_all(reduce_copy)
    total = pieces_in[0].astype(F32)
    for index in range(1, CREW):
        total = total + pieces_in[index].astype(F32)
    depth_in[depth] = total
    for step in range(1, DEPTH):
        remote(
            depth_in.at[depth],
            depth_in.at[depth],
            c_send.at[step],
            c_arrive.at[depth],
            spot.line(step),
        ).start()
    for step in range(1, DEPTH):
        other = lax.rem(depth + step, DEPTH)
        copy = remote(
            depth_in.at[depth],
            depth_in.at[other],
            c_send.at[step],
            c_arrive.at[other],
            spot.line(step),
        )
        copy.wait_recv()
        copy.wait_send()
    total = depth_in[0]
    for index in range(1, DEPTH):
        total = total + depth_in[index]
    full[me] = total.astype(BF16)
    start_all(gather_copy)
    wait_all(gather_copy)


def result_kernel(in_rows, logits, full, logits_out, grad_in, grad_out):
    logits_out[:, 0, :] = logits[...]
    joined = jnp.concatenate(
        [
            jnp.concatenate(
                [full[start + index].astype(F32) for index in range(CREW // 2)], axis=0
            )
            for start in (0, CREW // 2)
        ],
        axis=1,
    )
    grad_in[...] = joined[:in_rows]
    grad_out[...] = joined[in_rows : in_rows + CLASSES]


def fill_tables(place, count, out):
    slots = lax.broadcasted_iota(jnp.int32, (SLOTS, SLOTS), 1)
    others = lax.broadcasted_iota(jnp.int32, (SLOTS, SLOTS), 0)
    before = others < slots

    def turned(line):
        flat = jnp.broadcast_to(line.astype(F32), (SLOTS, SLOTS))
        column = jnp.sum(jnp.where(slots == others, flat, 0.0), axis=1, keepdims=True)
        return column.astype(jnp.int32)

    def top(match, entries):
        return jnp.max(jnp.where(match, entries, -1), axis=0, keepdims=True)

    def put(row, values):
        out[row : row + 1, :SLOTS] = values

    def settled(values):
        return jnp.where(values < 0, NONE, values)

    rows, columns, row_turned, column_turned, live = [], [], [], [], []
    for section in range(SEC):
        line = place[section : section + 1, :]
        rows.append(jnp.right_shift(line, 4))
        columns.append(jnp.bitwise_and(line, SLOTS - 1))
        row_turned.append(turned(rows[section]))
        column_turned.append(turned(columns[section]))
        live.append(others < count[section])
    numbers = slots[:1]
    last = jnp.full((1, SLOTS), -1, jnp.int32)
    for section in range(SEC):
        turn = FORWARD_ORDER.index(section)
        entries = others + turn * SLOTS
        latest = jnp.full((1, SLOTS), -1, jnp.int32)
        for earlier in FORWARD_ORDER[: turn + 1]:
            match = (row_turned[earlier] == rows[section]) & live[earlier]
            if earlier == section:
                match = match & before
            latest = jnp.maximum(
                latest, top(match, others + FORWARD_ORDER.index(earlier) * SLOTS)
            )
        last = jnp.maximum(last, top((row_turned[section] == numbers) & live[section], entries))
        put(SOURCE + section, jnp.bitwise_and(columns[section], 1) * REP + jnp.right_shift(columns[section], 1))
        put(PREVIOUS + section, settled(latest))
        put(ROW + section, rows[section])
        own = others + section * SLOTS
        match = (column_turned[section] == columns[section]) & live[section]
        put(BACK_PREVIOUS + section, settled(top(match & before, own)))
        match = (column_turned[section] == numbers) & live[section]
        put(BACK_LAST + section, settled(top(match, own)))
    put(LAST, settled(last))


def on_device(
    features,
    node_ids,
    labels,
    train_mask,
    tile_values,
    tile_place,
    tile_count,
    weight_in,
    weight_out,
    class_bias,
):
    width = features.shape[-1]
    own_rows = features.shape[1]
    scale = 1.0 / math.sqrt(own_rows * REP * BLK)
    shape = jax.ShapeDtypeStruct
    dma = pltpu.SemaphoreType.DMA
    vmem = pltpu.VMEM
    anywhere = pl.BlockSpec(memory_space=pl.ANY)
    logits, full = pl.pallas_call(
        lambda *refs: step_kernel(scale, *refs),
        out_shape=(shape((CLASSES, own_rows), F32), shape((CREW, CHUNK, LANES), BF16)),
        in_specs=[
            pl.BlockSpec(memory_space=pltpu.SMEM),
            whole(),
            anywhere,
            whole(),
            whole(),
            whole(),
            anywhere,
            anywhere,
            anywhere,
            whole(),
        ],
        out_specs=[whole()] * 2,
        scratch_shapes=[
            vmem((2, TILE, width), BF16),
            vmem((NONE, TILE, TILE), BF16),
            vmem((width, WIDE), BF16),
            vmem((CLASSES, WIDE), BF16),
            dma((5,)),
            vmem((24, LANES), jnp.int32),
            pltpu.SMEM((24, LANES), jnp.int32),
            vmem((WIDE, WIDE), BF16),
            vmem((1, WIDE), F32),
            vmem((NONE + 1, TILE, WIDE), F32),
            vmem((2, CODED, LANES), BF16),
            vmem((2, TILE, LANES), BF16),
            vmem((NONE, TILE, WIDE), BF16),
            vmem((NONE, TILE, WIDE), BF16),
            vmem((NONE, TILE, WIDE), BF16),
            vmem((width, WIDE), F32),
            vmem((WIDE, WIDE), F32),
            vmem((2 * REP, PACKED, LANES), BF16),
            vmem((2 * REP, TILE, WIDE), BF16),
            dma((2, REP)),
            dma((2, REP)),
            vmem((DEPTH, CHUNK, LANES), F32),
            vmem((CREW, CHUNK, LANES), BF16),
            vmem((CREW, CHUNK, LANES), BF16),
            dma((CREW,)),
            dma((CREW,)),
            dma((DEPTH,)),
            dma((DEPTH,)),
            dma((CREW,)),
            dma((CREW,)),
            *spread_scratch(CODED),
            *spread_scratch(TILE),
            *scatter_scratch(2, TILE, LANES, F32),
            *scatter_scratch(2, PACKED, LANES, BF16),
        ],
        compiler_params=pltpu.CompilerParams(
            collective_id=0, has_side_effects=True, vmem_limit_bytes=VMEM_LIMIT
        ),
        name="training_step",
    )(
        tile_count.reshape(SEC),
        tile_place.reshape(SEC, SLOTS),
        features.reshape(2, TILE, width),
        node_ids.reshape(2, TILE),
        labels.reshape(2, TILE),
        train_mask.reshape(2, TILE),
        tile_values.reshape(NONE, TILE, TILE),
        weight_in,
        weight_out.T,
        class_bias.reshape(1, CLASSES),
    )
    logits, grad_in, grad_out = pl.pallas_call(
        lambda *refs: result_kernel(width, *refs),
        out_shape=(
            shape((CLASSES, 1, own_rows), F32),
            shape((width, WIDE), F32),
            shape((CLASSES, WIDE), F32),
        ),
        in_specs=[whole()] * 2,
        out_specs=[whole()] * 3,
        name="results",
    )(logits, full)
    return (logits.transpose(1, 2, 0), grad_in, grad_out.T)


def solution(mesh):
    placed = (
        P("blk", "rep", None),
        P("blk", "rep"),
        P("blk", "rep"),
        P("blk", "rep"),
        P("blk", "rep", None, None, None, None),
        P("blk", "rep", None, None),
        P("blk", "rep", None),
        P(),
        P(),
        P(),
    )
    return jax.shard_map(
        on_device,
        mesh=mesh,
        in_specs=placed,
        out_specs=(P("blk", "rep", None), P(), P()),
        check_vma=False,
    )
```

```python
import math

import jax
import jax.numpy as jnp
from jax import lax
from jax.experimental import pallas as pl
from jax.experimental.pallas import tpu as pltpu
from jax.sharding import PartitionSpec as P

MESH = pl.DeviceIdType.MESH
F32 = jnp.float32
BF16 = jnp.bfloat16
REP = 8
BLK = 32
SEC = 4
TILE = 128
SLOTS = 16
WIDE = 256
CLASSES = 172
LANES = 128
PACKED = 192
DEPTH = 8
NONE = SEC * SLOTS
FORWARD_ORDER = (1, 2, 0, 3)
CODED = 144
CREW = 32
KEEP = 4.0 / 3.0
CHUNK = 24
SOURCE, PREVIOUS, ROW, BACK_PREVIOUS, BACK_LAST, LAST = 0, 4, 8, 12, 16, 20
VMEM_LIMIT = 60 << 20


def whole():
    return pl.BlockSpec(memory_space=pltpu.VMEM)


def remote(source, target, send, arrive, device):
    return pltpu.make_async_remote_copy(
        src_ref=source,
        dst_ref=target,
        send_sem=send,
        recv_sem=arrive,
        device_id=device,
        device_id_type=MESH,
    )


def landed(target, send, arrive, device):
    remote(target, target, send, arrive, device).wait_recv()


def greet(device):
    pl.semaphore_signal(
        pltpu.get_barrier_semaphore(), inc=1, device_id=device, device_id_type=MESH
    )


def blk_of(part, depth, core):
    return (part * (BLK // 4) + depth) * 2 + core


class Spot:
    def __init__(self):
        self.rep = lax.axis_index("rep")
        self.blk = lax.axis_index("blk")
        self.core = lax.rem(self.blk, 2)
        self.depth = lax.rem(self.blk // 2, DEPTH)
        self.part = self.blk // 16
        self.here = (self.rep, self.blk)
        self.up = (self.rep, lax.rem(self.blk + 1, BLK))
        self.down = (self.rep, lax.rem(self.blk + BLK - 1, BLK))
        low_block = lax.rem(self.blk - SEC * self.rep + BLK, BLK)
        high_block = lax.rem(self.blk - SEC * self.rep - (SEC - 1) + 2 * BLK, BLK)
        self.low_relay = (low_block // 16) * 16 + lax.rem(self.blk, 16)
        self.high_relay = blk_of(high_block // 16, self.depth, 1 - self.core)
        self.own_relay = self.low_relay == self.blk
        self.member = self.rep * 4 + self.part * 2 + self.core

    def line(self, step):
        return (self.rep, blk_of(self.part, lax.rem(self.depth + step + DEPTH, DEPTH), self.core))

    def crew(self, index):
        corner = lax.rem(index, 4)
        return (index // 4, blk_of(corner // 2, self.depth, lax.rem(corner, 2)))

    def local(self, piece):
        return jnp.logical_and(self.own_relay, piece == self.rep)

    def targets(self, half, slot):
        offset = 2 * slot + half * (1 + self.core)
        source = blk_of(self.part, lax.rem(self.depth - offset + 2 * DEPTH, DEPTH), self.core)
        for other in (slot, slot + 4):
            yield other, (other, lax.rem(source + (SEC - 1) * half + SEC * other, BLK))


def greet_everyone(spot):
    for step in range(1, CREW):
        greet(spot.crew(lax.rem(spot.member + step, CREW)))
    for step in range(1, DEPTH):
        greet(spot.line(step))
    for other in range(REP):
        @pl.when(jnp.logical_not(spot.local(other)))
        def _(other=other):
            greet((other, spot.low_relay))

        greet((other, spot.high_relay))
    greet(spot.up)
    greet(spot.down)
    count = (CREW - 1) + (DEPTH - 1) + 2 * REP + 2
    return count - jnp.where(spot.own_relay, 1, 0)


class Spread:
    def __init__(self, spot, shard, sections, relay, line_send, line_arrive, send, chain_send, arrive):
        self.spot, self.shard, self.sections, self.relay = spot, shard, sections, relay
        self.line_send, self.line_arrive, self.send = line_send, line_arrive, send
        self.chain_send, self.arrive = chain_send, arrive
        self.dummy = chain_send.at[0, 0, 0]

    def line_copy(self, half, source, slot, step):
        return remote(
            source,
            self.relay.at[half, slot],
            self.line_send.at[half, slot],
            self.line_arrive.at[half, slot],
            self.spot.line(step),
        )

    def line_wait(self, half, slot):
        landed(
            self.relay.at[half, slot], self.dummy, self.line_arrive.at[half, slot], self.spot.here
        )

    def hand_on(self, half, slot, source):
        spot = self.spot
        section = (SEC - 1) * half
        for other, device in spot.targets(half, slot):
            copy = remote(
                source,
                self.sections[section].at[half * REP + spot.rep],
                self.send.at[half, other],
                self.arrive.at[section, half, spot.rep],
                device,
            )
            if half == 0:
                same = jnp.logical_and(other == spot.rep, device[1] == spot.blk)

                @pl.when(same)
                def _(source=source):
                    self.sections[0][spot.rep] = source[...]

                @pl.when(jnp.logical_not(same))
                def _(copy=copy):
                    copy.start()
            else:
                copy.start()

    def start_low(self):
        self.low = [
            self.line_copy(0, self.shard.at[0], 1, 2),
            self.line_copy(0, self.shard.at[0], 3, -2),
        ]
        for copy in self.low:
            copy.start()
        self.hand_on(0, 0, self.shard.at[0])

    def start_high(self):
        core = self.spot.core
        self.high = [
            self.line_copy(1, self.shard.at[1], 0, 1 + core),
            self.line_copy(1, self.shard.at[1], 3 - core, -1 - core),
        ]
        for copy in self.high:
            copy.start()

        @pl.when(core == 1)
        def _():
            self.hand_on(1, 3, self.shard.at[1])

    def pass_on(self):
        core, relay = self.spot.core, self.relay
        self.line_wait(0, 1)
        self.onward = self.line_copy(0, relay.at[0, 1], 2, 2)
        self.onward.start()
        self.hand_on(0, 1, relay.at[0, 1])
        self.line_wait(0, 3)
        self.hand_on(0, 3, relay.at[0, 3])
        self.line_wait(1, 3 - core)
        self.back = self.line_copy(1, relay.at[1, 3 - core], 2 - core, -2)
        self.back.start()
        self.line_wait(1, 0)
        self.forth = self.line_copy(1, relay.at[1, 0], 1, 2)

        @pl.when(core == 0)
        def _():
            self.forth.start()

        self.hand_on(1, 0, relay.at[1, 0])
        self.hand_on(1, 3 - core, relay.at[1, 3 - core])
        self.line_wait(0, 2)
        self.hand_on(0, 2, relay.at[0, 2])
        self.line_wait(1, 2 - core)
        self.hand_on(1, 2 - core, relay.at[1, 2 - core])

        @pl.when(core == 0)
        def _():
            self.line_wait(1, 1)
            self.hand_on(1, 1, relay.at[1, 1])

    def arrived(self, section, half, piece):
        landed(
            self.sections[section].at[half * REP + piece],
            self.dummy,
            self.arrive.at[section, half, piece],
            self.spot.here,
        )

    def chains(self, meanwhile=None):
        spot = self.spot
        for section in range(SEC - 1):
            other_section = SEC - 1 - section

            def hop(step, carry, section=section, other_section=other_section):
                pair = step // 2
                far = pair + pair // 2 - 2 * (pair // 3)
                piece = 2 * lax.rem(spot.rep // 2 + far, 4) + lax.rem(spot.rep + step, 2)
                if section == 0:
                    @pl.when(jnp.logical_not(spot.local(piece)))
                    def _():
                        self.arrived(section, 0, piece)
                else:
                    self.arrived(section, 0, piece)
                remote(
                    self.sections[section].at[piece],
                    self.sections[section + 1].at[piece],
                    self.chain_send.at[0, section, piece],
                    self.arrive.at[section + 1, 0, piece],
                    spot.up,
                ).start()
                self.arrived(other_section, 1, piece)
                remote(
                    self.sections[other_section].at[REP + piece],
                    self.sections[other_section - 1].at[REP + piece],
                    self.chain_send.at[1, section, piece],
                    self.arrive.at[other_section - 1, 1, piece],
                    spot.down,
                ).start()
                return carry

            lax.fori_loop(0, REP, hop, 0)
            if meanwhile is not None:
                meanwhile(section)

    def last_arrivals(self):
        def finish(piece, carry):
            self.arrived(SEC - 1, 0, piece)
            self.arrived(0, 1, piece)
            return carry

        lax.fori_loop(0, REP, finish, 0)

    def drain(self):
        spot = self.spot
        sample = self.shard.at[0]

        def sent(semaphore):
            remote(sample, sample, semaphore, self.arrive.at[0, 0, 0], spot.here).wait_send()

        def body(piece, carry):
            for direction in range(2):
                for section in range(SEC - 1):
                    sent(self.chain_send.at[direction, section, piece])

            @pl.when(jnp.logical_not(spot.local(piece)))
            def _():
                sent(self.send.at[0, piece])

            sent(self.send.at[1, piece])
            return carry

        lax.fori_loop(0, REP, body, 0)
        for copy in (*self.low, *self.high, self.back, self.onward):
            copy.wait_send()

        @pl.when(spot.core == 0)
        def _():
            self.forth.wait_send()


def spread_scratch(height):
    dma = pltpu.SemaphoreType.DMA
    return [
        *[pltpu.VMEM((2 * REP, height, LANES), BF16)] * SEC,
        pltpu.VMEM((2, 4, height, LANES), BF16),
        dma((2, 4)),
        dma((2, 4)),
        dma((2, REP)),
        dma((2, SEC - 1, REP)),
        dma((SEC, 2, REP)),
    ]


class Scatter:
    def __init__(self, spot, pieces, landing, send, arrive):
        self.spot, self.pieces, self.landing = spot, pieces, landing
        self.send, self.arrive = send, arrive

    def copy(self, half, other, lands):
        return remote(
            self.pieces.at[half, other],
            self.landing.at[half, lands],
            self.send.at[half, other],
            self.arrive.at[half, lands],
            (other, self.spot.blk),
        )

    def put(self, half, make):
        rep = self.spot.rep

        def one(step, carry):
            other = lax.rem(rep + 1 + step, REP)
            self.pieces[half, other] = make(other)
            self.copy(half, other, rep).start()
            return carry

        lax.fori_loop(0, REP - 1, one, 0, unroll=7)
        self.landing[half, rep] = make(rep)

    def total(self, half):
        rep = self.spot.rep

        def one(step, carry):
            other = lax.rem(rep + 1 + step, REP)
            self.copy(half, other, other).wait_recv()
            return carry

        lax.fori_loop(0, REP - 1, one, 0)
        total = self.landing[half, 0].astype(F32)
        for index in range(1, REP):
            total = total + self.landing[half, index].astype(F32)
        return total

    def drain(self):
        def one(step, carry):
            other = lax.rem(self.spot.rep + 1 + step, REP)
            for half in range(self.pieces.shape[0]):
                self.copy(half, other, other).wait_send()
            return carry

        lax.fori_loop(0, REP - 1, one, 0)


def scatter_scratch(halves, height, width, dtype):
    dma = pltpu.SemaphoreType.DMA
    return [
        pltpu.VMEM((halves, REP, height, width), dtype),
        pltpu.VMEM((halves, REP, height, width), dtype),
        dma((halves, REP)),
        dma((halves, REP)),
    ]


def pack(values):
    half = TILE // 2
    lanes = lax.broadcasted_iota(jnp.int32, (half, LANES), 1)
    rest = jnp.where(
        lanes < half,
        values[:half, LANES:],
        pltpu.roll(values[half:, LANES:], half, 1),
    )
    return jnp.concatenate([values[:, :LANES], rest], axis=0).astype(BF16)


def unpack(packed):
    half = TILE // 2
    rest = packed[TILE:]
    turned = jnp.concatenate([rest[:, half:], rest[:, :half]], axis=1)
    return jnp.concatenate(
        [packed[:TILE], jnp.concatenate([rest, turned], axis=0)], axis=1
    )


def is_kept(ids):
    columns = lax.broadcasted_iota(jnp.int32, (1, WIDE), 1)
    mixed = (ids * 73244475 + 12345) + columns * 19349663
    mixed = jnp.bitwise_and(mixed ^ jnp.right_shift(mixed, 15), 32767) * (40503 % 32768)
    mixed = mixed ^ jnp.right_shift(mixed, 13)
    return jnp.bitwise_and(mixed, 3) != 0


def column_of(row):
    lanes = lax.broadcasted_iota(jnp.int32, (TILE, LANES), 1)
    rows = lax.broadcasted_iota(jnp.int32, (TILE, LANES), 0)
    spread_out = jnp.broadcast_to(row.astype(F32), (TILE, LANES))
    return jnp.sum(jnp.where(lanes == rows, spread_out, 0.0), axis=1, keepdims=True)


def step_kernel(
    scale,
    count,
    place,
    x_hbm,
    ids,
    labels,
    mask,
    tiles_hbm,
    weight_in_hbm,
    weight_out_hbm,
    bias,
    logits_out,
    full,
    x,
    tiles,
    weight_in,
    weight_out,
    input_sems,
    table_values,
    table,
    wide_out,
    wide_bias,
    running,
    coded,
    shard,
    kept,
    dense,
    back_rows,
    in_sum,
    out_sum,
    slopes,
    wide_slopes,
    slope_send,
    slope_arrive,
    depth_in,
    pieces,
    pieces_in,
    b_send,
    b_arrive,
    c_send,
    c_arrive,
    d_send,
    d_arrive,
    *rest,
):
    rest = list(rest)

    def take(count):
        taken = rest[:count]
        del rest[:count]
        return taken

    spot = Spot()
    rep, blk = spot.rep, spot.blk
    first_sections = take(SEC)
    first_spread = Spread(spot, coded, first_sections, *take(6))
    second_sections = take(SEC)
    second_spread = Spread(spot, shard, second_sections, *take(6))
    first_scatter = Scatter(spot, *take(4))
    second_scatter = Scatter(spot, *take(4))
    waits = greet_everyone(spot)
    input_copies = [
        pltpu.make_async_copy(source, target, input_sems.at[index])
        for index, (source, target) in enumerate(
            (
                (x_hbm, x),
                (weight_out_hbm, weight_out),
                (weight_in_hbm, weight_in),
                (tiles_hbm, tiles),
            )
        )
    ]
    for copy in input_copies:
        copy.start()
    table_copy = pltpu.make_async_copy(table_values, table, input_sems.at[len(input_copies)])

    def prepare(section):
        if section == 0:
            fill_tables(place, count, table_values)
            table_copy.start()
        elif section == 1:
            running[NONE] = jnp.zeros((TILE, WIDE), F32)
            wide_out[...] = jnp.zeros_like(wide_out)
            wide_bias[...] = jnp.zeros_like(wide_bias)
            wide_bias[:, :CLASSES] = bias[...]
            input_copies[1].wait()
            wide_out[:CLASSES, :] = weight_out[...]
            input_copies[2].wait()
            input_copies[3].wait()
            table_copy.wait()

    input_copies[0].wait()
    code_rows = lax.broadcasted_iota(jnp.int32, (CODED - TILE, LANES), 0)
    for half in range(2):
        coded[half, :TILE] = x[half]
        number = ids[half : half + 1, :]
        code = jnp.zeros((CODED - TILE, LANES), F32)
        for byte in range(3):
            value = jnp.bitwise_and(jnp.right_shift(number, 8 * byte), 255).astype(F32)
            code = jnp.where(code_rows == byte, jnp.broadcast_to(value, code.shape), code)
        coded[half, TILE:] = code.astype(BF16)
    pl.semaphore_wait(pltpu.get_barrier_semaphore(), waits)

    def products(section, width, source_of):
        place = FORWARD_ORDER.index(section)

        def some(group, carry):
            made = []
            for inner in range(4):
                slot = group * 4 + inner
                made.append(
                    jnp.dot(
                        tiles[section * SLOTS + slot],
                        source_of(table[SOURCE + section, slot]),
                        preferred_element_type=F32,
                    )
                )
            for inner in range(4):
                slot = group * 4 + inner
                running[place * SLOTS + slot, :, :width] = (
                    made[inner] + running[table[PREVIOUS + section, slot], :, :width]
                )
            return carry

        lax.fori_loop(0, SLOTS // 4, some, 0, unroll=2)

    def first_products(section):
        products(section, LANES, lambda index: first_sections[section][index, :TILE])

    def second_products(section):
        products(section, WIDE, lambda index: dense[section * SLOTS + index])

    def first_sum(half):
        return lambda other: running[table[LAST, 2 * other + half], :, :LANES]

    def second_sum(half):
        def one(other):
            part = running[table[LAST, 2 * other + half]].astype(BF16)
            return pack(
                lax.dot_general(
                    part, wide_out[...], (((1,), (1,)), ((), ())), preferred_element_type=F32
                )
            )

        return one

    def find_kept(section):
        lanes = lax.broadcasted_iota(jnp.int32, (TILE, LANES), 1)
        rows = lax.broadcasted_iota(jnp.int32, (TILE, LANES), 0)
        unit = jnp.where(lanes == rows, 1.0, 0.0).astype(BF16)

        def one(index, carry):
            code = lax.dot_general(
                unit,
                first_sections[section][index, TILE:],
                (((1,), (1,)), ((), ())),
                preferred_element_type=F32,
            )
            number = code[:, 0:1] + 256.0 * code[:, 1:2] + 65536.0 * code[:, 2:3]
            kept[section * SLOTS + index] = jnp.where(
                is_kept(number.astype(jnp.int32)), 1.0, 0.0
            ).astype(BF16)
            return carry

        lax.fori_loop(0, SLOTS, one, 0, unroll=4)

    def activate(section, half):
        def one(index, carry):
            pre_act = jnp.dot(
                second_sections[section][index], weight_in[...], preferred_element_type=F32
            )
            active = jnp.maximum(pre_act, 0.0) * F32(KEEP)
            flag = kept[section * SLOTS + index].astype(F32)
            dense[section * SLOTS + index] = jnp.where(flag > 0.0, active, 0.0).astype(BF16)
            return carry

        lax.fori_loop(half * REP, (half + 1) * REP, one, 0, unroll=4)

    def activate_arrived(section):
        activate(section, 0)
        activate(SEC - 1 - section, 1)

    first_spread.start_low()
    first_spread.start_high()
    first_spread.pass_on()
    first_spread.chains(prepare)
    first_products(1)
    first_products(2)
    first_spread.last_arrivals()
    first_products(0)
    first_products(3)
    first_scatter.put(0, first_sum(0))
    first_scatter.put(1, first_sum(1))
    for section in range(SEC):
        find_kept(section)
    shard[0] = first_scatter.total(0).astype(BF16)
    second_spread.start_low()
    shard[1] = first_scatter.total(1).astype(BF16)
    second_spread.start_high()
    second_spread.pass_on()
    second_spread.chains(activate_arrived)
    second_products(1)
    second_products(2)
    second_spread.last_arrivals()
    activate_arrived(SEC - 1)
    second_products(0)
    second_products(3)
    second_scatter.put(0, second_sum(0))
    second_scatter.put(1, second_sum(1))
    first_spread.drain()
    second_spread.drain()
    first_scatter.drain()

    def slope_copy(half, other, lands):
        return remote(
            slopes.at[2 * rep + half],
            slopes.at[2 * lands + half],
            slope_send.at[half, other],
            slope_arrive.at[half, lands],
            (other, blk),
        )

    def classes(half):
        logits = unpack(second_scatter.total(half)) + wide_bias[...]
        columns = lax.broadcasted_iota(jnp.int32, logits.shape, 1)
        real = columns < CLASSES
        top = jnp.max(jnp.where(real, logits, -jnp.inf), axis=1, keepdims=True)
        powers = jnp.where(real, jnp.exp(jnp.where(real, logits - top, 0.0)), 0.0)
        likelihood = powers / jnp.sum(powers, axis=1, keepdims=True)
        label = column_of(labels[half : half + 1, :]).astype(jnp.int32)
        onehot = jnp.where(columns == label, 1.0, 0.0)
        chosen = column_of(mask[half : half + 1, :]) * scale
        slopes[2 * rep + half] = pack((likelihood - onehot) * chosen)
        for step in range(1, REP):
            slope_copy(half, lax.rem(rep + step, REP), rep).start()
        return logits

    low_logits = classes(0)
    high_logits = classes(1)
    logits_out[:, :TILE] = low_logits.T[:CLASSES]
    logits_out[:, TILE:] = high_logits.T[:CLASSES]
    second_scatter.drain()

    def slope_waits(step, carry):
        other = lax.rem(rep + step, REP)
        for half in range(2):
            copy = remote(
                slopes.at[2 * rep + half],
                slopes.at[2 * other + half],
                slope_send.at[half, other],
                slope_arrive.at[half, other],
                (other, blk),
            )
            copy.wait_recv()
            copy.wait_send()
        return carry

    lax.fori_loop(1, REP, slope_waits, 0)

    def widen(index, carry):
        wide_slopes[index] = unpack(slopes[index])
        return carry

    lax.fori_loop(0, 2 * REP, widen, 0, unroll=4)

    def back_products(section):
        def some(group, carry):
            made = []
            for inner in range(4):
                slot = group * 4 + inner
                made.append(
                    lax.dot_general(
                        tiles[section * SLOTS + slot],
                        wide_slopes[table[ROW + section, slot]],
                        (((0,), (0,)), ((), ())),
                        preferred_element_type=F32,
                    )
                )
            for inner in range(4):
                slot = group * 4 + inner
                running[section * SLOTS + slot] = (
                    made[inner] + running[table[BACK_PREVIOUS + section, slot]]
                )
            return carry

        lax.fori_loop(0, SLOTS // 4, some, 0, unroll=2)

        def gather(piece, carry):
            for half in range(2):
                back_rows[section * SLOTS + half * REP + piece] = running[
                    table[BACK_LAST + section, 2 * piece + half]
                ].astype(BF16)
            return carry

        lax.fori_loop(0, REP, gather, 0, unroll=2)

    in_sum[...] = jnp.zeros_like(in_sum)
    out_sum[...] = jnp.zeros_like(out_sum)

    def terms(section):
        for half in range(2):
            inside = pl.ds(section * SLOTS + half * REP, REP)
            back = back_rows[inside].reshape(REP * TILE, WIDE)
            active = dense[inside].reshape(REP * TILE, WIDE)
            z_rows = second_sections[section][half * REP : (half + 1) * REP].reshape(
                REP * TILE, LANES
            )
            out_sum[...] += lax.dot_general(
                back, active, (((0,), (0,)), ((), ())), preferred_element_type=F32
            )
            hidden_rows = jnp.dot(back, wide_out[...], preferred_element_type=F32)
            pre_slope = jnp.where(
                active.astype(F32) > 0.0, hidden_rows * F32(KEEP), 0.0
            ).astype(BF16)
            in_sum[...] += lax.dot_general(
                z_rows, pre_slope, (((0,), (0,)), ((), ())), preferred_element_type=F32
            )

    for section in range(SEC):
        back_products(section)
        terms(section)
    joined = jnp.concatenate([in_sum[...], out_sum[...]], axis=0)
    for index in range(CREW):
        row = index % (CREW // 2) * CHUNK
        lane = index // (CREW // 2) * LANES
        pieces[index] = joined[row : row + CHUNK, lane : lane + LANES].astype(BF16)
    me, depth = spot.member, spot.depth

    def reduce_copy(other, lands):
        return remote(
            pieces.at[other],
            pieces_in.at[lands],
            b_send.at[other],
            b_arrive.at[lands],
            spot.crew(other),
        )

    def gather_copy(other, lands):
        return remote(
            full.at[me], full.at[lands], d_send.at[other], d_arrive.at[lands], spot.crew(other)
        )

    def start_all(copy):
        def one(step, carry):
            copy(lax.rem(me + step, CREW), me).start()
            return carry

        lax.fori_loop(1, CREW, one, 0, unroll=8)

    def wait_all(copy):
        def one(step, carry):
            other = lax.rem(me + step, CREW)
            both = copy(other, other)
            both.wait_recv()
            both.wait_send()
            return carry

        lax.fori_loop(1, CREW, one, 0, unroll=8)

    start_all(reduce_copy)
    pieces_in[me] = pieces[me]
    wait_all(reduce_copy)
    total = pieces_in[0].astype(F32)
    for index in range(1, CREW):
        total = total + pieces_in[index].astype(F32)
    depth_in[depth] = total
    for step in range(1, DEPTH):
        remote(
            depth_in.at[depth],
            depth_in.at[depth],
            c_send.at[step],
            c_arrive.at[depth],
            spot.line(step),
        ).start()
    for step in range(1, DEPTH):
        other = lax.rem(depth + step, DEPTH)
        copy = remote(
            depth_in.at[depth],
            depth_in.at[other],
            c_send.at[step],
            c_arrive.at[other],
            spot.line(step),
        )
        copy.wait_recv()
        copy.wait_send()
    total = depth_in[0]
    for index in range(1, DEPTH):
        total = total + depth_in[index]
    full[me] = total.astype(BF16)
    start_all(gather_copy)
    wait_all(gather_copy)


def result_kernel(in_rows, logits, full, logits_out, grad_in, grad_out):
    logits_out[:, 0, :] = logits[...]
    joined = jnp.concatenate(
        [
            jnp.concatenate(
                [full[start + index].astype(F32) for index in range(CREW // 2)], axis=0
            )
            for start in (0, CREW // 2)
        ],
        axis=1,
    )
    grad_in[...] = joined[:in_rows]
    grad_out[...] = joined[in_rows : in_rows + CLASSES]


def fill_tables(place, count, out):
    slots = lax.broadcasted_iota(jnp.int32, (SLOTS, SLOTS), 1)
    others = lax.broadcasted_iota(jnp.int32, (SLOTS, SLOTS), 0)
    before = others < slots

    def turned(line):
        flat = jnp.broadcast_to(line.astype(F32), (SLOTS, SLOTS))
        column = jnp.sum(jnp.where(slots == others, flat, 0.0), axis=1, keepdims=True)
        return column.astype(jnp.int32)

    def top(match, entries):
        return jnp.max(jnp.where(match, entries, -1), axis=0, keepdims=True)

    def put(row, values):
        out[row : row + 1, :SLOTS] = values

    def settled(values):
        return jnp.where(values < 0, NONE, values)

    rows, columns, row_turned, column_turned, live = [], [], [], [], []
    for section in range(SEC):
        line = place[section : section + 1, :]
        rows.append(jnp.right_shift(line, 4))
        columns.append(jnp.bitwise_and(line, SLOTS - 1))
        row_turned.append(turned(rows[section]))
        column_turned.append(turned(columns[section]))
        live.append(others < count[section])
    numbers = slots[:1]
    last = jnp.full((1, SLOTS), -1, jnp.int32)
    for section in range(SEC):
        turn = FORWARD_ORDER.index(section)
        entries = others + turn * SLOTS
        latest = jnp.full((1, SLOTS), -1, jnp.int32)
        for earlier in FORWARD_ORDER[: turn + 1]:
            match = (row_turned[earlier] == rows[section]) & live[earlier]
            if earlier == section:
                match = match & before
            latest = jnp.maximum(
                latest, top(match, others + FORWARD_ORDER.index(earlier) * SLOTS)
            )
        last = jnp.maximum(last, top((row_turned[section] == numbers) & live[section], entries))
        put(SOURCE + section, jnp.bitwise_and(columns[section], 1) * REP + jnp.right_shift(columns[section], 1))
        put(PREVIOUS + section, settled(latest))
        put(ROW + section, rows[section])
        own = others + section * SLOTS
        match = (column_turned[section] == columns[section]) & live[section]
        put(BACK_PREVIOUS + section, settled(top(match & before, own)))
        match = (column_turned[section] == numbers) & live[section]
        put(BACK_LAST + section, settled(top(match, own)))
    put(LAST, settled(last))


def on_device(
    features,
    node_ids,
    labels,
    train_mask,
    tile_values,
    tile_place,
    tile_count,
    weight_in,
    weight_out,
    class_bias,
):
    width = features.shape[-1]
    own_rows = features.shape[1]
    scale = 1.0 / math.sqrt(own_rows * REP * BLK)
    shape = jax.ShapeDtypeStruct
    dma = pltpu.SemaphoreType.DMA
    vmem = pltpu.VMEM
    anywhere = pl.BlockSpec(memory_space=pl.ANY)
    logits, full = pl.pallas_call(
        lambda *refs: step_kernel(scale, *refs),
        out_shape=(shape((CLASSES, own_rows), F32), shape((CREW, CHUNK, LANES), BF16)),
        in_specs=[
            pl.BlockSpec(memory_space=pltpu.SMEM),
            whole(),
            anywhere,
            whole(),
            whole(),
            whole(),
            anywhere,
            anywhere,
            anywhere,
            whole(),
        ],
        out_specs=[whole()] * 2,
        scratch_shapes=[
            vmem((2, TILE, width), BF16),
            vmem((NONE, TILE, TILE), BF16),
            vmem((width, WIDE), BF16),
            vmem((CLASSES, WIDE), BF16),
            dma((5,)),
            vmem((24, LANES), jnp.int32),
            pltpu.SMEM((24, LANES), jnp.int32),
            vmem((WIDE, WIDE), BF16),
            vmem((1, WIDE), F32),
            vmem((NONE + 1, TILE, WIDE), F32),
            vmem((2, CODED, LANES), BF16),
            vmem((2, TILE, LANES), BF16),
            vmem((NONE, TILE, WIDE), BF16),
            vmem((NONE, TILE, WIDE), BF16),
            vmem((NONE, TILE, WIDE), BF16),
            vmem((width, WIDE), F32),
            vmem((WIDE, WIDE), F32),
            vmem((2 * REP, PACKED, LANES), BF16),
            vmem((2 * REP, TILE, WIDE), BF16),
            dma((2, REP)),
            dma((2, REP)),
            vmem((DEPTH, CHUNK, LANES), F32),
            vmem((CREW, CHUNK, LANES), BF16),
            vmem((CREW, CHUNK, LANES), BF16),
            dma((CREW,)),
            dma((CREW,)),
            dma((DEPTH,)),
            dma((DEPTH,)),
            dma((CREW,)),
            dma((CREW,)),
            *spread_scratch(CODED),
            *spread_scratch(TILE),
            *scatter_scratch(2, TILE, LANES, F32),
            *scatter_scratch(2, PACKED, LANES, BF16),
        ],
        compiler_params=pltpu.CompilerParams(
            collective_id=0, has_side_effects=True, vmem_limit_bytes=VMEM_LIMIT
        ),
        name="training_step",
    )(
        tile_count.reshape(SEC),
        tile_place.reshape(SEC, SLOTS),
        features.reshape(2, TILE, width),
        node_ids.reshape(2, TILE),
        labels.reshape(2, TILE),
        train_mask.reshape(2, TILE),
        tile_values.reshape(NONE, TILE, TILE),
        weight_in,
        weight_out.T,
        class_bias.reshape(1, CLASSES),
    )
    logits, grad_in, grad_out = pl.pallas_call(
        lambda *refs: result_kernel(width, *refs),
        out_shape=(
            shape((CLASSES, 1, own_rows), F32),
            shape((width, WIDE), F32),
            shape((CLASSES, WIDE), F32),
        ),
        in_specs=[whole()] * 2,
        out_specs=[whole()] * 3,
        name="results",
    )(logits, full)
    return (logits.transpose(1, 2, 0), grad_in, grad_out.T)


def solution(mesh):
    placed = (
        P("blk", "rep", None),
        P("blk", "rep"),
        P("blk", "rep"),
        P("blk", "rep"),
        P("blk", "rep", None, None, None, None),
        P("blk", "rep", None, None),
        P("blk", "rep", None),
        P(),
        P(),
        P(),
    )
    return jax.shard_map(
        on_device,
        mesh=mesh,
        in_specs=placed,
        out_specs=(P("blk", "rep", None), P(), P()),
        check_vma=False,
    )
```
